32 devices in a mesh: aux: 4 (over z), pair: 8 (over y, x, core).
Axes of the slice: x: 2, y: 2, z: 4, core: 2. Of those that a mesh axis runs over, the one named last changes fastest.
Arguments:
- metric: bfloat16 [4096, 4096], P('aux', 'pair'), may hold values from -0.09375 to 0.09375
- amplitudes: bfloat16 [4096, 16384], P('aux', 'pair'), may hold values from -0.59765625 to 0.59765625
- virt_coef: bfloat16 [1024, 1280], replicated, may hold values from -1.5 to 1.5
Outputs:
- density: float32 [4096, 4096], P('aux', 'pair')
- fitted_ao: bfloat16 [4096, 20480], P(('aux', 'pair'))
The draws below stay inside these ranges and needn't reach their ends.
All inputs are finite; a program needn't handle non-finite values.
Results may differ from the reference program's by a relative error of at most 0.012.
Values may be sent and summed in bfloat16 or wider, within the bound.
A program may use at most 128 MiB of HBM per device.

```python
import jax
import jax.numpy as jnp
from jax import lax

P_SIZE = 4096
V = 1024
AO = 1280
OCC = 16
PAIRS = 16384


def raised(drawn, key, source, target, blocks, factor):
    owner, partner = [(jnp.arange(drawn.shape[position]) // (drawn.shape[position] // blocks)).reshape([-1 if axis == position else 1 for axis in range(drawn.ndim)]) for position in (source, target)]
    chosen = jax.random.permutation(key, blocks)[partner]
    strong = (owner == chosen) | (owner == (partner + blocks // 2) % blocks)
    return jnp.where(strong, factor * drawn, drawn)


def block_levels(key, shape, cuts, least, top_value):
    factor_of, own = 1.0, jax.random.fold_in(key, 6)
    for axis_at, parts in cuts:
        heights = jnp.exp(jax.random.uniform(jax.random.fold_in(own, axis_at), (parts,), jnp.float32, least / len(cuts), top_value / len(cuts)))
        factor_of = factor_of * jnp.repeat(heights, shape[axis_at] // parts).reshape([-1 if axis == axis_at else 1 for axis in range(len(shape))])
    return factor_of


def bell_draw(own_key, dims, deviation, limit, cuts=(), dtype=jnp.bfloat16):
    gain = block_levels(own_key, dims, cuts, -0.22, 0.18) if cuts else 1.0
    array = jax.random.normal(own_key, dims, jnp.float32) * deviation * gain
    return jnp.minimum(jnp.maximum(array, -limit), limit).astype(dtype)


def heavy_noise(stream_key, shape, width, reach, pieces, heavy, kind=jnp.bfloat16):
    entries = width * jax.random.normal(stream_key, shape, jnp.float32)
    if pieces:
        entries = entries * block_levels(stream_key, shape, pieces, -0.22, 0.18)
    return jnp.clip(raised(entries, jax.random.fold_in(stream_key, 3), *heavy), -reach, reach).astype(kind)


def setup_inputs(seed: int = 0) -> dict:
    streams_of = jax.random.split(jax.random.key(seed), 4)
    return {
        "metric": bell_draw(streams_of[0], (P_SIZE, P_SIZE), P_SIZE ** -0.5, 0.09375, ((0, 4), (1, 8))),
        "amplitudes": heavy_noise(streams_of[1], (P_SIZE, PAIRS), 0.1, 0.59765625, ((0, 4), (1, 8)), (1, 0, 8, 2.0)),
        "virt_coef": bell_draw(streams_of[2], (V, AO), (V // 64) ** -0.5, 1.5),
    }


def reference(metric, amplitudes, virt_coef):
    fitted = jnp.dot(metric, amplitudes, preferred_element_type=jnp.float32).astype(jnp.bfloat16)
    density = lax.dot_general(fitted, amplitudes, (((1,), (1,)), ((), ())), preferred_element_type=jnp.float32)
    blocks = fitted.reshape(P_SIZE * OCC, V)
    fitted_ao = jnp.dot(blocks, virt_coef, preferred_element_type=jnp.float32).astype(jnp.bfloat16)
    return density, fitted_ao.reshape(P_SIZE, OCC * AO)
```

```python
import functools

import jax
import jax.numpy as jnp
from jax import lax
from jax.experimental import pallas as pl
from jax.experimental.pallas import tpu as pltpu
from jax.sharding import PartitionSpec as P

MESH = pl.DeviceIdType.MESH


def kernel(
    na, n, count, metric, amp, virt_coef, density, fitted_ao,
    m_v, a_v, d_v, f_v, g_v, c_v, one_v, two_v, o_v,
    m_send, m_recv, z_send, z_recv, x_send, x_recv, one_send, one_recv, two_send, two_recv, o_sem, local_sem,
):
    a, b = lax.axis_index("aux"), lax.axis_index("pair")
    p, q = metric.shape
    per = amp.shape[1]
    w = per // count
    rows = p // n
    virt, ao = virt_coef.shape
    half = n // 2
    parity, chip = lax.rem(b, 2), b // 2
    partner = b + 1 - 2 * parity
    tile = min(256, p)
    tiles = p // tile

    barrier = pltpu.get_barrier_semaphore()
    for d in range(1, n):
        pl.semaphore_signal(barrier, inc=1, device_id=(a, lax.rem(b + d, n)), device_id_type=MESH)

    @pl.when(a > 0)
    def _():
        pl.semaphore_signal(barrier, inc=1, device_id=(a - 1, b), device_id_type=MESH)

    @pl.when(a < na - 1)
    def _():
        pl.semaphore_signal(barrier, inc=1, device_id=(a + 1, b), device_id_type=MESH)

    pl.semaphore_wait(barrier, n - 1 + jnp.where(a > 0, 1, 0) + jnp.where(a < na - 1, 1, 0))

    def block_of(s, c):
        return a_v.at[c, pl.ds(pl.multiple_of(s * p, p), p), :]

    def hop(src, s, c, way, target):
        return pltpu.make_async_remote_copy(
            src_ref=src, dst_ref=block_of(s, c), send_sem=z_send.at[way, s, c],
            recv_sem=z_recv.at[s, c], device_id=(target, b), device_id_type=MESH,
        )

    def metric_copy(owner, target):
        return pltpu.make_async_remote_copy(
            src_ref=metric, dst_ref=m_v.at[:, pl.ds(pl.multiple_of(owner * q, q), q)],
            send_sem=m_send.at[target], recv_sem=m_recv.at[owner],
            device_id=(a, target), device_id_type=MESH,
        )

    def regroup(owner, target, c):
        return pltpu.make_async_remote_copy(
            src_ref=f_v.at[c, pl.ds(pl.multiple_of(target * rows, rows), rows), :],
            dst_ref=g_v.at[:, pl.ds(pl.multiple_of(owner * per + c * w, w), w)],
            send_sem=x_send.at[target, c], recv_sem=x_recv.at[owner, c],
            device_id=(a, target), device_id_type=MESH,
        )

    def staged(j):
        return m_v.at[:, pl.ds(pl.multiple_of(j * q, q), q)]

    def first(j):
        return pltpu.make_async_remote_copy(
            src_ref=staged(j), dst_ref=one_v.at[j // 2], send_sem=one_send.at[j // 2],
            recv_sem=one_recv.at[j // 2], device_id=(a, partner), device_id_type=MESH,
        )

    def second(source, j):
        return pltpu.make_async_remote_copy(
            src_ref=staged(j), dst_ref=two_v.at[source], send_sem=two_send.at[0, j // 2],
            recv_sem=two_recv.at[0, source], device_id=(a, j), device_id_type=MESH,
        )

    def mine(c):
        return amp.at[:, c * w : (c + 1) * w]

    for c in range(count):
        @pl.when(a > 0)
        def _():
            hop(mine(c), a, c, 0, jnp.maximum(a - 1, 0)).start()

        @pl.when(a < na - 1)
        def _():
            hop(mine(c), a, c, 1, jnp.minimum(a + 1, na - 1)).start()

    @pl.loop(1, n)
    def _(d):
        metric_copy(b, lax.rem(b + d, n)).start()

    own_copies = [pltpu.make_async_copy(mine(c), block_of(a, c), local_sem.at[c]) for c in range(count)]
    own_copies.append(pltpu.make_async_copy(metric, staged(b), local_sem.at[count]))
    own_copies.append(pltpu.make_async_copy(virt_coef, c_v, local_sem.at[count + 1]))
    for copy in own_copies:
        copy.start()

    def arrive(t, c):
        @pl.when(a - t >= 0)
        def _():
            s = jnp.maximum(a - t, 0)
            hop(block_of(s, c), s, c, 1, a).wait_recv()

            @pl.when(a < na - 1)
            def _():
                hop(block_of(s, c), s, c, 1, jnp.minimum(a + 1, na - 1)).start()

        @pl.when(a + t < na)
        def _():
            s = jnp.minimum(a + t, na - 1)
            hop(block_of(s, c), s, c, 0, a).wait_recv()

            @pl.when(a > 0)
            def _():
                hop(block_of(s, c), s, c, 0, jnp.maximum(a - 1, 0)).start()

    @pl.loop(1, na - 1)
    def _(t):
        @pl.loop(0, count)
        def _(c):
            arrive(t, c)

    for copy in own_copies:
        copy.wait()

    @pl.loop(1, n)
    def _(d):
        metric_copy(lax.rem(b + n - d, n), b).wait_recv()

    @pl.loop(1, n)
    def _(d):
        metric_copy(b, lax.rem(b + d, n)).wait_send()

    def row(r):
        return pl.ds(pl.multiple_of(r * tile, tile), tile)

    def product(j, r, c):
        right = a_v[c, pl.ds(pl.multiple_of(j * q, q), q), :]
        return lax.dot_general(
            f_v[c, row(r), :], right, (((1,), (1,)), ((), ())), preferred_element_type=jnp.float32
        )

    def fit(c):
        @pl.loop(0, tiles)
        def _(r):
            f_v[c, row(r), :] = jnp.dot(
                m_v[row(r), :], a_v[c], preferred_element_type=jnp.float32
            ).astype(f_v.dtype)

        @pl.loop(1, n)
        def _(d):
            regroup(b, lax.rem(b + d, n), c).start()

        pltpu.make_async_copy(
            f_v.at[c, pl.ds(pl.multiple_of(b * rows, rows), rows), :],
            g_v.at[:, pl.ds(pl.multiple_of(b * per + c * w, w), w)], x_send.at[b, c],
        ).start()

    @pl.loop(0, n * tiles)
    def _(i):
        d_v[i // tiles, row(lax.rem(i, tiles)), :] = jnp.zeros((tile, q), jnp.float32)

    @pl.loop(0, count - 1)
    def _(c):
        arrive(na - 1, c)
        fit(c)

        @pl.loop(0, n * tiles)
        def _(i):
            j, r = i // tiles, lax.rem(i, tiles)
            d_v[j, row(r), :] += product(j, r, c)

    last = count - 1
    arrive(na - 1, last)
    fit(last)

    quad = half == 4
    mid = p // 2
    near = (chip + 1 - 2 * lax.rem(chip, 2), lax.rem(chip + 2, 4))
    far = 3 - chip

    def turn(h):
        if not quad:
            return lax.rem(chip + h, half)
        return jnp.where(h == 0, far, jnp.where(h == 1, near[0], jnp.where(h == 2, near[1], chip)))

    @pl.loop(0, half)
    def _(h):
        j = 2 * turn(h) + 1 - parity

        @pl.loop(0, tiles)
        def _(r):
            m_v[row(r), pl.ds(pl.multiple_of(j * q, q), q)] = (
                d_v[j, row(r), :] + product(j, r, last)
            ).astype(m_v.dtype)

        first(j).start()

    @pl.loop(0, 0 if quad else half)
    def _(h):
        j = 2 * lax.rem(chip + h, half) + parity

        @pl.loop(0, tiles)
        def _(r):
            d_v[j, row(r), :] += product(j, r, last)

    def part(way):
        return pl.ds(way * mid, mid)

    def cast(slot, way):
        j = 2 * slot + parity
        m_v[part(way), pl.ds(pl.multiple_of(j * q, q), q)] = d_v[j, part(way), :].astype(m_v.dtype)

    def piece(slot, way, place, target):
        j = 2 * slot + parity
        return pltpu.make_async_remote_copy(
            src_ref=m_v.at[part(way), pl.ds(pl.multiple_of(j * q, q), q)],
            dst_ref=two_v.at[place, part(way), :], send_sem=two_send.at[way, place],
            recv_sem=two_recv.at[way, place], device_id=(a, 2 * target + parity), device_id_type=MESH,
        )

    def add_in(slot, place, way):
        j = 2 * slot + parity
        d_v[j, part(way), :] += two_v[place, part(way), :].astype(jnp.float32)

    if quad:
        for h in range(4):
            slot = (far, near[0], near[1], chip)[h]

            @pl.loop(0, tiles)
            def _(r, slot=slot):
                d_v[2 * slot + parity, row(r), :] += product(2 * slot + parity, r, last)

            first(2 * slot + parity).wait_recv()

            @pl.loop(0, tiles)
            def _(r, slot=slot):
                j = 2 * slot + parity
                d_v[j, row(r), :] += one_v[slot, row(r), :].astype(jnp.float32)

            if h == 0:
                for way in range(2):
                    cast(far, way)
                    piece(far, way, 0, near[way]).start()
            elif h < 3:
                cast(near[h - 1], h - 1)
                piece(near[h - 1], h - 1, 1, near[h - 1]).start()
    else:
        @pl.loop(1, half)
        def _(h):
            slot = lax.rem(chip + h, half)
            j = 2 * slot + parity
            first(j).wait_recv()

            @pl.loop(0, tiles)
            def _(r):
                m_v[row(r), pl.ds(pl.multiple_of(j * q, q), q)] = (
                    d_v[j, row(r), :] + one_v[slot, row(r), :].astype(jnp.float32)
                ).astype(m_v.dtype)

            second(chip, j).start()

        first(b).wait_recv()

        @pl.loop(0, tiles)
        def _(r):
            d_v[b, row(r), :] += one_v[chip, row(r), :].astype(jnp.float32)

    if quad:
        for way in range(2):
            other = near[1 - way]
            piece(other, way, 0, near[way]).wait_recv()
            add_in(other, 0, way)
            cast(other, way)
            piece(other, way, 2, other).start()

    @pl.loop(0, count)
    def _(c):
        pltpu.make_async_copy(
            f_v.at[c, pl.ds(pl.multiple_of(b * rows, rows), rows), :],
            g_v.at[:, pl.ds(pl.multiple_of(b * per + c * w, w), w)], x_send.at[b, c],
        ).wait()

        @pl.loop(1, n)
        def _(d):
            regroup(lax.rem(b + n - d, n), b, c).wait_recv()

    occ = n * per // virt

    def out_copy(i, slot):
        return pltpu.make_async_copy(
            o_v.at[slot], fitted_ao.at[:, pl.ds(pl.multiple_of(i * ao, ao), ao)], o_sem.at[slot]
        )

    @pl.loop(0, occ)
    def _(i):
        slot = lax.rem(i, 2)

        @pl.when(i >= 2)
        def _():
            out_copy(i - 2, slot).wait()

        o_v[slot] = jnp.dot(
            g_v[:, pl.ds(pl.multiple_of(i * virt, virt), virt)], c_v[...], preferred_element_type=jnp.float32
        ).astype(o_v.dtype)
        out_copy(i, slot).start()

    for i in range(max(occ - 2, 0), occ):
        out_copy(i, i % 2).wait()

    if quad:
        for way in range(2):
            piece(chip, way, 1, near[way]).wait_recv()
            add_in(chip, 1, way)
        for way in range(2):
            piece(chip, way, 2, near[1 - way]).wait_recv()
            add_in(chip, 2, way)
    else:
        @pl.loop(1, half)
        def _(h):
            source = lax.rem(chip + half - h, half)
            second(source, b).wait_recv()

            @pl.loop(0, tiles)
            def _(r):
                d_v[b, row(r), :] += two_v[source, row(r), :].astype(jnp.float32)

    result = pltpu.make_async_copy(d_v.at[b], density, local_sem.at[0])
    result.start()

    @pl.loop(0, half)
    def _(h):
        first(2 * h + 1 - parity).wait_send()

    if quad:
        for way in range(2):
            piece(far, way, 0, near[way]).wait_send()
            piece(near[way], way, 1, near[way]).wait_send()
            piece(near[1 - way], way, 2, near[1 - way]).wait_send()
    else:
        @pl.loop(1, half)
        def _(h):
            second(chip, 2 * lax.rem(chip + h, half) + parity).wait_send()

    @pl.loop(0, count)
    def _(c):
        @pl.loop(1, n)
        def _(d):
            regroup(b, lax.rem(b + d, n), c).wait_send()

        @pl.loop(0, na)
        def _(s):
            @pl.when(jnp.logical_and(s >= a, a > 0))
            def _():
                hop(block_of(s, c), s, c, 0, jnp.maximum(a - 1, 0)).wait_send()

            @pl.when(jnp.logical_and(s <= a, a < na - 1))
            def _():
                hop(block_of(s, c), s, c, 1, jnp.minimum(a + 1, na - 1)).wait_send()

    result.wait()


def shards(na, n, metric, amplitudes, virt_coef):
    p, q = metric.shape
    per = amplitudes.shape[1]
    virt, ao = virt_coef.shape
    count = next(c for c in (8, 4, 2, 1) if per % (128 * c) == 0)
    w = per // count
    rows = p // n
    bf16 = jnp.bfloat16
    dma = pltpu.SemaphoreType.DMA
    return pl.pallas_call(
        functools.partial(kernel, na, n, count),
        out_shape=(
            jax.ShapeDtypeStruct((p, q), jnp.float32),
            jax.ShapeDtypeStruct((rows, n * per // virt * ao), bf16),
        ),
        in_specs=[pl.BlockSpec(memory_space=pl.ANY)] * 3,
        out_specs=(pl.BlockSpec(memory_space=pl.ANY), pl.BlockSpec(memory_space=pl.ANY)),
        scratch_shapes=[
            pltpu.VMEM((p, n * q), bf16),
            pltpu.VMEM((count, na * p, w), bf16),
            pltpu.VMEM((n, p, q), jnp.float32),
            pltpu.VMEM((count, p, w), bf16),
            pltpu.VMEM((rows, n * per), bf16),
            pltpu.VMEM((virt, ao), bf16),
            pltpu.VMEM((n // 2, p, q), bf16),
            pltpu.VMEM((n // 2, p, q), bf16),
            pltpu.VMEM((2, rows, ao), bf16),
            dma((n,)), dma((n,)),
            dma((2, na, count)), dma((na, count)),
            dma((n, count)), dma((n, count)),
            dma((n // 2,)), dma((n // 2,)),
            dma((2, n // 2)), dma((2, n // 2)),
            dma((2,)), dma((count + 2,)),
        ],
        compiler_params=pltpu.CompilerParams(
            collective_id=0, has_side_effects=True, vmem_limit_bytes=67043328
        ),
    )(metric, amplitudes, virt_coef)

def cube_kernel(
    na, n, count, ha, metric, amp, virt_coef, density, fitted_ao, g_hbm,
    m_v, o_m, a_v, d_v, f_v, e_v, one_v, two_v,
    m_send, m_recv, z_send, z_recv, e_send, e_recv, x_send, x_recv,
    one_send, one_recv, two_send, two_recv, r_send, r_recv,
    mm_sem, fin_sem, g_sem, o_sem, local_sem, credit,
):
    a, b = lax.axis_index("aux"), lax.axis_index("pair")
    p, q = metric.shape
    per = amp.shape[1]
    w = per // count
    rows = p // n
    virt, ao = virt_coef.shape
    parity, chip = lax.rem(b, 2), b // 2
    flip = 1 - 2 * parity
    partner = b + flip
    near = (chip + 1 - 2 * lax.rem(chip, 2), lax.rem(chip + 2, 4))
    far = 3 - chip
    xb, yb, fb = 2 * near[0] + parity, 2 * near[1] + parity, 2 * far + parity
    tile = min(256, p)
    tiles = p // tile
    mid = p // 2
    last = count - 1

    middle = jnp.logical_and(a > 0, a < na - 1)
    end = jnp.logical_not(middle)
    mate = a + 1 - 2 * lax.rem(a, 2)
    across = na - 1 - a
    beyond = na - 1 - mate

    barrier = pltpu.get_barrier_semaphore()
    for d in range(1, n):
        pl.semaphore_signal(barrier, inc=1, device_id=(a, lax.rem(b + d, n)), device_id_type=MESH)
    pl.semaphore_signal(barrier, inc=1, device_id=(mate, b), device_id_type=MESH)

    @pl.when(middle)
    def _():
        pl.semaphore_signal(barrier, inc=1, device_id=(across, b), device_id_type=MESH)

    pl.semaphore_wait(barrier, n + jnp.where(middle, 1, 0))

    def cols(c):
        return pl.ds(pl.multiple_of(c * w, w), w)

    def row(r):
        return pl.ds(pl.multiple_of(r * tile, tile), tile)

    def part(way):
        return pl.ds(way * mid, mid)

    def wide(j):
        return pl.ds(pl.multiple_of(j * q, q), q)

    def block_of(s, c):
        return a_v.at[pl.ds(pl.multiple_of(s * p, p), p), cols(c)]

    def z(s, c, way, own=False):
        return pltpu.make_async_remote_copy(
            src_ref=amp.at[:, cols(c)] if own else block_of(s, c), dst_ref=block_of(s, c),
            send_sem=z_send.at[way, s, c], recv_sem=z_recv.at[s, c],
            device_id=(mate if way == 0 else across, b), device_id_type=MESH,
        )

    def relay(s, c, way):
        z(s, c, way).wait_recv()
        z(s, c, way).start()

    def lend():
        return pltpu.make_async_remote_copy(
            src_ref=metric, dst_ref=o_m.at[:, wide(b)], send_sem=mm_sem.at[0], recv_sem=mm_sem.at[1],
            device_id=(mate, b), device_id_type=MESH,
        )

    def give(c):
        return pltpu.make_async_remote_copy(
            src_ref=e_v.at[:, cols(c)], dst_ref=f_v.at[:, cols(c)], send_sem=e_send.at[c], recv_sem=e_recv.at[c],
            device_id=(mate, b), device_id_type=MESH,
        )

    def staged(j):
        return o_m.at[:, wide(j)]

    def finish():
        return pltpu.make_async_remote_copy(
            src_ref=staged(b), dst_ref=e_v.at[:, 0:q], send_sem=fin_sem.at[0], recv_sem=fin_sem.at[1],
            device_id=(mate, b), device_id_type=MESH,
        )

    def region(kind, mirror):
        mine = (b, b, b, xb, yb, xb, yb, fb, fb)
        theirs = (xb, yb, partner, fb, fb, xb + flip, yb + flip, fb + flip, fb + flip)
        half = (None, None, None, 0, 1, None, None, 0, 1)[kind]
        j = (theirs if mirror else mine)[kind]
        return (slice(None) if half is None else part(half), wide(j))

    def gather(g, kind, mirror=False):
        buf = (m_v, o_m)[g]
        where = region(kind, mirror)
        target = (xb, yb, partner, yb, xb, partner, partner, partner, partner)[kind]
        return pltpu.make_async_remote_copy(
            src_ref=metric if g == 0 and kind < 3 and not mirror else buf.at[where], dst_ref=buf.at[where],
            send_sem=m_send.at[g, kind], recv_sem=m_recv.at[g, kind],
            device_id=(a, target), device_id_type=MESH,
        )

    def got(g, kind):
        gather(g, kind, True).wait_recv()

    def gather_open(g):
        for kind in range(3):
            gather(g, kind).start()

    def gather_turn(g):
        got(g, 0)
        gather(g, 3).start()
        gather(g, 5).start()
        got(g, 1)
        gather(g, 4).start()
        gather(g, 6).start()

    def gather_close(g):
        got(g, 3)
        gather(g, 7).start()
        got(g, 4)
        gather(g, 8).start()
        for kind in (2, 5, 6, 7, 8):
            got(g, kind)
        for kind in range(9):
            gather(g, kind).wait_send()

    def regroup(owner, target, c):
        return pltpu.make_async_remote_copy(
            src_ref=f_v.at[pl.ds(pl.multiple_of(target * rows, rows), rows), cols(c)],
            dst_ref=g_hbm.at[:, pl.ds(pl.multiple_of(owner * per + c * w, w), w)],
            send_sem=x_send.at[target, c], recv_sem=x_recv.at[owner, c],
            device_id=(a, target), device_id_type=MESH,
        )

    def keep(c):
        return pltpu.make_async_copy(
            f_v.at[pl.ds(pl.multiple_of(b * rows, rows), rows), cols(c)],
            g_hbm.at[:, pl.ds(pl.multiple_of(b * per + c * w, w), w)], x_send.at[b, c],
        )

    def regroup_all(c):
        @pl.loop(1, n)
        def _(d):
            regroup(b, lax.rem(b + d, n), c).start()

        keep(c).start()

    def fit(mat, dst, c):
        @pl.loop(0, tiles)
        def _(r):
            dst[row(r), cols(c)] = jnp.dot(
                mat[row(r), :], a_v[:, cols(c)], preferred_element_type=jnp.float32
            ).astype(dst.dtype)

    def product(left, j, r, span):
        return lax.dot_general(
            left[row(r), span], a_v[wide(j), span], (((1,), (1,)), ((), ())), preferred_element_type=jnp.float32
        )

    early = slice(0, ha * w)

    def first(turn, j):
        return pltpu.make_async_remote_copy(
            src_ref=staged(j), dst_ref=one_v.at[j // 2], send_sem=one_send.at[turn, j // 2],
            recv_sem=one_recv.at[turn, j // 2], device_id=(a, partner), device_id_type=MESH,
        )

    def direct(kind):
        target = (xb, yb, fb)[kind]
        return pltpu.make_async_remote_copy(
            src_ref=staged(target), dst_ref=two_v.at[kind], send_sem=r_send.at[kind],
            recv_sem=r_recv.at[kind], device_id=(a, target), device_id_type=MESH,
        )

    own_copies = [
        pltpu.make_async_copy(amp, a_v.at[pl.ds(pl.multiple_of(a * p, p), p), :], local_sem.at[0]),
        pltpu.make_async_copy(metric, m_v.at[:, wide(b)], local_sem.at[1]),
    ]

    gather_open(0)

    @pl.when(end)
    def _():
        lend().start()

        @pl.loop(0, count)
        def _(c):
            z(a, c, 0, True).start()

    @pl.when(middle)
    def _():
        @pl.loop(0, ha)
        def _(c):
            z(a, c, 1, True).start()

        @pl.loop(ha, count)
        def _(c):
            z(a, c, 0, True).start()

    for copy in own_copies:
        copy.start()

    @pl.loop(0, n * tiles)
    def _(i):
        d_v[i // tiles, row(lax.rem(i, tiles)), :] = jnp.zeros((tile, q), jnp.float32)

    @pl.when(end)
    def _():
        gather_turn(0)
        gather_close(0)

    @pl.when(middle)
    def _():
        lend().wait_recv()
        gather_open(1)
        relay(mate, 0, 1)
        gather_turn(1)
        relay(mate, 1, 1)
        gather_turn(0)
        relay(mate, 2, 1)
        z(a, ha, 1, True).start()
        gather_close(1)

    for copy in own_copies:
        copy.wait()

    def accumulate(left, span):
        @pl.loop(0, n * tiles)
        def _(i):
            j, r = i // tiles, lax.rem(i, tiles)
            d_v[j, row(r), :] += product(left, j, r, span)

    def arrive(c):
        @pl.when(middle)
        def _():
            @pl.when(c < ha)
            def _():
                z(across, c, 0).wait_recv()
                z(beyond, c, 0).wait_recv()

            @pl.when(c >= ha)
            def _():
                relay(beyond, c, 0)

        @pl.when(end)
        def _():
            @pl.when(c < ha)
            def _():
                give(jnp.minimum(c, ha - 1)).wait_recv()

            @pl.when(c >= ha)
            def _():
                z(mate, c, 0).wait_recv()
                z(across, c, 0).wait_recv()
                z(beyond, c, 0).wait_recv()

    def first_share():
        @pl.loop(0, n // 2)
        def _(h):
            j = 2 * h + 1 - parity

            @pl.loop(0, tiles)
            def _(r):
                o_m[row(r), wide(j)] = product(e_v, j, r, early).astype(o_m.dtype)

            first(0, j).start()

    def first_total(j, r):
        return product(e_v, j, r, early) + one_v[j // 2, row(r), :].astype(jnp.float32)

    def second_share():
        for kind in (2, 0, 1):
            j = (xb, yb, fb)[kind]
            first(0, j).wait_recv()

            @pl.loop(0, tiles)
            def _(r, j=j):
                o_m[row(r), wide(j)] = first_total(j, r).astype(o_m.dtype)

            direct(kind).start()

    def third_share():
        first(0, b).wait_recv()
        for kind in range(3):
            direct(kind).wait_recv()

        @pl.loop(0, tiles)
        def _(r):
            total = first_total(b, r)
            for kind in range(3):
                total += two_v[kind, row(r), :].astype(jnp.float32)
            o_m[row(r), wide(b)] = total.astype(o_m.dtype)

        for target in (partner, xb, yb):
            pl.semaphore_signal(credit, inc=1, device_id=(a, target), device_id_type=MESH)

        @pl.loop(0, n // 2)
        def _(h):
            first(0, 2 * h + 1 - parity).wait_send()

        for kind in range(3):
            direct(kind).wait_send()

    @pl.loop(0, last)
    def _(c):
        @pl.when(middle)
        def _():
            @pl.when(jnp.logical_and(c >= 1, c + 2 < count))
            def _():
                relay(mate, c + 2, 1)

            @pl.when(jnp.logical_and(c >= 1, c + ha < count))
            def _():
                z(a, c + ha, 1, True).start()

            @pl.when(jnp.logical_and(c + 1 >= ha, c != ha))
            def _():
                relay(across, c + 1, 0)

        arrive(c)

        @pl.when(jnp.logical_and(middle, c < ha))
        def _():
            k = jnp.minimum(c, ha - 1)
            fit(o_m, e_v, k)
            give(k).start()

            @pl.when(c == 0)
            def _():
                gather_close(0)

        @pl.when(jnp.logical_or(middle, c >= ha))
        def _():
            fit(m_v, f_v, c)

        regroup_all(c)

        @pl.when(c >= ha)
        def _():
            accumulate(f_v, cols(c))

        @pl.when(jnp.logical_and(middle, c == ha - 1))
        def _():
            first_share()
            relay(across, ha + 1, 0)
            second_share()
            accumulate(f_v, early)

    @pl.when(middle)
    def _():
        third_share()

    arrive(last)

    @pl.when(middle)
    def _():
        finish().start()

    fit(m_v, f_v, last)
    regroup_all(last)

    @pl.when(middle)
    def _():
        pl.semaphore_wait(credit, 3)

    late = slice(last * w, count * w)

    @pl.loop(0, n // 2)
    def _(h):
        slot = jnp.where(h == 0, far, jnp.where(h == 1, near[0], jnp.where(h == 2, near[1], chip)))
        j = 2 * slot + 1 - parity

        @pl.loop(0, tiles)
        def _(r):
            o_m[row(r), wide(j)] = (d_v[j, row(r), :] + product(f_v, j, r, late)).astype(o_m.dtype)

        first(1, j).start()

    def cast(slot, way):
        j = 2 * slot + parity
        o_m[part(way), wide(j)] = d_v[j, part(way), :].astype(o_m.dtype)

    def piece(slot, way, place, target):
        return pltpu.make_async_remote_copy(
            src_ref=o_m.at[part(way), wide(2 * slot + parity)],
            dst_ref=two_v.at[place, part(way), :], send_sem=two_send.at[way, place],
            recv_sem=two_recv.at[way, place], device_id=(a, 2 * target + parity), device_id_type=MESH,
        )

    def add_in(slot, place, way):
        d_v[2 * slot + parity, part(way), :] += two_v[place, part(way), :].astype(jnp.float32)

    for h in range(4):
        slot = (far, near[0], near[1], chip)[h]
        j = 2 * slot + parity
        first(1, j).wait_recv()

        @pl.loop(0, tiles)
        def _(r, slot=slot, j=j):
            d_v[j, row(r), :] += product(f_v, j, r, late) + one_v[slot, row(r), :].astype(jnp.float32)

        if h == 0:
            for way in range(2):
                cast(far, way)
                piece(far, way, 0, near[way]).start()
        elif h < 3:
            cast(near[h - 1], h - 1)
            piece(near[h - 1], h - 1, 1, near[h - 1]).start()

    for way in range(2):
        other = near[1 - way]
        piece(other, way, 0, near[way]).wait_recv()
        add_in(other, 0, way)
        cast(other, way)
        piece(other, way, 2, other).start()

    coef = m_v.at[pl.ds(0, virt), pl.ds(0, ao)]
    load_coef = pltpu.make_async_copy(virt_coef, coef, local_sem.at[0])
    load_coef.start()

    @pl.loop(0, count)
    def _(c):
        keep(c).wait()

        @pl.loop(1, n)
        def _(d):
            regroup(lax.rem(b + n - d, n), b, c).wait_recv()

    occ = n * per // virt

    def slot_rows(slot):
        return pl.ds(pl.multiple_of(slot * rows, rows), rows)

    def block_copy(i, slot):
        return pltpu.make_async_copy(
            g_hbm.at[:, pl.ds(pl.multiple_of(i * virt, virt), virt)],
            m_v.at[slot_rows(slot), pl.ds(ao, virt)], g_sem.at[slot],
        )

    def out_copy(i, slot):
        return pltpu.make_async_copy(
            m_v.at[slot_rows(slot), pl.ds(ao + virt, ao)],
            fitted_ao.at[:, pl.ds(pl.multiple_of(i * ao, ao), ao)], o_sem.at[slot],
        )

    block_copy(0, 0).start()
    load_coef.wait()

    @pl.loop(0, occ)
    def _(i):
        slot = lax.rem(i, 2)

        @pl.when(i + 1 < occ)
        def _():
            block_copy(i + 1, 1 - slot).start()

        @pl.when(i >= 2)
        def _():
            out_copy(i - 2, slot).wait()

        block_copy(i, slot).wait()
        m_v[slot_rows(slot), pl.ds(ao + virt, ao)] = jnp.dot(
            m_v[slot_rows(slot), pl.ds(ao, virt)], m_v[pl.ds(0, virt), pl.ds(0, ao)],
            preferred_element_type=jnp.float32,
        ).astype(m_v.dtype)
        out_copy(i, slot).start()

    for i in range(max(occ - 2, 0), occ):
        out_copy(i, i % 2).wait()

    for way in range(2):
        piece(chip, way, 1, near[way]).wait_recv()
        add_in(chip, 1, way)
    for way in range(2):
        piece(chip, way, 2, near[1 - way]).wait_recv()
        add_in(chip, 2, way)

    @pl.when(end)
    def _():
        finish().wait_recv()

        @pl.loop(0, tiles)
        def _(r):
            d_v[b, row(r), :] += e_v[row(r), 0:q].astype(jnp.float32)

    result = pltpu.make_async_copy(d_v.at[b], density, local_sem.at[0])
    result.start()

    @pl.loop(0, n // 2)
    def _(h):
        first(1, 2 * h + 1 - parity).wait_send()

    for way in range(2):
        piece(far, way, 0, near[way]).wait_send()
        piece(near[way], way, 1, near[way]).wait_send()
        piece(near[1 - way], way, 2, near[1 - way]).wait_send()

    @pl.loop(0, count)
    def _(c):
        @pl.loop(1, n)
        def _(d):
            regroup(b, lax.rem(b + d, n), c).wait_send()

    @pl.when(end)
    def _():
        lend().wait_send()

        @pl.loop(0, count)
        def _(c):
            z(a, c, 0, True).wait_send()

    @pl.when(middle)
    def _():
        finish().wait_send()

        @pl.loop(0, ha)
        def _(c):
            give(c).wait_send()

        @pl.loop(0, count)
        def _(c):
            z(a, c, 1, True).wait_send()
            z(mate, c, 1).wait_send()

        @pl.loop(ha, count)
        def _(c):
            z(a, c, 0, True).wait_send()
            z(across, c, 0).wait_send()
            z(beyond, c, 0).wait_send()

    result.wait()


def cube_shards(na, n, count, metric, amplitudes, virt_coef):
    p, q = metric.shape
    per = amplitudes.shape[1]
    virt, ao = virt_coef.shape
    ha = count // 2
    rows = p // n
    bf16 = jnp.bfloat16
    dma = pltpu.SemaphoreType.DMA
    density, fitted_ao, _ = pl.pallas_call(
        functools.partial(cube_kernel, na, n, count, ha),
        out_shape=(
            jax.ShapeDtypeStruct((p, q), jnp.float32),
            jax.ShapeDtypeStruct((rows, n * per // virt * ao), bf16),
            jax.ShapeDtypeStruct((rows, n * per), bf16),
        ),
        in_specs=[pl.BlockSpec(memory_space=pl.ANY)] * 3,
        out_specs=(pl.BlockSpec(memory_space=pl.ANY),) * 3,
        scratch_shapes=[
            pltpu.VMEM((p, n * q), bf16),
            pltpu.VMEM((p, n * q), bf16),
            pltpu.VMEM((na * p, per), bf16),
            pltpu.VMEM((n, p, q), jnp.float32),
            pltpu.VMEM((p, per), bf16),
            pltpu.VMEM((p, max(per * ha // count, q)), bf16),
            pltpu.VMEM((n // 2, p, q), bf16),
            pltpu.VMEM((3, p, q), bf16),
            dma((2, 9)), dma((2, 9)),
            dma((2, na, count)), dma((na, count)),
            dma((ha,)), dma((ha,)),
            dma((n, count)), dma((n, count)),
            dma((2, n // 2)), dma((2, n // 2)),
            dma((2, 3)), dma((2, 3)),
            dma((3,)), dma((3,)),
            dma((2,)), dma((2,)), dma((2,)), dma((2,)), dma((2,)),
            pltpu.SemaphoreType.REGULAR,
        ],
        compiler_params=pltpu.CompilerParams(
            collective_id=0, has_side_effects=True, vmem_limit_bytes=67043328
        ),
    )(metric, amplitudes, virt_coef)
    return density, fitted_ao


def fits_cube(na, n, metric, amplitudes, virt_coef):
    p, per, (virt, ao) = metric.shape[0], amplitudes.shape[1], virt_coef.shape
    return (
        na == 4 and n == 8 and per % 1024 == 0 and p % 256 == 0
        and metric.shape[1] * n == na * p and virt <= p and virt + 2 * ao <= na * p
        and virt % 128 == 0 and ao % 128 == 0 and n * per % virt == 0
    )


def any_shards(na, n, metric, amplitudes, virt_coef):
    if fits_cube(na, n, metric, amplitudes, virt_coef):
        return cube_shards(na, n, 8, metric, amplitudes, virt_coef)
    return shards(na, n, metric, amplitudes, virt_coef)


def solution(mesh):
    in_specs = (P("aux", "pair"), P("aux", "pair"), P())
    out_specs = (P("aux", "pair"), P(("aux", "pair"), None))
    body = functools.partial(any_shards, mesh.shape["aux"], mesh.shape["pair"])
    return jax.shard_map(body, mesh=mesh, in_specs=in_specs, out_specs=out_specs, check_vma=False)
```

```python
import functools

import jax
import jax.numpy as jnp
from jax import lax
from jax.experimental import pallas as pl
from jax.experimental.pallas import tpu as pltpu
from jax.sharding import PartitionSpec as P

MESH = pl.DeviceIdType.MESH


def kernel(
    na, n, count, metric, amp, virt_coef, density, fitted_ao,
    m_v, a_v, d_v, f_v, g_v, c_v, one_v, two_v, o_v,
    m_send, m_recv, z_send, z_recv, x_send, x_recv, one_send, one_recv, two_send, two_recv, o_sem, local_sem,
):
    a, b = lax.axis_index("aux"), lax.axis_index("pair")
    p, q = metric.shape
    per = amp.shape[1]
    w = per // count
    rows = p // n
    virt, ao = virt_coef.shape
    half = n // 2
    parity, chip = lax.rem(b, 2), b // 2
    partner = b + 1 - 2 * parity
    tile = min(256, p)
    tiles = p // tile

    barrier = pltpu.get_barrier_semaphore()
    for d in range(1, n):
        pl.semaphore_signal(barrier, inc=1, device_id=(a, lax.rem(b + d, n)), device_id_type=MESH)

    @pl.when(a > 0)
    def _():
        pl.semaphore_signal(barrier, inc=1, device_id=(a - 1, b), device_id_type=MESH)

    @pl.when(a < na - 1)
    def _():
        pl.semaphore_signal(barrier, inc=1, device_id=(a + 1, b), device_id_type=MESH)

    pl.semaphore_wait(barrier, n - 1 + jnp.where(a > 0, 1, 0) + jnp.where(a < na - 1, 1, 0))

    def block_of(s, c):
        return a_v.at[c, pl.ds(pl.multiple_of(s * p, p), p), :]

    def hop(src, s, c, way, target):
        return pltpu.make_async_remote_copy(
            src_ref=src, dst_ref=block_of(s, c), send_sem=z_send.at[way, s, c],
            recv_sem=z_recv.at[s, c], device_id=(target, b), device_id_type=MESH,
        )

    def metric_copy(owner, target):
        return pltpu.make_async_remote_copy(
            src_ref=metric, dst_ref=m_v.at[:, pl.ds(pl.multiple_of(owner * q, q), q)],
            send_sem=m_send.at[target], recv_sem=m_recv.at[owner],
            device_id=(a, target), device_id_type=MESH,
        )

    def regroup(owner, target, c):
        return pltpu.make_async_remote_copy(
            src_ref=f_v.at[c, pl.ds(pl.multiple_of(target * rows, rows), rows), :],
            dst_ref=g_v.at[:, pl.ds(pl.multiple_of(owner * per + c * w, w), w)],
            send_sem=x_send.at[target, c], recv_sem=x_recv.at[owner, c],
            device_id=(a, target), device_id_type=MESH,
        )

    def staged(j):
        return m_v.at[:, pl.ds(pl.multiple_of(j * q, q), q)]

    def first(j):
        return pltpu.make_async_remote_copy(
            src_ref=staged(j), dst_ref=one_v.at[j // 2], send_sem=one_send.at[j // 2],
            recv_sem=one_recv.at[j // 2], device_id=(a, partner), device_id_type=MESH,
        )

    def second(source, j):
        return pltpu.make_async_remote_copy(
            src_ref=staged(j), dst_ref=two_v.at[source], send_sem=two_send.at[0, j // 2],
            recv_sem=two_recv.at[0, source], device_id=(a, j), device_id_type=MESH,
        )

    def mine(c):
        return amp.at[:, c * w : (c + 1) * w]

    for c in range(count):
        @pl.when(a > 0)
        def _():
            hop(mine(c), a, c, 0, jnp.maximum(a - 1, 0)).start()

        @pl.when(a < na - 1)
        def _():
            hop(mine(c), a, c, 1, jnp.minimum(a + 1, na - 1)).start()

    @pl.loop(1, n)
    def _(d):
        metric_copy(b, lax.rem(b + d, n)).start()

    own_copies = [pltpu.make_async_copy(mine(c), block_of(a, c), local_sem.at[c]) for c in range(count)]
    own_copies.append(pltpu.make_async_copy(metric, staged(b), local_sem.at[count]))
    own_copies.append(pltpu.make_async_copy(virt_coef, c_v, local_sem.at[count + 1]))
    for copy in own_copies:
        copy.start()

    def arrive(t, c):
        @pl.when(a - t >= 0)
        def _():
            s = jnp.maximum(a - t, 0)
            hop(block_of(s, c), s, c, 1, a).wait_recv()

            @pl.when(a < na - 1)
            def _():
                hop(block_of(s, c), s, c, 1, jnp.minimum(a + 1, na - 1)).start()

        @pl.when(a + t < na)
        def _():
            s = jnp.minimum(a + t, na - 1)
            hop(block_of(s, c), s, c, 0, a).wait_recv()

            @pl.when(a > 0)
            def _():
                hop(block_of(s, c), s, c, 0, jnp.maximum(a - 1, 0)).start()

    @pl.loop(1, na - 1)
    def _(t):
        @pl.loop(0, count)
        def _(c):
            arrive(t, c)

    for copy in own_copies:
        copy.wait()

    @pl.loop(1, n)
    def _(d):
        metric_copy(lax.rem(b + n - d, n), b).wait_recv()

    @pl.loop(1, n)
    def _(d):
        metric_copy(b, lax.rem(b + d, n)).wait_send()

    def row(r):
        return pl.ds(pl.multiple_of(r * tile, tile), tile)

    def product(j, r, c):
        right = a_v[c, pl.ds(pl.multiple_of(j * q, q), q), :]
        return lax.dot_general(
            f_v[c, row(r), :], right, (((1,), (1,)), ((), ())), preferred_element_type=jnp.float32
        )

    def fit(c):
        @pl.loop(0, tiles)
        def _(r):
            f_v[c, row(r), :] = jnp.dot(
                m_v[row(r), :], a_v[c], preferred_element_type=jnp.float32
            ).astype(f_v.dtype)

        @pl.loop(1, n)
        def _(d):
            regroup(b, lax.rem(b + d, n), c).start()

        pltpu.make_async_copy(
            f_v.at[c, pl.ds(pl.multiple_of(b * rows, rows), rows), :],
            g_v.at[:, pl.ds(pl.multiple_of(b * per + c * w, w), w)], x_send.at[b, c],
        ).start()

    @pl.loop(0, n * tiles)
    def _(i):
        d_v[i // tiles, row(lax.rem(i, tiles)), :] = jnp.zeros((tile, q), jnp.float32)

    @pl.loop(0, count - 1)
    def _(c):
        arrive(na - 1, c)
        fit(c)

        @pl.loop(0, n * tiles)
        def _(i):
            j, r = i // tiles, lax.rem(i, tiles)
            d_v[j, row(r), :] += product(j, r, c)

    last = count - 1
    arrive(na - 1, last)
    fit(last)

    quad = half == 4
    mid = p // 2
    near = (chip + 1 - 2 * lax.rem(chip, 2), lax.rem(chip + 2, 4))
    far = 3 - chip

    def turn(h):
        if not quad:
            return lax.rem(chip + h, half)
        return jnp.where(h == 0, far, jnp.where(h == 1, near[0], jnp.where(h == 2, near[1], chip)))

    @pl.loop(0, half)
    def _(h):
        j = 2 * turn(h) + 1 - parity

        @pl.loop(0, tiles)
        def _(r):
            m_v[row(r), pl.ds(pl.multiple_of(j * q, q), q)] = (
                d_v[j, row(r), :] + product(j, r, last)
            ).astype(m_v.dtype)

        first(j).start()

    @pl.loop(0, 0 if quad else half)
    def _(h):
        j = 2 * lax.rem(chip + h, half) + parity

        @pl.loop(0, tiles)
        def _(r):
            d_v[j, row(r), :] += product(j, r, last)

    def part(way):
        return pl.ds(way * mid, mid)

    def cast(slot, way):
        j = 2 * slot + parity
        m_v[part(way), pl.ds(pl.multiple_of(j * q, q), q)] = d_v[j, part(way), :].astype(m_v.dtype)

    def piece(slot, way, place, target):
        j = 2 * slot + parity
        return pltpu.make_async_remote_copy(
            src_ref=m_v.at[part(way), pl.ds(pl.multiple_of(j * q, q), q)],
            dst_ref=two_v.at[place, part(way), :], send_sem=two_send.at[way, place],
            recv_sem=two_recv.at[way, place], device_id=(a, 2 * target + parity), device_id_type=MESH,
        )

    def add_in(slot, place, way):
        j = 2 * slot + parity
        d_v[j, part(way), :] += two_v[place, part(way), :].astype(jnp.float32)

    if quad:
        for h in range(4):
            slot = (far, near[0], near[1], chip)[h]

            @pl.loop(0, tiles)
            def _(r, slot=slot):
                d_v[2 * slot + parity, row(r), :] += product(2 * slot + parity, r, last)

            first(2 * slot + parity).wait_recv()

            @pl.loop(0, tiles)
            def _(r, slot=slot):
                j = 2 * slot + parity
                d_v[j, row(r), :] += one_v[slot, row(r), :].astype(jnp.float32)

            if h == 0:
                for way in range(2):
                    cast(far, way)
                    piece(far, way, 0, near[way]).start()
            elif h < 3:
                cast(near[h - 1], h - 1)
                piece(near[h - 1], h - 1, 1, near[h - 1]).start()
    else:
        @pl.loop(1, half)
        def _(h):
            slot = lax.rem(chip + h, half)
            j = 2 * slot + parity
            first(j).wait_recv()

            @pl.loop(0, tiles)
            def _(r):
                m_v[row(r), pl.ds(pl.multiple_of(j * q, q), q)] = (
                    d_v[j, row(r), :] + one_v[slot, row(r), :].astype(jnp.float32)
                ).astype(m_v.dtype)

            second(chip, j).start()

        first(b).wait_recv()

        @pl.loop(0, tiles)
        def _(r):
            d_v[b, row(r), :] += one_v[chip, row(r), :].astype(jnp.float32)

    if quad:
        for way in range(2):
            other = near[1 - way]
            piece(other, way, 0, near[way]).wait_recv()
            add_in(other, 0, way)
            cast(other, way)
            piece(other, way, 2, other).start()

    @pl.loop(0, count)
    def _(c):
        pltpu.make_async_copy(
            f_v.at[c, pl.ds(pl.multiple_of(b * rows, rows), rows), :],
            g_v.at[:, pl.ds(pl.multiple_of(b * per + c * w, w), w)], x_send.at[b, c],
        ).wait()

        @pl.loop(1, n)
        def _(d):
            regroup(lax.rem(b + n - d, n), b, c).wait_recv()

    occ = n * per // virt

    def out_copy(i, slot):
        return pltpu.make_async_copy(
            o_v.at[slot], fitted_ao.at[:, pl.ds(pl.multiple_of(i * ao, ao), ao)], o_sem.at[slot]
        )

    @pl.loop(0, occ)
    def _(i):
        slot = lax.rem(i, 2)

        @pl.when(i >= 2)
        def _():
            out_copy(i - 2, slot).wait()

        o_v[slot] = jnp.dot(
            g_v[:, pl.ds(pl.multiple_of(i * virt, virt), virt)], c_v[...], preferred_element_type=jnp.float32
        ).astype(o_v.dtype)
        out_copy(i, slot).start()

    for i in range(max(occ - 2, 0), occ):
        out_copy(i, i % 2).wait()

    if quad:
        for way in range(2):
            piece(chip, way, 1, near[way]).wait_recv()
            add_in(chip, 1, way)
        for way in range(2):
            piece(chip, way, 2, near[1 - way]).wait_recv()
            add_in(chip, 2, way)
    else:
        @pl.loop(1, half)
        def _(h):
            source = lax.rem(chip + half - h, half)
            second(source, b).wait_recv()

            @pl.loop(0, tiles)
            def _(r):
                d_v[b, row(r), :] += two_v[source, row(r), :].astype(jnp.float32)

    result = pltpu.make_async_copy(d_v.at[b], density, local_sem.at[0])
    result.start()

    @pl.loop(0, half)
    def _(h):
        first(2 * h + 1 - parity).wait_send()

    if quad:
        for way in range(2):
            piece(far, way, 0, near[way]).wait_send()
            piece(near[way], way, 1, near[way]).wait_send()
            piece(near[1 - way], way, 2, near[1 - way]).wait_send()
    else:
        @pl.loop(1, half)
        def _(h):
            second(chip, 2 * lax.rem(chip + h, half) + parity).wait_send()

    @pl.loop(0, count)
    def _(c):
        @pl.loop(1, n)
        def _(d):
            regroup(b, lax.rem(b + d, n), c).wait_send()

        @pl.loop(0, na)
        def _(s):
            @pl.when(jnp.logical_and(s >= a, a > 0))
            def _():
                hop(block_of(s, c), s, c, 0, jnp.maximum(a - 1, 0)).wait_send()

            @pl.when(jnp.logical_and(s <= a, a < na - 1))
            def _():
                hop(block_of(s, c), s, c, 1, jnp.minimum(a + 1, na - 1)).wait_send()

    result.wait()


def shards(na, n, metric, amplitudes, virt_coef):
    p, q = metric.shape
    per = amplitudes.shape[1]
    virt, ao = virt_coef.shape
    count = next(c for c in (8, 4, 2, 1) if per % (128 * c) == 0)
    w = per // count
    rows = p // n
    bf16 = jnp.bfloat16
    dma = pltpu.SemaphoreType.DMA
    return pl.pallas_call(
        functools.partial(kernel, na, n, count),
        out_shape=(
            jax.ShapeDtypeStruct((p, q), jnp.float32),
            jax.ShapeDtypeStruct((rows, n * per // virt * ao), bf16),
        ),
        in_specs=[pl.BlockSpec(memory_space=pl.ANY)] * 3,
        out_specs=(pl.BlockSpec(memory_space=pl.ANY), pl.BlockSpec(memory_space=pl.ANY)),
        scratch_shapes=[
            pltpu.VMEM((p, n * q), bf16),
            pltpu.VMEM((count, na * p, w), bf16),
            pltpu.VMEM((n, p, q), jnp.float32),
            pltpu.VMEM((count, p, w), bf16),
            pltpu.VMEM((rows, n * per), bf16),
            pltpu.VMEM((virt, ao), bf16),
            pltpu.VMEM((n // 2, p, q), bf16),
            pltpu.VMEM((n // 2, p, q), bf16),
            pltpu.VMEM((2, rows, ao), bf16),
            dma((n,)), dma((n,)),
            dma((2, na, count)), dma((na, count)),
            dma((n, count)), dma((n, count)),
            dma((n // 2,)), dma((n // 2,)),
            dma((2, n // 2)), dma((2, n // 2)),
            dma((2,)), dma((count + 2,)),
        ],
        compiler_params=pltpu.CompilerParams(
            collective_id=0, has_side_effects=True, vmem_limit_bytes=67043328
        ),
    )(metric, amplitudes, virt_coef)

def cube_kernel(
    na, n, count, ha, metric, amp, virt_coef, density, fitted_ao, g_hbm,
    m_v, o_m, a_v, d_v, f_v, e_v, one_v, two_v,
    m_send, m_recv, z_send, z_recv, e_send, e_recv, x_send, x_recv,
    one_send, one_recv, two_send, two_recv, r_send, r_recv,
    mm_sem, fin_sem, g_sem, o_sem, local_sem, credit,
):
    a, b = lax.axis_index("aux"), lax.axis_index("pair")
    p, q = metric.shape
    per = amp.shape[1]
    w = per // count
    rows = p // n
    virt, ao = virt_coef.shape
    parity, chip = lax.rem(b, 2), b // 2
    flip = 1 - 2 * parity
    partner = b + flip
    near = (chip + 1 - 2 * lax.rem(chip, 2), lax.rem(chip + 2, 4))
    far = 3 - chip
    xb, yb, fb = 2 * near[0] + parity, 2 * near[1] + parity, 2 * far + parity
    tile = min(256, p)
    tiles = p // tile
    mid = p // 2
    last = count - 1

    middle = jnp.logical_and(a > 0, a < na - 1)
    end = jnp.logical_not(middle)
    mate = a + 1 - 2 * lax.rem(a, 2)
    across = na - 1 - a
    beyond = na - 1 - mate

    barrier = pltpu.get_barrier_semaphore()
    for d in range(1, n):
        pl.semaphore_signal(barrier, inc=1, device_id=(a, lax.rem(b + d, n)), device_id_type=MESH)
    pl.semaphore_signal(barrier, inc=1, device_id=(mate, b), device_id_type=MESH)

    @pl.when(middle)
    def _():
        pl.semaphore_signal(barrier, inc=1, device_id=(across, b), device_id_type=MESH)

    pl.semaphore_wait(barrier, n + jnp.where(middle, 1, 0))

    def at(c):
        if isinstance(c, int) and c >= last:
            return last * w + (c - last) * (w // 2), w // 2
        return c * w, w

    def cols(c, base=0):
        start, size = at(c)
        return pl.ds(pl.multiple_of(base + start, size), size)

    def row(r):
        return pl.ds(pl.multiple_of(r * tile, tile), tile)

    def part(way):
        return pl.ds(way * mid, mid)

    def wide(j):
        return pl.ds(pl.multiple_of(j * q, q), q)

    def block_of(s, c):
        return a_v.at[pl.ds(pl.multiple_of(s * p, p), p), cols(c)]

    def z(s, c, way, own=False):
        return pltpu.make_async_remote_copy(
            src_ref=amp.at[:, cols(c)] if own else block_of(s, c), dst_ref=block_of(s, c),
            send_sem=z_send.at[way, s, c], recv_sem=z_recv.at[s, c],
            device_id=(mate if way == 0 else across, b), device_id_type=MESH,
        )

    def relay(s, c, way):
        z(s, c, way).wait_recv()
        z(s, c, way).start()

    def lend():
        return pltpu.make_async_remote_copy(
            src_ref=metric, dst_ref=o_m.at[:, wide(b)], send_sem=mm_sem.at[0], recv_sem=mm_sem.at[1],
            device_id=(mate, b), device_id_type=MESH,
        )

    def give(c):
        return pltpu.make_async_remote_copy(
            src_ref=e_v.at[:, cols(c)], dst_ref=f_v.at[:, cols(c)], send_sem=e_send.at[c], recv_sem=e_recv.at[c],
            device_id=(mate, b), device_id_type=MESH,
        )

    def staged(j):
        return o_m.at[:, wide(j)]

    def finish():
        return pltpu.make_async_remote_copy(
            src_ref=staged(b), dst_ref=e_v.at[:, 0:q], send_sem=fin_sem.at[0], recv_sem=fin_sem.at[1],
            device_id=(mate, b), device_id_type=MESH,
        )

    def region(kind, mirror):
        mine = (b, b, b, xb, yb, xb, yb, fb, fb)
        theirs = (xb, yb, partner, fb, fb, xb + flip, yb + flip, fb + flip, fb + flip)
        half = (None, None, None, 0, 1, None, None, 0, 1)[kind]
        j = (theirs if mirror else mine)[kind]
        return (slice(None) if half is None else part(half), wide(j))

    def gather(g, kind, mirror=False):
        buf = (m_v, o_m)[g]
        where = region(kind, mirror)
        target = (xb, yb, partner, yb, xb, partner, partner, partner, partner)[kind]
        return pltpu.make_async_remote_copy(
            src_ref=metric if g == 0 and kind < 3 and not mirror else buf.at[where], dst_ref=buf.at[where],
            send_sem=m_send.at[g, kind], recv_sem=m_recv.at[g, kind],
            device_id=(a, target), device_id_type=MESH,
        )

    def got(g, kind):
        gather(g, kind, True).wait_recv()

    def gather_open(g):
        for kind in range(3):
            gather(g, kind).start()

    def gather_turn(g):
        got(g, 0)
        gather(g, 3).start()
        gather(g, 5).start()
        got(g, 1)
        gather(g, 4).start()
        gather(g, 6).start()

    def gather_close(g):
        got(g, 3)
        gather(g, 7).start()
        got(g, 4)
        gather(g, 8).start()
        for kind in (2, 5, 6, 7, 8):
            got(g, kind)
        for kind in range(9):
            gather(g, kind).wait_send()

    def regroup(owner, target, c):
        return pltpu.make_async_remote_copy(
            src_ref=f_v.at[pl.ds(pl.multiple_of(target * rows, rows), rows), cols(c)],
            dst_ref=g_hbm.at[:, cols(c, owner * per)],
            send_sem=x_send.at[target, c], recv_sem=x_recv.at[owner, c],
            device_id=(a, target), device_id_type=MESH,
        )

    def keep(c):
        return pltpu.make_async_copy(
            f_v.at[pl.ds(pl.multiple_of(b * rows, rows), rows), cols(c)],
            g_hbm.at[:, cols(c, b * per)], x_send.at[b, c],
        )

    def regroup_all(c):
        @pl.loop(1, n)
        def _(d):
            regroup(b, lax.rem(b + d, n), c).start()

        keep(c).start()

    def fit(mat, dst, c):
        @pl.loop(0, tiles)
        def _(r):
            dst[row(r), cols(c)] = jnp.dot(
                mat[row(r), :], a_v[:, cols(c)], preferred_element_type=jnp.float32
            ).astype(dst.dtype)

    def product(left, j, r, span):
        return lax.dot_general(
            left[row(r), span], a_v[wide(j), span], (((1,), (1,)), ((), ())), preferred_element_type=jnp.float32
        )

    early = slice(0, ha * w)
    most = slice(0, (last - 1) * w)

    def first(turn, j):
        return pltpu.make_async_remote_copy(
            src_ref=staged(j), dst_ref=one_v.at[j // 2], send_sem=one_send.at[turn, j // 2],
            recv_sem=one_recv.at[turn, j // 2], device_id=(a, partner), device_id_type=MESH,
        )

    def direct(kind):
        target = (xb, yb, fb)[kind]
        return pltpu.make_async_remote_copy(
            src_ref=staged(target), dst_ref=two_v.at[kind], send_sem=r_send.at[kind],
            recv_sem=r_recv.at[kind], device_id=(a, target), device_id_type=MESH,
        )

    own_copies = [
        pltpu.make_async_copy(amp, a_v.at[pl.ds(pl.multiple_of(a * p, p), p), :], local_sem.at[0]),
        pltpu.make_async_copy(metric, m_v.at[:, wide(b)], local_sem.at[1]),
    ]

    gather_open(0)

    @pl.when(end)
    def _():
        lend().start()
        for c in range(count + 1):
            z(a, c, 0, True).start()

    @pl.when(middle)
    def _():
        for c in (ha, ha + 1, 0):
            z(a, c, 1, True).start()
        for c in range(ha, count + 1):
            z(a, c, 0, True).start()

    for copy in own_copies:
        copy.start()

    @pl.loop(0, n * tiles)
    def _(i):
        d_v[i // tiles, row(lax.rem(i, tiles)), :] = jnp.zeros((tile, q), jnp.float32)

    @pl.when(end)
    def _():
        gather_turn(0)
        gather_close(0)

    @pl.when(middle)
    def _():
        lend().wait_recv()
        gather_open(1)
        relay(across, ha, 0)
        relay(across, ha + 1, 0)
        relay(mate, 0, 1)
        z(a, 1, 1, True).start()
        gather_turn(1)
        relay(mate, 1, 1)
        z(a, 2, 1, True).start()
        gather_turn(0)
        relay(mate, 2, 1)
        z(a, 3, 1, True).start()
        gather_close(1)

    for copy in own_copies:
        copy.wait()

    def accumulate(left, span, low=0, high=n):
        @pl.loop(low * tiles, high * tiles)
        def _(i):
            j, r = i // tiles, lax.rem(i, tiles)
            d_v[j, row(r), :] += product(left, j, r, span)

    def arrive_early(c):
        @pl.when(middle)
        def _():
            z(across, c, 0).wait_recv()
            z(beyond, c, 0).wait_recv()

        @pl.when(end)
        def _():
            give(c).wait_recv()

    def arrive_late(c):
        @pl.when(middle)
        def _():
            relay(beyond, c, 0)

        @pl.when(end)
        def _():
            for source in (mate, across, beyond):
                z(source, c, 0).wait_recv()

    def first_share():
        @pl.loop(0, n // 2)
        def _(h):
            j = 2 * h + 1 - parity

            @pl.loop(0, tiles)
            def _(r):
                o_m[row(r), wide(j)] = product(e_v, j, r, early).astype(o_m.dtype)

            first(0, j).start()

    def first_total(j, r):
        return product(e_v, j, r, early) + one_v[j // 2, row(r), :].astype(jnp.float32)

    def second_share():
        for kind in (2, 0, 1):
            j = (xb, yb, fb)[kind]
            first(0, j).wait_recv()

            @pl.loop(0, tiles)
            def _(r, j=j):
                o_m[row(r), wide(j)] = first_total(j, r).astype(o_m.dtype)

            direct(kind).start()

    def third_share():
        first(0, b).wait_recv()
        for kind in range(3):
            direct(kind).wait_recv()

        @pl.loop(0, tiles)
        def _(r):
            total = first_total(b, r)
            for kind in range(3):
                total += two_v[kind, row(r), :].astype(jnp.float32)
            o_m[row(r), wide(b)] = total.astype(o_m.dtype)

        for target in (partner, xb, yb):
            pl.semaphore_signal(credit, inc=1, device_id=(a, target), device_id_type=MESH)

        @pl.loop(0, n // 2)
        def _(h):
            first(0, 2 * h + 1 - parity).wait_send()

        for kind in range(3):
            direct(kind).wait_send()

    @pl.loop(0, last)
    def _(c):
        @pl.when(c < ha)
        def _():
            arrive_early(jnp.minimum(c, ha - 1))

        @pl.when(jnp.logical_and(middle, c < ha))
        def _():
            k = jnp.minimum(c, ha - 1)
            fit(o_m, e_v, k)
            give(k).start()
            relay(mate, k + 3, 1)

            @pl.when(c == 0)
            def _():
                gather_close(0)

            @pl.when(c == ha - 2)
            def _():
                z(a, last - 1, 1, True).start()

            @pl.when(c == ha - 1)
            def _():
                z(a, last, 1, True).start()
                z(a, last + 1, 1, True).start()

        @pl.when(jnp.logical_and(middle, c == ha))
        def _():
            relay(mate, last, 1)
            relay(mate, last + 1, 1)

        @pl.when(jnp.logical_and(middle, c == last - 1))
        def _():
            relay(across, last - 1, 0)
            accumulate(f_v, most, n // 2, n)

        @pl.when(c >= ha)
        def _():
            arrive_late(c)

        @pl.when(jnp.logical_and(middle, c == ha))
        def _():
            second_share()

        @pl.when(jnp.logical_or(middle, c >= ha))
        def _():
            fit(m_v, f_v, c)

        regroup_all(c)

        @pl.when(jnp.logical_and(middle, c == ha - 1))
        def _():
            first_share()

        @pl.when(jnp.logical_and(middle, c == last - 2))
        def _():
            accumulate(f_v, most, 0, n // 2)

        @pl.when(jnp.logical_and(middle, c == last - 1))
        def _():
            relay(across, last, 0)
            relay(across, last + 1, 0)

        @pl.when(jnp.logical_or(jnp.logical_and(end, c >= ha), c == last - 1))
        def _():
            accumulate(f_v, cols(c))

    for c in (last, last + 1):
        arrive_late(c)
        fit(m_v, f_v, c)
        regroup_all(c)

    @pl.when(middle)
    def _():
        third_share()
        finish().start()
        pl.semaphore_wait(credit, 3)

    late = slice(last * w, count * w)
    turns = (far, near[0], near[1], chip)

    def for_partner(slot):
        j = 2 * slot + 1 - parity

        @pl.loop(0, tiles)
        def _(r):
            o_m[row(r), wide(j)] = (d_v[j, row(r), :] + product(f_v, j, r, late)).astype(o_m.dtype)

        first(1, j).start()

    def piece(slot, way, place, target):
        return pltpu.make_async_remote_copy(
            src_ref=o_m.at[part(way), wide(2 * slot + parity)],
            dst_ref=two_v.at[place, part(way), :], send_sem=two_send.at[way, place],
            recv_sem=two_recv.at[way, place], device_id=(a, 2 * target + parity), device_id_type=MESH,
        )

    def add_in(slot, place, way):
        d_v[2 * slot + parity, part(way), :] += two_v[place, part(way), :].astype(jnp.float32)

    for_partner(far)
    for h in range(4):
        if h < 3:
            for_partner(turns[h + 1])
        slot = turns[h]
        j = 2 * slot + parity
        first(1, j).wait_recv()

        @pl.loop(0, tiles)
        def _(r, slot=slot, j=j, h=h):
            total = d_v[j, row(r), :] + product(f_v, j, r, late) + one_v[slot, row(r), :].astype(jnp.float32)
            if h < 3:
                o_m[row(r), wide(j)] = total.astype(o_m.dtype)
            if h > 0:
                d_v[j, row(r), :] = total

        if h == 0:
            for way in range(2):
                piece(far, way, 0, near[way]).start()
        elif h < 3:
            piece(near[h - 1], h - 1, 1, near[h - 1]).start()

    for way in range(2):
        other = near[1 - way]
        j = 2 * other + parity
        piece(other, way, 0, near[way]).wait_recv()
        o_m[part(way), wide(j)] = (d_v[j, part(way), :] + two_v[0, part(way), :].astype(jnp.float32)).astype(o_m.dtype)
        piece(other, way, 2, other).start()

    coef = m_v.at[pl.ds(0, virt), pl.ds(0, ao)]
    load_coef = pltpu.make_async_copy(virt_coef, coef, local_sem.at[0])
    load_coef.start()

    def regrouped(c):
        keep(c).wait()

        @pl.loop(1, n)
        def _(d):
            regroup(lax.rem(b + n - d, n), b, c).wait_recv()

    @pl.loop(0, last)
    def _(c):
        regrouped(c)

    regrouped(last)
    regrouped(last + 1)

    occ = n * per // virt

    def slot_rows(slot):
        return pl.ds(pl.multiple_of(slot * rows, rows), rows)

    def block_copy(i, slot):
        return pltpu.make_async_copy(
            g_hbm.at[:, pl.ds(pl.multiple_of(i * virt, virt), virt)],
            m_v.at[slot_rows(slot), pl.ds(ao, virt)], g_sem.at[slot],
        )

    def out_copy(i, slot):
        return pltpu.make_async_copy(
            m_v.at[slot_rows(slot), pl.ds(ao + virt, ao)],
            fitted_ao.at[:, pl.ds(pl.multiple_of(i * ao, ao), ao)], o_sem.at[slot],
        )

    block_copy(0, 0).start()
    load_coef.wait()

    @pl.loop(0, occ)
    def _(i):
        slot = lax.rem(i, 2)

        @pl.when(i + 1 < occ)
        def _():
            block_copy(i + 1, 1 - slot).start()

        @pl.when(i >= 2)
        def _():
            out_copy(i - 2, slot).wait()

        block_copy(i, slot).wait()
        m_v[slot_rows(slot), pl.ds(ao + virt, ao)] = jnp.dot(
            m_v[slot_rows(slot), pl.ds(ao, virt)], m_v[pl.ds(0, virt), pl.ds(0, ao)],
            preferred_element_type=jnp.float32,
        ).astype(m_v.dtype)
        out_copy(i, slot).start()

    for i in range(max(occ - 2, 0), occ):
        out_copy(i, i % 2).wait()

    for way in range(2):
        piece(chip, way, 1, near[way]).wait_recv()
        add_in(chip, 1, way)
    for way in range(2):
        piece(chip, way, 2, near[1 - way]).wait_recv()
        add_in(chip, 2, way)

    @pl.when(end)
    def _():
        finish().wait_recv()

        @pl.loop(0, tiles)
        def _(r):
            d_v[b, row(r), :] += e_v[row(r), 0:q].astype(jnp.float32)

    result = pltpu.make_async_copy(d_v.at[b], density, local_sem.at[0])
    result.start()

    @pl.loop(0, n // 2)
    def _(h):
        first(1, 2 * h + 1 - parity).wait_send()

    for way in range(2):
        piece(far, way, 0, near[way]).wait_send()
        piece(near[way], way, 1, near[way]).wait_send()
        piece(near[1 - way], way, 2, near[1 - way]).wait_send()

    def regroup_sent(c):
        @pl.loop(1, n)
        def _(d):
            regroup(b, lax.rem(b + d, n), c).wait_send()

    @pl.loop(0, last)
    def _(c):
        regroup_sent(c)

    regroup_sent(last)
    regroup_sent(last + 1)

    @pl.when(end)
    def _():
        lend().wait_send()
        for c in range(count + 1):
            z(a, c, 0, True).wait_send()

    @pl.when(middle)
    def _():
        finish().wait_send()

        @pl.loop(0, ha)
        def _(c):
            give(c).wait_send()

        for c in range(count + 1):
            z(a, c, 1, True).wait_send()
            z(mate, c, 1).wait_send()
        for c in range(ha, count + 1):
            z(a, c, 0, True).wait_send()
            z(across, c, 0).wait_send()
            z(beyond, c, 0).wait_send()

    result.wait()


def cube_shards(na, n, count, metric, amplitudes, virt_coef):
    p, q = metric.shape
    per = amplitudes.shape[1]
    virt, ao = virt_coef.shape
    ha = count // 2
    rows = p // n
    bf16 = jnp.bfloat16
    dma = pltpu.SemaphoreType.DMA
    density, fitted_ao, _ = pl.pallas_call(
        functools.partial(cube_kernel, na, n, count, ha),
        out_shape=(
            jax.ShapeDtypeStruct((p, q), jnp.float32),
            jax.ShapeDtypeStruct((rows, n * per // virt * ao), bf16),
            jax.ShapeDtypeStruct((rows, n * per), bf16),
        ),
        in_specs=[pl.BlockSpec(memory_space=pl.ANY)] * 3,
        out_specs=(pl.BlockSpec(memory_space=pl.ANY),) * 3,
        scratch_shapes=[
            pltpu.VMEM((p, n * q), bf16),
            pltpu.VMEM((p, n * q), bf16),
            pltpu.VMEM((na * p, per), bf16),
            pltpu.VMEM((n, p, q), jnp.float32),
            pltpu.VMEM((p, per), bf16),
            pltpu.VMEM((p, max(per * ha // count, q)), bf16),
            pltpu.VMEM((n // 2, p, q), bf16),
            pltpu.VMEM((3, p, q), bf16),
            dma((2, 9)), dma((2, 9)),
            dma((2, na, count + 1)), dma((na, count + 1)),
            dma((ha,)), dma((ha,)),
            dma((n, count + 1)), dma((n, count + 1)),
            dma((2, n // 2)), dma((2, n // 2)),
            dma((2, 3)), dma((2, 3)),
            dma((3,)), dma((3,)),
            dma((2,)), dma((2,)), dma((2,)), dma((2,)), dma((2,)),
            pltpu.SemaphoreType.REGULAR,
        ],
        compiler_params=pltpu.CompilerParams(
            collective_id=0, has_side_effects=True, vmem_limit_bytes=67043328
        ),
    )(metric, amplitudes, virt_coef)
    return density, fitted_ao


def fits_cube(na, n, metric, amplitudes, virt_coef):
    p, per, (virt, ao) = metric.shape[0], amplitudes.shape[1], virt_coef.shape
    return (
        na == 4 and n == 8 and per % 2048 == 0 and p % 256 == 0
        and metric.shape[1] * n == na * p and virt <= p and virt + 2 * ao <= na * p
        and virt % 128 == 0 and ao % 128 == 0 and n * per % virt == 0
    )


def any_shards(na, n, metric, amplitudes, virt_coef):
    if fits_cube(na, n, metric, amplitudes, virt_coef):
        return cube_shards(na, n, 8, metric, amplitudes, virt_coef)
    return shards(na, n, metric, amplitudes, virt_coef)


def solution(mesh):
    in_specs = (P("aux", "pair"), P("aux", "pair"), P())
    out_specs = (P("aux", "pair"), P(("aux", "pair"), None))
    body = functools.partial(any_shards, mesh.shape["aux"], mesh.shape["pair"])
    return jax.shard_map(body, mesh=mesh, in_specs=in_specs, out_specs=out_specs, check_vma=False)
```

```python
import functools

import jax
import jax.numpy as jnp
from jax import lax
from jax.experimental import pallas as pl
from jax.experimental.pallas import tpu as pltpu
from jax.sharding import PartitionSpec as P

MESH = pl.DeviceIdType.MESH


def kernel(
    na, n, count, metric, amp, virt_coef, density, fitted_ao,
    m_v, a_v, d_v, f_v, g_v, c_v, one_v, two_v, o_v,
    m_send, m_recv, z_send, z_recv, x_send, x_recv, one_send, one_recv, two_send, two_recv, o_sem, local_sem,
):
    a, b = lax.axis_index("aux"), lax.axis_index("pair")
    p, q = metric.shape
    per = amp.shape[1]
    w = per // count
    rows = p // n
    virt, ao = virt_coef.shape
    half = n // 2
    parity, chip = lax.rem(b, 2), b // 2
    partner = b + 1 - 2 * parity
    tile = min(256, p)
    tiles = p // tile

    barrier = pltpu.get_barrier_semaphore()
    for d in range(1, n):
        pl.semaphore_signal(barrier, inc=1, device_id=(a, lax.rem(b + d, n)), device_id_type=MESH)

    @pl.when(a > 0)
    def _():
        pl.semaphore_signal(barrier, inc=1, device_id=(a - 1, b), device_id_type=MESH)

    @pl.when(a < na - 1)
    def _():
        pl.semaphore_signal(barrier, inc=1, device_id=(a + 1, b), device_id_type=MESH)

    pl.semaphore_wait(barrier, n - 1 + jnp.where(a > 0, 1, 0) + jnp.where(a < na - 1, 1, 0))

    def block_of(s, c):
        return a_v.at[c, pl.ds(pl.multiple_of(s * p, p), p), :]

    def hop(src, s, c, way, target):
        return pltpu.make_async_remote_copy(
            src_ref=src, dst_ref=block_of(s, c), send_sem=z_send.at[way, s, c],
            recv_sem=z_recv.at[s, c], device_id=(target, b), device_id_type=MESH,
        )

    def metric_copy(owner, target):
        return pltpu.make_async_remote_copy(
            src_ref=metric, dst_ref=m_v.at[:, pl.ds(pl.multiple_of(owner * q, q), q)],
            send_sem=m_send.at[target], recv_sem=m_recv.at[owner],
            device_id=(a, target), device_id_type=MESH,
        )

    def regroup(owner, target, c):
        return pltpu.make_async_remote_copy(
            src_ref=f_v.at[c, pl.ds(pl.multiple_of(target * rows, rows), rows), :],
            dst_ref=g_v.at[:, pl.ds(pl.multiple_of(owner * per + c * w, w), w)],
            send_sem=x_send.at[target, c], recv_sem=x_recv.at[owner, c],
            device_id=(a, target), device_id_type=MESH,
        )

    def staged(j):
        return m_v.at[:, pl.ds(pl.multiple_of(j * q, q), q)]

    def first(j):
        return pltpu.make_async_remote_copy(
            src_ref=staged(j), dst_ref=one_v.at[j // 2], send_sem=one_send.at[j // 2],
            recv_sem=one_recv.at[j // 2], device_id=(a, partner), device_id_type=MESH,
        )

    def second(source, j):
        return pltpu.make_async_remote_copy(
            src_ref=staged(j), dst_ref=two_v.at[source], send_sem=two_send.at[0, j // 2],
            recv_sem=two_recv.at[0, source], device_id=(a, j), device_id_type=MESH,
        )

    def mine(c):
        return amp.at[:, c * w : (c + 1) * w]

    for c in range(count):
        @pl.when(a > 0)
        def _():
            hop(mine(c), a, c, 0, jnp.maximum(a - 1, 0)).start()

        @pl.when(a < na - 1)
        def _():
            hop(mine(c), a, c, 1, jnp.minimum(a + 1, na - 1)).start()

    @pl.loop(1, n)
    def _(d):
        metric_copy(b, lax.rem(b + d, n)).start()

    own_copies = [pltpu.make_async_copy(mine(c), block_of(a, c), local_sem.at[c]) for c in range(count)]
    own_copies.append(pltpu.make_async_copy(metric, staged(b), local_sem.at[count]))
    own_copies.append(pltpu.make_async_copy(virt_coef, c_v, local_sem.at[count + 1]))
    for copy in own_copies:
        copy.start()

    def arrive(t, c):
        @pl.when(a - t >= 0)
        def _():
            s = jnp.maximum(a - t, 0)
            hop(block_of(s, c), s, c, 1, a).wait_recv()

            @pl.when(a < na - 1)
            def _():
                hop(block_of(s, c), s, c, 1, jnp.minimum(a + 1, na - 1)).start()

        @pl.when(a + t < na)
        def _():
            s = jnp.minimum(a + t, na - 1)
            hop(block_of(s, c), s, c, 0, a).wait_recv()

            @pl.when(a > 0)
            def _():
                hop(block_of(s, c), s, c, 0, jnp.maximum(a - 1, 0)).start()

    @pl.loop(1, na - 1)
    def _(t):
        @pl.loop(0, count)
        def _(c):
            arrive(t, c)

    for copy in own_copies:
        copy.wait()

    @pl.loop(1, n)
    def _(d):
        metric_copy(lax.rem(b + n - d, n), b).wait_recv()

    @pl.loop(1, n)
    def _(d):
        metric_copy(b, lax.rem(b + d, n)).wait_send()

    def row(r):
        return pl.ds(pl.multiple_of(r * tile, tile), tile)

    def product(j, r, c):
        right = a_v[c, pl.ds(pl.multiple_of(j * q, q), q), :]
        return lax.dot_general(
            f_v[c, row(r), :], right, (((1,), (1,)), ((), ())), preferred_element_type=jnp.float32
        )

    def fit(c):
        @pl.loop(0, tiles)
        def _(r):
            f_v[c, row(r), :] = jnp.dot(
                m_v[row(r), :], a_v[c], preferred_element_type=jnp.float32
            ).astype(f_v.dtype)

        @pl.loop(1, n)
        def _(d):
            regroup(b, lax.rem(b + d, n), c).start()

        pltpu.make_async_copy(
            f_v.at[c, pl.ds(pl.multiple_of(b * rows, rows), rows), :],
            g_v.at[:, pl.ds(pl.multiple_of(b * per + c * w, w), w)], x_send.at[b, c],
        ).start()

    @pl.loop(0, n * tiles)
    def _(i):
        d_v[i // tiles, row(lax.rem(i, tiles)), :] = jnp.zeros((tile, q), jnp.float32)

    @pl.loop(0, count - 1)
    def _(c):
        arrive(na - 1, c)
        fit(c)

        @pl.loop(0, n * tiles)
        def _(i):
            j, r = i // tiles, lax.rem(i, tiles)
            d_v[j, row(r), :] += product(j, r, c)

    last = count - 1
    arrive(na - 1, last)
    fit(last)

    quad = half == 4
    mid = p // 2
    near = (chip + 1 - 2 * lax.rem(chip, 2), lax.rem(chip + 2, 4))
    far = 3 - chip

    def turn(h):
        if not quad:
            return lax.rem(chip + h, half)
        return jnp.where(h == 0, far, jnp.where(h == 1, near[0], jnp.where(h == 2, near[1], chip)))

    @pl.loop(0, half)
    def _(h):
        j = 2 * turn(h) + 1 - parity

        @pl.loop(0, tiles)
        def _(r):
            m_v[row(r), pl.ds(pl.multiple_of(j * q, q), q)] = (
                d_v[j, row(r), :] + product(j, r, last)
            ).astype(m_v.dtype)

        first(j).start()

    @pl.loop(0, 0 if quad else half)
    def _(h):
        j = 2 * lax.rem(chip + h, half) + parity

        @pl.loop(0, tiles)
        def _(r):
            d_v[j, row(r), :] += product(j, r, last)

    def part(way):
        return pl.ds(way * mid, mid)

    def cast(slot, way):
        j = 2 * slot + parity
        m_v[part(way), pl.ds(pl.multiple_of(j * q, q), q)] = d_v[j, part(way), :].astype(m_v.dtype)

    def piece(slot, way, place, target):
        j = 2 * slot + parity
        return pltpu.make_async_remote_copy(
            src_ref=m_v.at[part(way), pl.ds(pl.multiple_of(j * q, q), q)],
            dst_ref=two_v.at[place, part(way), :], send_sem=two_send.at[way, place],
            recv_sem=two_recv.at[way, place], device_id=(a, 2 * target + parity), device_id_type=MESH,
        )

    def add_in(slot, place, way):
        j = 2 * slot + parity
        d_v[j, part(way), :] += two_v[place, part(way), :].astype(jnp.float32)

    if quad:
        for h in range(4):
            slot = (far, near[0], near[1], chip)[h]

            @pl.loop(0, tiles)
            def _(r, slot=slot):
                d_v[2 * slot + parity, row(r), :] += product(2 * slot + parity, r, last)

            first(2 * slot + parity).wait_recv()

            @pl.loop(0, tiles)
            def _(r, slot=slot):
                j = 2 * slot + parity
                d_v[j, row(r), :] += one_v[slot, row(r), :].astype(jnp.float32)

            if h == 0:
                for way in range(2):
                    cast(far, way)
                    piece(far, way, 0, near[way]).start()
            elif h < 3:
                cast(near[h - 1], h - 1)
                piece(near[h - 1], h - 1, 1, near[h - 1]).start()
    else:
        @pl.loop(1, half)
        def _(h):
            slot = lax.rem(chip + h, half)
            j = 2 * slot + parity
            first(j).wait_recv()

            @pl.loop(0, tiles)
            def _(r):
                m_v[row(r), pl.ds(pl.multiple_of(j * q, q), q)] = (
                    d_v[j, row(r), :] + one_v[slot, row(r), :].astype(jnp.float32)
                ).astype(m_v.dtype)

            second(chip, j).start()

        first(b).wait_recv()

        @pl.loop(0, tiles)
        def _(r):
            d_v[b, row(r), :] += one_v[chip, row(r), :].astype(jnp.float32)

    if quad:
        for way in range(2):
            other = near[1 - way]
            piece(other, way, 0, near[way]).wait_recv()
            add_in(other, 0, way)
            cast(other, way)
            piece(other, way, 2, other).start()

    @pl.loop(0, count)
    def _(c):
        pltpu.make_async_copy(
            f_v.at[c, pl.ds(pl.multiple_of(b * rows, rows), rows), :],
            g_v.at[:, pl.ds(pl.multiple_of(b * per + c * w, w), w)], x_send.at[b, c],
        ).wait()

        @pl.loop(1, n)
        def _(d):
            regroup(lax.rem(b + n - d, n), b, c).wait_recv()

    occ = n * per // virt

    def out_copy(i, slot):
        return pltpu.make_async_copy(
            o_v.at[slot], fitted_ao.at[:, pl.ds(pl.multiple_of(i * ao, ao), ao)], o_sem.at[slot]
        )

    @pl.loop(0, occ)
    def _(i):
        slot = lax.rem(i, 2)

        @pl.when(i >= 2)
        def _():
            out_copy(i - 2, slot).wait()

        o_v[slot] = jnp.dot(
            g_v[:, pl.ds(pl.multiple_of(i * virt, virt), virt)], c_v[...], preferred_element_type=jnp.float32
        ).astype(o_v.dtype)
        out_copy(i, slot).start()

    for i in range(max(occ - 2, 0), occ):
        out_copy(i, i % 2).wait()

    if quad:
        for way in range(2):
            piece(chip, way, 1, near[way]).wait_recv()
            add_in(chip, 1, way)
        for way in range(2):
            piece(chip, way, 2, near[1 - way]).wait_recv()
            add_in(chip, 2, way)
    else:
        @pl.loop(1, half)
        def _(h):
            source = lax.rem(chip + half - h, half)
            second(source, b).wait_recv()

            @pl.loop(0, tiles)
            def _(r):
                d_v[b, row(r), :] += two_v[source, row(r), :].astype(jnp.float32)

    result = pltpu.make_async_copy(d_v.at[b], density, local_sem.at[0])
    result.start()

    @pl.loop(0, half)
    def _(h):
        first(2 * h + 1 - parity).wait_send()

    if quad:
        for way in range(2):
            piece(far, way, 0, near[way]).wait_send()
            piece(near[way], way, 1, near[way]).wait_send()
            piece(near[1 - way], way, 2, near[1 - way]).wait_send()
    else:
        @pl.loop(1, half)
        def _(h):
            second(chip, 2 * lax.rem(chip + h, half) + parity).wait_send()

    @pl.loop(0, count)
    def _(c):
        @pl.loop(1, n)
        def _(d):
            regroup(b, lax.rem(b + d, n), c).wait_send()

        @pl.loop(0, na)
        def _(s):
            @pl.when(jnp.logical_and(s >= a, a > 0))
            def _():
                hop(block_of(s, c), s, c, 0, jnp.maximum(a - 1, 0)).wait_send()

            @pl.when(jnp.logical_and(s <= a, a < na - 1))
            def _():
                hop(block_of(s, c), s, c, 1, jnp.minimum(a + 1, na - 1)).wait_send()

    result.wait()


def shards(na, n, metric, amplitudes, virt_coef):
    p, q = metric.shape
    per = amplitudes.shape[1]
    virt, ao = virt_coef.shape
    count = next(c for c in (8, 4, 2, 1) if per % (128 * c) == 0)
    w = per // count
    rows = p // n
    bf16 = jnp.bfloat16
    dma = pltpu.SemaphoreType.DMA
    return pl.pallas_call(
        functools.partial(kernel, na, n, count),
        out_shape=(
            jax.ShapeDtypeStruct((p, q), jnp.float32),
            jax.ShapeDtypeStruct((rows, n * per // virt * ao), bf16),
        ),
        in_specs=[pl.BlockSpec(memory_space=pl.ANY)] * 3,
        out_specs=(pl.BlockSpec(memory_space=pl.ANY), pl.BlockSpec(memory_space=pl.ANY)),
        scratch_shapes=[
            pltpu.VMEM((p, n * q), bf16),
            pltpu.VMEM((count, na * p, w), bf16),
            pltpu.VMEM((n, p, q), jnp.float32),
            pltpu.VMEM((count, p, w), bf16),
            pltpu.VMEM((rows, n * per), bf16),
            pltpu.VMEM((virt, ao), bf16),
            pltpu.VMEM((n // 2, p, q), bf16),
            pltpu.VMEM((n // 2, p, q), bf16),
            pltpu.VMEM((2, rows, ao), bf16),
            dma((n,)), dma((n,)),
            dma((2, na, count)), dma((na, count)),
            dma((n, count)), dma((n, count)),
            dma((n // 2,)), dma((n // 2,)),
            dma((2, n // 2)), dma((2, n // 2)),
            dma((2,)), dma((count + 2,)),
        ],
        compiler_params=pltpu.CompilerParams(
            collective_id=0, has_side_effects=True, vmem_limit_bytes=67043328
        ),
    )(metric, amplitudes, virt_coef)

def cube_kernel(
    na, n, count, ha, metric, amp, virt_coef, part_hbm, late_hbm, fitted_ao, g_hbm,
    m_v, o_m, a_v, t_v, s_v, f_v, e_v, one_v, two_v,
    m_send, m_recv, z_send, z_recv, e_send, e_recv, x_send, x_recv,
    one_send, one_recv, two_send, two_recv, r_send, r_recv,
    mm_sem, fin_sem, g_sem, o_sem, local_sem,
):
    a, b = lax.axis_index("aux"), lax.axis_index("pair")
    p, q = metric.shape
    per = amp.shape[1]
    w = per // count
    rows = p // n
    virt, ao = virt_coef.shape
    parity, chip = lax.rem(b, 2), b // 2
    flip = 1 - 2 * parity
    partner = b + flip
    near = (chip + 1 - 2 * lax.rem(chip, 2), lax.rem(chip + 2, 4))
    far = 3 - chip
    xb, yb, fb = 2 * near[0] + parity, 2 * near[1] + parity, 2 * far + parity
    tile = min(256, p)
    tiles = p // tile
    mid = p // 2
    last = count - 1

    middle = jnp.logical_and(a > 0, a < na - 1)
    end = jnp.logical_not(middle)
    mate = a + 1 - 2 * lax.rem(a, 2)
    across = na - 1 - a
    beyond = na - 1 - mate

    barrier = pltpu.get_barrier_semaphore()
    for d in range(1, n):
        pl.semaphore_signal(barrier, inc=1, device_id=(a, lax.rem(b + d, n)), device_id_type=MESH)
    pl.semaphore_signal(barrier, inc=1, device_id=(mate, b), device_id_type=MESH)

    @pl.when(middle)
    def _():
        pl.semaphore_signal(barrier, inc=1, device_id=(across, b), device_id_type=MESH)

    pl.semaphore_wait(barrier, n + jnp.where(middle, 1, 0))

    v = w // 2

    def cols(c, base=0):
        return pl.ds(pl.multiple_of(base + c * w, w), w)

    def half(k, base=0):
        return pl.ds(pl.multiple_of(base + k * v, v), v)

    def row(r):
        return pl.ds(pl.multiple_of(r * tile, tile), tile)

    def part(way):
        return pl.ds(way * mid, mid)

    def wide(j):
        return pl.ds(pl.multiple_of(j * q, q), q)

    def block_of(s, k):
        return a_v.at[pl.ds(pl.multiple_of(s * p, p), p), half(k)]

    def z(s, k, way, own=False):
        return pltpu.make_async_remote_copy(
            src_ref=amp.at[:, half(k)] if own else block_of(s, k), dst_ref=block_of(s, k),
            send_sem=z_send.at[way, s, k], recv_sem=z_recv.at[s, k],
            device_id=(mate if way == 0 else across, b), device_id_type=MESH,
        )

    def own(way, *halves):
        for k in halves:
            z(a, k, way, True).start()

    def relay(s, k, way):
        z(s, k, way).wait_recv()
        z(s, k, way).start()

    def lend():
        return pltpu.make_async_remote_copy(
            src_ref=metric, dst_ref=o_m.at[:, wide(b)], send_sem=mm_sem.at[0], recv_sem=mm_sem.at[1],
            device_id=(mate, b), device_id_type=MESH,
        )

    def give(k):
        return pltpu.make_async_remote_copy(
            src_ref=e_v.at[:, half(k)], dst_ref=f_v.at[:, half(k)], send_sem=e_send.at[k], recv_sem=e_recv.at[k],
            device_id=(mate, b), device_id_type=MESH,
        )

    def staged(j):
        return o_m.at[:, wide(j)]

    def finish():
        return pltpu.make_async_remote_copy(
            src_ref=staged(b), dst_ref=late_hbm.at[2], send_sem=fin_sem.at[0], recv_sem=fin_sem.at[1],
            device_id=(mate, b), device_id_type=MESH,
        )

    def region(kind, mirror):
        mine = (b, b, b, xb, yb, xb, yb, fb, fb)
        theirs = (xb, yb, partner, fb, fb, xb + flip, yb + flip, fb + flip, fb + flip)
        side = (None, None, None, 0, 1, None, None, 0, 1)[kind]
        j = (theirs if mirror else mine)[kind]
        return (slice(None) if side is None else part(side), wide(j))

    def gather(g, kind, mirror=False):
        buf = (m_v, o_m)[g]
        where = region(kind, mirror)
        target = (xb, yb, partner, yb, xb, partner, partner, partner, partner)[kind]
        return pltpu.make_async_remote_copy(
            src_ref=metric if g == 0 and kind < 3 and not mirror else buf.at[where], dst_ref=buf.at[where],
            send_sem=m_send.at[g, kind], recv_sem=m_recv.at[g, kind],
            device_id=(a, target), device_id_type=MESH,
        )

    def got(g, kind):
        gather(g, kind, True).wait_recv()

    def gather_open(g):
        for kind in range(3):
            gather(g, kind).start()

    def gather_turn(g):
        got(g, 0)
        gather(g, 3).start()
        gather(g, 5).start()
        got(g, 1)
        gather(g, 4).start()
        gather(g, 6).start()

    def gather_close(g):
        got(g, 3)
        gather(g, 7).start()
        got(g, 4)
        gather(g, 8).start()
        for kind in (2, 5, 6, 7, 8):
            got(g, kind)
        for kind in range(9):
            gather(g, kind).wait_send()

    def regroup(owner, target, slot, where):
        return pltpu.make_async_remote_copy(
            src_ref=f_v.at[pl.ds(pl.multiple_of(target * rows, rows), rows), where()],
            dst_ref=g_hbm.at[:, where(owner * per)],
            send_sem=x_send.at[target, slot], recv_sem=x_recv.at[owner, slot],
            device_id=(a, target), device_id_type=MESH,
        )

    def keep(slot, where):
        return pltpu.make_async_copy(
            f_v.at[pl.ds(pl.multiple_of(b * rows, rows), rows), where()],
            g_hbm.at[:, where(b * per)], x_send.at[b, slot],
        )

    def regroup_all(slot, where):
        @pl.loop(1, n)
        def _(d):
            regroup(b, lax.rem(b + d, n), slot, where).start()

        keep(slot, where).start()

    def each_piece(act):
        @pl.loop(0, last)
        def _(c):
            act(c, functools.partial(cols, c))

        for k in (2 * last, 2 * last + 1):
            act(k - last, functools.partial(half, k))

    def fit(mat, dst, where):
        @pl.loop(0, tiles)
        def _(r):
            dst[row(r), where] = jnp.dot(
                mat[row(r), :], a_v[:, where], preferred_element_type=jnp.float32
            ).astype(dst.dtype)

    def product(left, j, r, span):
        return lax.dot_general(
            left[row(r), span], a_v[wide(j), span], (((1,), (1,)), ((), ())), preferred_element_type=jnp.float32
        )

    early, rest, whole = slice(0, ha * w), slice(ha * w, per), slice(0, per)

    def first(turn, j):
        return pltpu.make_async_remote_copy(
            src_ref=staged(j), dst_ref=one_v.at[turn, j // 2], send_sem=one_send.at[turn, j // 2],
            recv_sem=one_recv.at[turn, j // 2], device_id=(a, partner), device_id_type=MESH,
        )

    def direct(kind):
        target = (xb, yb, fb)[kind]
        return pltpu.make_async_remote_copy(
            src_ref=staged(target), dst_ref=two_v.at[kind], send_sem=r_send.at[kind],
            recv_sem=r_recv.at[kind], device_id=(a, target), device_id_type=MESH,
        )

    own_copies = [
        pltpu.make_async_copy(amp, a_v.at[pl.ds(pl.multiple_of(a * p, p), p), :], local_sem.at[0]),
        pltpu.make_async_copy(metric, m_v.at[:, wide(b)], local_sem.at[1]),
    ]

    gather_open(0)

    @pl.when(end)
    def _():
        lend().start()
        own(0, *range(2 * count))

    @pl.when(middle)
    def _():
        own(1, 2 * ha, 2 * ha + 1, 2 * ha + 2, 2 * ha + 3, 0, 1)
        own(0, *range(2 * ha, 2 * count))

    for copy in own_copies:
        copy.start()

    @pl.when(end)
    def _():
        gather_turn(0)
        gather_close(0)

    @pl.when(middle)
    def _():
        lend().wait_recv()
        gather_open(1)
        for k in range(2 * ha, 2 * ha + 4):
            relay(across, k, 0)
        relay(mate, 0, 1)
        relay(mate, 1, 1)
        own(1, 2, 3)
        gather_turn(1)
        relay(mate, 2, 1)
        relay(mate, 3, 1)
        own(1, 4, 5)
        gather_turn(0)
        relay(mate, 4, 1)
        relay(mate, 5, 1)
        own(1, 6)
        gather_close(1)

    for copy in own_copies:
        copy.wait()

    def first_share(low, high):
        @pl.loop(low, high)
        def _(h):
            j = 2 * h + 1 - parity

            @pl.loop(0, tiles)
            def _(r):
                o_m[row(r), wide(j)] = product(e_v, j, r, early).astype(o_m.dtype)

            first(0, j).start()

    def first_total(j, r):
        return product(e_v, j, r, early) + one_v[0, j // 2, row(r), :].astype(jnp.float32)

    def second_share(low, high):
        @pl.loop(low, high)
        def _(h):
            kind = lax.rem(h + 2, 3)
            j = jnp.where(h == 0, fb, jnp.where(h == 1, xb, yb))
            first(0, j).wait_recv()

            @pl.loop(0, tiles)
            def _(r):
                o_m[row(r), wide(j)] = first_total(j, r).astype(o_m.dtype)

            pltpu.make_async_remote_copy(
                src_ref=staged(j), dst_ref=two_v.at[kind], send_sem=r_send.at[kind],
                recv_sem=r_recv.at[kind], device_id=(a, j), device_id_type=MESH,
            ).start()

    def third_share():
        first(0, b).wait_recv()
        for kind in range(3):
            direct(kind).wait_recv()

        @pl.loop(0, tiles)
        def _(r):
            total = first_total(b, r)
            for kind in range(3):
                total += two_v[kind, row(r), :].astype(jnp.float32)
            o_m[row(r), wide(b)] = total.astype(o_m.dtype)

        for kind in range(3):
            direct(kind).wait_send()

    @pl.loop(0, ha - 1)
    def _(c):
        @pl.when(middle)
        def _():
            for k in (2 * c, 2 * c + 1):
                z(across, k, 0).wait_recv()
                z(beyond, k, 0).wait_recv()
            fit(o_m, e_v, cols(c))
            give(2 * c).start()
            give(2 * c + 1).start()
            relay(mate, 2 * c + 6, 1)

            @pl.when(c == 0)
            def _():
                own(1, 7)

            relay(mate, 2 * c + 7, 1)

            @pl.when(c == 2)
            def _():
                own(1, 12, 13)

            @pl.when(c == 0)
            def _():
                gather_close(0)

            fit(m_v, f_v, cols(c))

        @pl.when(end)
        def _():
            give(2 * c).wait_recv()
            give(2 * c + 1).wait_recv()

        regroup_all(c, functools.partial(cols, c))

    @pl.when(middle)
    def _():
        for k in (6, 7):
            z(across, k, 0).wait_recv()
            z(beyond, k, 0).wait_recv()
            fit(o_m, e_v, half(k))
            give(k).start()
            if k == 6:
                relay(mate, 12, 1)
                relay(mate, 13, 1)
                own(1, 14)
        relay(mate, 14, 1)
        own(1, 15)
        relay(mate, 15, 1)
        fit(m_v, f_v, cols(ha - 1))

    @pl.when(end)
    def _():
        give(6).wait_recv()
        give(7).wait_recv()

    regroup_all(ha - 1, functools.partial(cols, ha - 1))

    def all_in(k):
        for source in (mate, across, beyond):
            z(source, k, 0).wait_recv()

    @pl.loop(ha, last)
    def _(c):
        @pl.when(middle)
        def _():
            @pl.when(c == last - 1)
            def _():
                relay(across, 2 * c, 0)
                relay(across, 2 * c + 1, 0)

            relay(beyond, 2 * c, 0)

            @pl.when(c == ha)
            def _():
                first_share(0, 2)

            @pl.when(c == ha + 1)
            def _():
                second_share(0, 1)

            relay(beyond, 2 * c + 1, 0)

            @pl.when(c == ha)
            def _():
                first_share(2, n // 2)

            @pl.when(c == ha + 1)
            def _():
                second_share(1, 3)

        @pl.when(end)
        def _():
            all_in(2 * c)
            all_in(2 * c + 1)

        fit(m_v, f_v, cols(c))
        regroup_all(c, functools.partial(cols, c))

    for k in (2 * last, 2 * last + 1):
        @pl.when(middle)
        def _():
            relay(across, k, 0)
            relay(beyond, k, 0)

        @pl.when(end)
        def _():
            all_in(k)

        fit(m_v, f_v, half(k))
        regroup_all(k - last, functools.partial(half, k))

    def by_role(act):
        for role, span in ((middle, whole), (end, rest)):
            @pl.when(role)
            def _():
                @pl.loop(0, tiles)
                def _(r):
                    act(r, span)

    def for_partner(slot):
        j = 2 * slot + 1 - parity

        def act(r, span):
            o_m[row(r), wide(j)] = product(f_v, j, r, span).astype(o_m.dtype)

        by_role(act)
        first(1, j).start()

    @pl.when(middle)
    def _():
        @pl.loop(0, n // 2)
        def _(h):
            first(0, 2 * h + 1 - parity).wait_send()

    def piece(place_of, way, place, target):
        return pltpu.make_async_remote_copy(
            src_ref=s_v.at[place_of, part(way), :],
            dst_ref=two_v.at[3, part(way), :] if place == 0 else late_hbm.at[place - 1, part(way), :],
            send_sem=two_send.at[way, place], recv_sem=two_recv.at[way, place],
            device_id=(a, 2 * target + parity), device_id_type=MESH,
        )

    def turn(h):
        return jnp.where(h == 0, far, jnp.where(h == 1, near[0], jnp.where(h == 2, near[1], chip)))

    for_partner(far)

    @pl.loop(0, n // 2)
    def _(h):
        @pl.when(h < n // 2 - 1)
        def _():
            for_partner(turn(h + 1))

        slot = turn(h)
        j = 2 * slot + parity
        first(1, j).wait_recv()

        def act(r, span):
            total = product(f_v, j, r, span) + one_v[1, slot, row(r), :].astype(jnp.float32)
            s_v[h, row(r), :] = total.astype(s_v.dtype)
            t_v[h, row(r), :] = total

        by_role(act)

        @pl.when(h == 0)
        def _():
            for way in range(2):
                piece(0, way, 0, near[way]).start()

        for way in range(2):
            @pl.when(h == 1 + way)
            def _():
                piece(1 + way, way, 1, near[way]).start()

    @pl.when(middle)
    def _():
        third_share()
        finish().start()

    for way in range(2):
        at = 1 - way
        piece(0, way, 0, near[way]).wait_recv()
        s_v[1 + at, part(way), :] = (t_v[1 + at, part(way), :] + two_v[3, part(way), :].astype(jnp.float32)).astype(s_v.dtype)
        piece(1 + at, way, 2, near[at]).start()

    result = pltpu.make_async_copy(t_v.at[3], part_hbm, local_sem.at[1])
    result.start()

    coef = m_v.at[pl.ds(0, virt), pl.ds(0, ao)]
    load_coef = pltpu.make_async_copy(virt_coef, coef, local_sem.at[0])
    load_coef.start()

    def regrouped(slot, where):
        keep(slot, where).wait()

        @pl.loop(1, n)
        def _(d):
            regroup(lax.rem(b + n - d, n), b, slot, where).wait_recv()

    each_piece(regrouped)

    occ = n * per // virt

    def slot_rows(slot):
        return pl.ds(pl.multiple_of(slot * rows, rows), rows)

    def block_copy(i, slot):
        return pltpu.make_async_copy(
            g_hbm.at[:, pl.ds(pl.multiple_of(i * virt, virt), virt)],
            m_v.at[slot_rows(slot), pl.ds(ao, virt)], g_sem.at[slot],
        )

    def out_copy(i, slot):
        return pltpu.make_async_copy(
            m_v.at[slot_rows(slot), pl.ds(ao + virt, ao)],
            fitted_ao.at[:, pl.ds(pl.multiple_of(i * ao, ao), ao)], o_sem.at[slot],
        )

    block_copy(0, 0).start()
    load_coef.wait()

    @pl.loop(0, occ)
    def _(i):
        slot = lax.rem(i, 2)

        @pl.when(i + 1 < occ)
        def _():
            block_copy(i + 1, 1 - slot).start()

        @pl.when(i >= 2)
        def _():
            out_copy(i - 2, slot).wait()

        block_copy(i, slot).wait()
        m_v[slot_rows(slot), pl.ds(ao + virt, ao)] = jnp.dot(
            m_v[slot_rows(slot), pl.ds(ao, virt)], m_v[pl.ds(0, virt), pl.ds(0, ao)],
            preferred_element_type=jnp.float32,
        ).astype(m_v.dtype)
        out_copy(i, slot).start()

    for i in range(max(occ - 2, 0), occ):
        out_copy(i, i % 2).wait()

    for way in range(2):
        piece(1, way, 1, near[way]).wait_recv()
        piece(1, way, 2, near[1 - way]).wait_recv()

    @pl.when(end)
    def _():
        finish().wait_recv()

    @pl.loop(0, n // 2)
    def _(h):
        first(1, 2 * h + 1 - parity).wait_send()

    for way in range(2):
        piece(0, way, 0, near[way]).wait_send()
        piece(1, way, 1, near[way]).wait_send()
        piece(1, way, 2, near[1 - way]).wait_send()

    def regroup_sent(slot, where):
        @pl.loop(1, n)
        def _(d):
            regroup(b, lax.rem(b + d, n), slot, where).wait_send()

    each_piece(regroup_sent)

    @pl.when(end)
    def _():
        lend().wait_send()

        @pl.loop(0, 2 * count)
        def _(k):
            z(a, k, 0).wait_send()

    @pl.when(middle)
    def _():
        finish().wait_send()

        @pl.loop(0, 2 * ha)
        def _(k):
            give(k).wait_send()

        @pl.loop(0, 2 * count)
        def _(k):
            z(a, k, 1).wait_send()
            z(mate, k, 1).wait_send()

        @pl.loop(2 * ha, 2 * count)
        def _(k):
            z(a, k, 0).wait_send()
            z(across, k, 0).wait_send()
            z(beyond, k, 0).wait_send()

    result.wait()


def close_kernel(na, part, late, ao_in, density, ao_out, p_v, l_v, w_v, copy_sem, in_sem, out_sem):
    a = lax.axis_index("aux")
    cuts = copy_sem.shape[1]
    span = ao_in.shape[1] // cuts
    steps = out_sem.shape[0]
    size = part.shape[0] // steps
    held = [slice(k * span, (k + 1) * span) for k in range(cuts)]
    fetches = [pltpu.make_async_copy(ao_in.at[:, held[k]], w_v.at[:, held[k]], copy_sem.at[0, k]) for k in range(cuts)]
    writes = [pltpu.make_async_copy(w_v.at[:, held[k]], ao_out.at[:, held[k]], copy_sem.at[1, k]) for k in range(cuts)]
    where = [pl.ds(k * size, size) for k in range(steps)]
    loads = [
        (
            pltpu.make_async_copy(part.at[where[k], :], p_v.at[where[k], :], in_sem.at[0, k]),
            pltpu.make_async_copy(late.at[:, where[k], :], l_v.at[:, where[k], :], in_sem.at[1, k]),
        )
        for k in range(steps)
    ]
    stores = [pltpu.make_async_copy(p_v.at[where[k], :], density.at[where[k], :], out_sem.at[k]) for k in range(steps)]
    at_end = jnp.logical_or(a == 0, a == na - 1)
    for copy in fetches:
        copy.start()
    for pair in loads:
        for copy in pair:
            copy.start()
    for k in range(cuts):
        fetches[k].wait()
        writes[k].start()
    for k in range(steps):
        for copy in loads[k]:
            copy.wait()
        total = p_v[where[k], :] + l_v[0, where[k], :].astype(jnp.float32) + l_v[1, where[k], :].astype(jnp.float32)
        third = jnp.where(at_end, l_v[2, where[k], :].astype(jnp.float32), 0.0)
        p_v[where[k], :] = total + third
        stores[k].start()
    for copy in stores + writes:
        copy.wait()


def cube_shards(na, n, count, metric, amplitudes, virt_coef):
    p, q = metric.shape
    per = amplitudes.shape[1]
    virt, ao = virt_coef.shape
    ha = count // 2
    rows = p // n
    bf16 = jnp.bfloat16
    dma = pltpu.SemaphoreType.DMA
    part, late, blocks, _ = pl.pallas_call(
        functools.partial(cube_kernel, na, n, count, ha),
        out_shape=(
            jax.ShapeDtypeStruct((p, q), jnp.float32),
            jax.ShapeDtypeStruct((3, p, q), bf16),
            jax.ShapeDtypeStruct((rows, n * per // virt * ao), bf16),
            jax.ShapeDtypeStruct((rows, n * per), bf16),
        ),
        in_specs=[pl.BlockSpec(memory_space=pl.ANY)] * 3,
        out_specs=(pl.BlockSpec(memory_space=pl.ANY),) * 4,
        scratch_shapes=[
            pltpu.VMEM((p, n * q), bf16),
            pltpu.VMEM((p, n * q), bf16),
            pltpu.VMEM((na * p, per), bf16),
            pltpu.VMEM((4, p, q), jnp.float32),
            pltpu.VMEM((4, p, q), bf16),
            pltpu.VMEM((p, per), bf16),
            pltpu.VMEM((p, per * ha // count), bf16),
            pltpu.VMEM((2, n // 2, p, q), bf16),
            pltpu.VMEM((4, p, q), bf16),
            dma((2, 9)), dma((2, 9)),
            dma((2, na, 2 * count)), dma((na, 2 * count)),
            dma((2 * ha,)), dma((2 * ha,)),
            dma((n, count + 1)), dma((n, count + 1)),
            dma((2, n // 2)), dma((2, n // 2)),
            dma((2, 3)), dma((2, 3)),
            dma((3,)), dma((3,)),
            dma((2,)), dma((2,)), dma((2,)), dma((2,)), dma((2,)),
        ],
        compiler_params=pltpu.CompilerParams(
            collective_id=0, has_side_effects=True, vmem_limit_bytes=67043328
        ),
    )(metric, amplitudes, virt_coef)
    return pl.pallas_call(
        functools.partial(close_kernel, na),
        out_shape=(jax.ShapeDtypeStruct(part.shape, part.dtype), jax.ShapeDtypeStruct(blocks.shape, blocks.dtype)),
        in_specs=[pl.BlockSpec(memory_space=pl.ANY)] * 3,
        out_specs=(pl.BlockSpec(memory_space=pl.ANY),) * 2,
        scratch_shapes=[
            pltpu.VMEM((p, q), jnp.float32), pltpu.VMEM((3, p, q), bf16), pltpu.VMEM(blocks.shape, bf16),
            dma((2, 8)), dma((2, 4)), dma((4,)),
        ],
        compiler_params=pltpu.CompilerParams(vmem_limit_bytes=67043328),
    )(part, late, blocks)


def fits_cube(na, n, metric, amplitudes, virt_coef):
    p, per, (virt, ao) = metric.shape[0], amplitudes.shape[1], virt_coef.shape
    return (
        na == 4 and n == 8 and per % 2048 == 0 and p % 256 == 0
        and metric.shape[1] * n == na * p and virt <= p and virt + 2 * ao <= na * p
        and virt % 128 == 0 and ao % 128 == 0 and n * per % virt == 0
    )


def any_shards(na, n, metric, amplitudes, virt_coef):
    if fits_cube(na, n, metric, amplitudes, virt_coef):
        return cube_shards(na, n, 8, metric, amplitudes, virt_coef)
    return shards(na, n, metric, amplitudes, virt_coef)


def solution(mesh):
    in_specs = (P("aux", "pair"), P("aux", "pair"), P())
    out_specs = (P("aux", "pair"), P(("aux", "pair"), None))
    body = functools.partial(any_shards, mesh.shape["aux"], mesh.shape["pair"])
    return jax.shard_map(body, mesh=mesh, in_specs=in_specs, out_specs=out_specs, check_vma=False)
```

```python
import functools

import jax
import jax.numpy as jnp
from jax import lax
from jax.experimental import pallas as pl
from jax.experimental.pallas import tpu as pltpu
from jax.sharding import PartitionSpec as P

MESH = pl.DeviceIdType.MESH


def kernel(
    na, n, count, metric, amp, virt_coef, density, fitted_ao,
    m_v, a_v, d_v, f_v, g_v, c_v, one_v, two_v, o_v,
    m_send, m_recv, z_send, z_recv, x_send, x_recv, one_send, one_recv, two_send, two_recv, o_sem, local_sem,
):
    a, b = lax.axis_index("aux"), lax.axis_index("pair")
    p, q = metric.shape
    per = amp.shape[1]
    w = per // count
    rows = p // n
    virt, ao = virt_coef.shape
    half = n // 2
    parity, chip = lax.rem(b, 2), b // 2
    partner = b + 1 - 2 * parity
    tile = min(256, p)
    tiles = p // tile

    barrier = pltpu.get_barrier_semaphore()
    for d in range(1, n):
        pl.semaphore_signal(barrier, inc=1, device_id=(a, lax.rem(b + d, n)), device_id_type=MESH)

    @pl.when(a > 0)
    def _():
        pl.semaphore_signal(barrier, inc=1, device_id=(a - 1, b), device_id_type=MESH)

    @pl.when(a < na - 1)
    def _():
        pl.semaphore_signal(barrier, inc=1, device_id=(a + 1, b), device_id_type=MESH)

    pl.semaphore_wait(barrier, n - 1 + jnp.where(a > 0, 1, 0) + jnp.where(a < na - 1, 1, 0))

    def block_of(s, c):
        return a_v.at[c, pl.ds(pl.multiple_of(s * p, p), p), :]

    def hop(src, s, c, way, target):
        return pltpu.make_async_remote_copy(
            src_ref=src, dst_ref=block_of(s, c), send_sem=z_send.at[way, s, c],
            recv_sem=z_recv.at[s, c], device_id=(target, b), device_id_type=MESH,
        )

    def metric_copy(owner, target):
        return pltpu.make_async_remote_copy(
            src_ref=metric, dst_ref=m_v.at[:, pl.ds(pl.multiple_of(owner * q, q), q)],
            send_sem=m_send.at[target], recv_sem=m_recv.at[owner],
            device_id=(a, target), device_id_type=MESH,
        )

    def regroup(owner, target, c):
        return pltpu.make_async_remote_copy(
            src_ref=f_v.at[c, pl.ds(pl.multiple_of(target * rows, rows), rows), :],
            dst_ref=g_v.at[:, pl.ds(pl.multiple_of(owner * per + c * w, w), w)],
            send_sem=x_send.at[target, c], recv_sem=x_recv.at[owner, c],
            device_id=(a, target), device_id_type=MESH,
        )

    def staged(j):
        return m_v.at[:, pl.ds(pl.multiple_of(j * q, q), q)]

    def first(j):
        return pltpu.make_async_remote_copy(
            src_ref=staged(j), dst_ref=one_v.at[j // 2], send_sem=one_send.at[j // 2],
            recv_sem=one_recv.at[j // 2], device_id=(a, partner), device_id_type=MESH,
        )

    def second(source, j):
        return pltpu.make_async_remote_copy(
            src_ref=staged(j), dst_ref=two_v.at[source], send_sem=two_send.at[0, j // 2],
            recv_sem=two_recv.at[0, source], device_id=(a, j), device_id_type=MESH,
        )

    def mine(c):
        return amp.at[:, c * w : (c + 1) * w]

    for c in range(count):
        @pl.when(a > 0)
        def _():
            hop(mine(c), a, c, 0, jnp.maximum(a - 1, 0)).start()

        @pl.when(a < na - 1)
        def _():
            hop(mine(c), a, c, 1, jnp.minimum(a + 1, na - 1)).start()

    @pl.loop(1, n)
    def _(d):
        metric_copy(b, lax.rem(b + d, n)).start()

    own_copies = [pltpu.make_async_copy(mine(c), block_of(a, c), local_sem.at[c]) for c in range(count)]
    own_copies.append(pltpu.make_async_copy(metric, staged(b), local_sem.at[count]))
    own_copies.append(pltpu.make_async_copy(virt_coef, c_v, local_sem.at[count + 1]))
    for copy in own_copies:
        copy.start()

    def arrive(t, c):
        @pl.when(a - t >= 0)
        def _():
            s = jnp.maximum(a - t, 0)
            hop(block_of(s, c), s, c, 1, a).wait_recv()

            @pl.when(a < na - 1)
            def _():
                hop(block_of(s, c), s, c, 1, jnp.minimum(a + 1, na - 1)).start()

        @pl.when(a + t < na)
        def _():
            s = jnp.minimum(a + t, na - 1)
            hop(block_of(s, c), s, c, 0, a).wait_recv()

            @pl.when(a > 0)
            def _():
                hop(block_of(s, c), s, c, 0, jnp.maximum(a - 1, 0)).start()

    @pl.loop(1, na - 1)
    def _(t):
        @pl.loop(0, count)
        def _(c):
            arrive(t, c)

    for copy in own_copies:
        copy.wait()

    @pl.loop(1, n)
    def _(d):
        metric_copy(lax.rem(b + n - d, n), b).wait_recv()

    @pl.loop(1, n)
    def _(d):
        metric_copy(b, lax.rem(b + d, n)).wait_send()

    def row(r):
        return pl.ds(pl.multiple_of(r * tile, tile), tile)

    def product(j, r, c):
        right = a_v[c, pl.ds(pl.multiple_of(j * q, q), q), :]
        return lax.dot_general(
            f_v[c, row(r), :], right, (((1,), (1,)), ((), ())), preferred_element_type=jnp.float32
        )

    def fit(c):
        @pl.loop(0, tiles)
        def _(r):
            f_v[c, row(r), :] = jnp.dot(
                m_v[row(r), :], a_v[c], preferred_element_type=jnp.float32
            ).astype(f_v.dtype)

        @pl.loop(1, n)
        def _(d):
            regroup(b, lax.rem(b + d, n), c).start()

        pltpu.make_async_copy(
            f_v.at[c, pl.ds(pl.multiple_of(b * rows, rows), rows), :],
            g_v.at[:, pl.ds(pl.multiple_of(b * per + c * w, w), w)], x_send.at[b, c],
        ).start()

    @pl.loop(0, n * tiles)
    def _(i):
        d_v[i // tiles, row(lax.rem(i, tiles)), :] = jnp.zeros((tile, q), jnp.float32)

    @pl.loop(0, count - 1)
    def _(c):
        arrive(na - 1, c)
        fit(c)

        @pl.loop(0, n * tiles)
        def _(i):
            j, r = i // tiles, lax.rem(i, tiles)
            d_v[j, row(r), :] += product(j, r, c)

    last = count - 1
    arrive(na - 1, last)
    fit(last)

    quad = half == 4
    mid = p // 2
    near = (chip + 1 - 2 * lax.rem(chip, 2), lax.rem(chip + 2, 4))
    far = 3 - chip

    def turn(h):
        if not quad:
            return lax.rem(chip + h, half)
        return jnp.where(h == 0, far, jnp.where(h == 1, near[0], jnp.where(h == 2, near[1], chip)))

    @pl.loop(0, half)
    def _(h):
        j = 2 * turn(h) + 1 - parity

        @pl.loop(0, tiles)
        def _(r):
            m_v[row(r), pl.ds(pl.multiple_of(j * q, q), q)] = (
                d_v[j, row(r), :] + product(j, r, last)
            ).astype(m_v.dtype)

        first(j).start()

    @pl.loop(0, 0 if quad else half)
    def _(h):
        j = 2 * lax.rem(chip + h, half) + parity

        @pl.loop(0, tiles)
        def _(r):
            d_v[j, row(r), :] += product(j, r, last)

    def part(way):
        return pl.ds(way * mid, mid)

    def cast(slot, way):
        j = 2 * slot + parity
        m_v[part(way), pl.ds(pl.multiple_of(j * q, q), q)] = d_v[j, part(way), :].astype(m_v.dtype)

    def piece(slot, way, place, target):
        j = 2 * slot + parity
        return pltpu.make_async_remote_copy(
            src_ref=m_v.at[part(way), pl.ds(pl.multiple_of(j * q, q), q)],
            dst_ref=two_v.at[place, part(way), :], send_sem=two_send.at[way, place],
            recv_sem=two_recv.at[way, place], device_id=(a, 2 * target + parity), device_id_type=MESH,
        )

    def add_in(slot, place, way):
        j = 2 * slot + parity
        d_v[j, part(way), :] += two_v[place, part(way), :].astype(jnp.float32)

    if quad:
        for h in range(4):
            slot = (far, near[0], near[1], chip)[h]

            @pl.loop(0, tiles)
            def _(r, slot=slot):
                d_v[2 * slot + parity, row(r), :] += product(2 * slot + parity, r, last)

            first(2 * slot + parity).wait_recv()

            @pl.loop(0, tiles)
            def _(r, slot=slot):
                j = 2 * slot + parity
                d_v[j, row(r), :] += one_v[slot, row(r), :].astype(jnp.float32)

            if h == 0:
                for way in range(2):
                    cast(far, way)
                    piece(far, way, 0, near[way]).start()
            elif h < 3:
                cast(near[h - 1], h - 1)
                piece(near[h - 1], h - 1, 1, near[h - 1]).start()
    else:
        @pl.loop(1, half)
        def _(h):
            slot = lax.rem(chip + h, half)
            j = 2 * slot + parity
            first(j).wait_recv()

            @pl.loop(0, tiles)
            def _(r):
                m_v[row(r), pl.ds(pl.multiple_of(j * q, q), q)] = (
                    d_v[j, row(r), :] + one_v[slot, row(r), :].astype(jnp.float32)
                ).astype(m_v.dtype)

            second(chip, j).start()

        first(b).wait_recv()

        @pl.loop(0, tiles)
        def _(r):
            d_v[b, row(r), :] += one_v[chip, row(r), :].astype(jnp.float32)

    if quad:
        for way in range(2):
            other = near[1 - way]
            piece(other, way, 0, near[way]).wait_recv()
            add_in(other, 0, way)
            cast(other, way)
            piece(other, way, 2, other).start()

    @pl.loop(0, count)
    def _(c):
        pltpu.make_async_copy(
            f_v.at[c, pl.ds(pl.multiple_of(b * rows, rows), rows), :],
            g_v.at[:, pl.ds(pl.multiple_of(b * per + c * w, w), w)], x_send.at[b, c],
        ).wait()

        @pl.loop(1, n)
        def _(d):
            regroup(lax.rem(b + n - d, n), b, c).wait_recv()

    occ = n * per // virt

    def out_copy(i, slot):
        return pltpu.make_async_copy(
            o_v.at[slot], fitted_ao.at[:, pl.ds(pl.multiple_of(i * ao, ao), ao)], o_sem.at[slot]
        )

    @pl.loop(0, occ)
    def _(i):
        slot = lax.rem(i, 2)

        @pl.when(i >= 2)
        def _():
            out_copy(i - 2, slot).wait()

        o_v[slot] = jnp.dot(
            g_v[:, pl.ds(pl.multiple_of(i * virt, virt), virt)], c_v[...], preferred_element_type=jnp.float32
        ).astype(o_v.dtype)
        out_copy(i, slot).start()

    for i in range(max(occ - 2, 0), occ):
        out_copy(i, i % 2).wait()

    if quad:
        for way in range(2):
            piece(chip, way, 1, near[way]).wait_recv()
            add_in(chip, 1, way)
        for way in range(2):
            piece(chip, way, 2, near[1 - way]).wait_recv()
            add_in(chip, 2, way)
    else:
        @pl.loop(1, half)
        def _(h):
            source = lax.rem(chip + half - h, half)
            second(source, b).wait_recv()

            @pl.loop(0, tiles)
            def _(r):
                d_v[b, row(r), :] += two_v[source, row(r), :].astype(jnp.float32)

    result = pltpu.make_async_copy(d_v.at[b], density, local_sem.at[0])
    result.start()

    @pl.loop(0, half)
    def _(h):
        first(2 * h + 1 - parity).wait_send()

    if quad:
        for way in range(2):
            piece(far, way, 0, near[way]).wait_send()
            piece(near[way], way, 1, near[way]).wait_send()
            piece(near[1 - way], way, 2, near[1 - way]).wait_send()
    else:
        @pl.loop(1, half)
        def _(h):
            second(chip, 2 * lax.rem(chip + h, half) + parity).wait_send()

    @pl.loop(0, count)
    def _(c):
        @pl.loop(1, n)
        def _(d):
            regroup(b, lax.rem(b + d, n), c).wait_send()

        @pl.loop(0, na)
        def _(s):
            @pl.when(jnp.logical_and(s >= a, a > 0))
            def _():
                hop(block_of(s, c), s, c, 0, jnp.maximum(a - 1, 0)).wait_send()

            @pl.when(jnp.logical_and(s <= a, a < na - 1))
            def _():
                hop(block_of(s, c), s, c, 1, jnp.minimum(a + 1, na - 1)).wait_send()

    result.wait()


def shards(na, n, metric, amplitudes, virt_coef):
    p, q = metric.shape
    per = amplitudes.shape[1]
    virt, ao = virt_coef.shape
    count = next(c for c in (8, 4, 2, 1) if per % (128 * c) == 0)
    w = per // count
    rows = p // n
    bf16 = jnp.bfloat16
    dma = pltpu.SemaphoreType.DMA
    return pl.pallas_call(
        functools.partial(kernel, na, n, count),
        out_shape=(
            jax.ShapeDtypeStruct((p, q), jnp.float32),
            jax.ShapeDtypeStruct((rows, n * per // virt * ao), bf16),
        ),
        in_specs=[pl.BlockSpec(memory_space=pl.ANY)] * 3,
        out_specs=(pl.BlockSpec(memory_space=pl.ANY), pl.BlockSpec(memory_space=pl.ANY)),
        scratch_shapes=[
            pltpu.VMEM((p, n * q), bf16),
            pltpu.VMEM((count, na * p, w), bf16),
            pltpu.VMEM((n, p, q), jnp.float32),
            pltpu.VMEM((count, p, w), bf16),
            pltpu.VMEM((rows, n * per), bf16),
            pltpu.VMEM((virt, ao), bf16),
            pltpu.VMEM((n // 2, p, q), bf16),
            pltpu.VMEM((n // 2, p, q), bf16),
            pltpu.VMEM((2, rows, ao), bf16),
            dma((n,)), dma((n,)),
            dma((2, na, count)), dma((na, count)),
            dma((n, count)), dma((n, count)),
            dma((n // 2,)), dma((n // 2,)),
            dma((2, n // 2)), dma((2, n // 2)),
            dma((2,)), dma((count + 2,)),
        ],
        compiler_params=pltpu.CompilerParams(
            collective_id=0, has_side_effects=True, vmem_limit_bytes=67043328
        ),
    )(metric, amplitudes, virt_coef)

def cube_kernel(
    na, n, count, ha, metric, amp, virt_coef, part_hbm, late_hbm, fitted_ao, g_hbm,
    m_v, o_m, a_v, t_v, s_v, f_v, e_v, one_v, two_v,
    m_send, m_recv, z_send, z_recv, e_send, e_recv, x_send, x_recv,
    one_send, one_recv, two_send, two_recv, r_send, r_recv,
    mm_sem, fin_sem, far_sem, g_sem, o_sem, local_sem,
):
    a, b = lax.axis_index("aux"), lax.axis_index("pair")
    p, q = metric.shape
    per = amp.shape[1]
    w = per // count
    rows = p // n
    virt, ao = virt_coef.shape
    parity, chip = lax.rem(b, 2), b // 2
    flip = 1 - 2 * parity
    partner = b + flip
    near = (chip + 1 - 2 * lax.rem(chip, 2), lax.rem(chip + 2, 4))
    far = 3 - chip
    xb, yb, fb = 2 * near[0] + parity, 2 * near[1] + parity, 2 * far + parity
    tile = 256 if p % 512 == 0 else 128
    tiles = p // tile
    mid = p // 2
    last = count - 1

    middle = jnp.logical_and(a > 0, a < na - 1)
    end = jnp.logical_not(middle)
    mate = a + 1 - 2 * lax.rem(a, 2)
    across = na - 1 - a
    beyond = na - 1 - mate

    barrier = pltpu.get_barrier_semaphore()
    for d in range(1, n):
        pl.semaphore_signal(barrier, inc=1, device_id=(a, lax.rem(b + d, n)), device_id_type=MESH)
    pl.semaphore_signal(barrier, inc=1, device_id=(mate, b), device_id_type=MESH)

    @pl.when(middle)
    def _():
        pl.semaphore_signal(barrier, inc=1, device_id=(across, b), device_id_type=MESH)

    pl.semaphore_wait(barrier, n + jnp.where(middle, 1, 0))

    v = w // 2

    def cols(c, base=0):
        return pl.ds(pl.multiple_of(base + c * w, w), w)

    def half(k, base=0):
        return pl.ds(pl.multiple_of(base + k * v, v), v)

    def row(r):
        return pl.ds(pl.multiple_of(r * tile, tile), tile)

    def part(way):
        return pl.ds(way * mid, mid)

    def wide(j):
        return pl.ds(pl.multiple_of(j * q, q), q)

    def block_of(s, k):
        return a_v.at[pl.ds(pl.multiple_of(s * p, p), p), half(k)]

    def z(s, k, way, own=False):
        return pltpu.make_async_remote_copy(
            src_ref=amp.at[:, half(k)] if own else block_of(s, k), dst_ref=block_of(s, k),
            send_sem=z_send.at[way, s, k], recv_sem=z_recv.at[s, k],
            device_id=(mate if way == 0 else across, b), device_id_type=MESH,
        )

    def own(way, *halves):
        for k in halves:
            z(a, k, way, True).start()

    def relay(s, k, way):
        z(s, k, way).wait_recv()
        z(s, k, way).start()

    def lend():
        return pltpu.make_async_remote_copy(
            src_ref=metric, dst_ref=o_m.at[:, wide(b)], send_sem=mm_sem.at[0], recv_sem=mm_sem.at[1],
            device_id=(mate, b), device_id_type=MESH,
        )

    def give(k):
        return pltpu.make_async_remote_copy(
            src_ref=e_v.at[:, half(k)], dst_ref=f_v.at[:, half(k)], send_sem=e_send.at[k], recv_sem=e_recv.at[k],
            device_id=(mate, b), device_id_type=MESH,
        )

    def staged(j):
        return o_m.at[:, wide(j)]

    def finish():
        return pltpu.make_async_remote_copy(
            src_ref=staged(b), dst_ref=late_hbm.at[2], send_sem=fin_sem.at[0], recv_sem=fin_sem.at[1],
            device_id=(mate, b), device_id_type=MESH,
        )

    def region(kind, mirror):
        mine = (b, b, b, xb, yb, xb, yb, fb, fb)
        theirs = (xb, yb, partner, fb, fb, xb + flip, yb + flip, fb + flip, fb + flip)
        side = (None, None, None, 0, 1, None, None, 0, 1)[kind]
        j = (theirs if mirror else mine)[kind]
        return (slice(None) if side is None else part(side), wide(j))

    def gather(g, kind, mirror=False):
        buf = (m_v, o_m)[g]
        where = region(kind, mirror)
        target = (xb, yb, partner, yb, xb, partner, partner, partner, partner)[kind]
        return pltpu.make_async_remote_copy(
            src_ref=metric if g == 0 and kind < 3 and not mirror else buf.at[where], dst_ref=buf.at[where],
            send_sem=m_send.at[g, kind], recv_sem=m_recv.at[g, kind],
            device_id=(a, target), device_id_type=MESH,
        )

    def got(g, kind):
        gather(g, kind, True).wait_recv()

    def gather_open(g):
        for kind in range(3):
            gather(g, kind).start()

    def gather_turn(g):
        got(g, 0)
        gather(g, 3).start()
        gather(g, 5).start()
        got(g, 1)
        gather(g, 4).start()
        gather(g, 6).start()

    def gather_close(g):
        got(g, 3)
        gather(g, 7).start()
        got(g, 4)
        gather(g, 8).start()
        for kind in (2, 5, 6, 7, 8):
            got(g, kind)
        for kind in range(9):
            gather(g, kind).wait_send()

    def regroup(owner, target, slot, where):
        return pltpu.make_async_remote_copy(
            src_ref=f_v.at[pl.ds(pl.multiple_of(target * rows, rows), rows), where()],
            dst_ref=g_hbm.at[:, where(owner * per)],
            send_sem=x_send.at[target, slot], recv_sem=x_recv.at[owner, slot],
            device_id=(a, target), device_id_type=MESH,
        )

    def keep(slot, where):
        return pltpu.make_async_copy(
            f_v.at[pl.ds(pl.multiple_of(b * rows, rows), rows), where()],
            g_hbm.at[:, where(b * per)], x_send.at[b, slot],
        )

    def regroup_all(slot, where):
        @pl.loop(1, n)
        def _(d):
            regroup(b, lax.rem(b + d, n), slot, where).start()

        keep(slot, where).start()

    def each_piece(act):
        @pl.loop(0, last)
        def _(c):
            act(c, functools.partial(cols, c))

        for k in (2 * last, 2 * last + 1):
            act(k - last, functools.partial(half, k))

    def fit(mat, dst, where):
        @pl.loop(0, tiles)
        def _(r):
            dst[row(r), where] = jnp.dot(
                mat[row(r), :], a_v[:, where], preferred_element_type=jnp.float32
            ).astype(dst.dtype)

    def product(left, j, r, span):
        return lax.dot_general(
            left[row(r), span], a_v[wide(j), span], (((1,), (1,)), ((), ())), preferred_element_type=jnp.float32
        )

    early, rest, whole = slice(0, ha * w), slice(ha * w, per), slice(0, per)

    def first(turn, j):
        return pltpu.make_async_remote_copy(
            src_ref=staged(j), dst_ref=one_v.at[turn, j // 2], send_sem=one_send.at[turn, j // 2],
            recv_sem=one_recv.at[turn, j // 2], device_id=(a, partner), device_id_type=MESH,
        )

    def early_piece(target, way, place):
        return pltpu.make_async_remote_copy(
            src_ref=o_m.at[part(way), wide((xb, yb, fb)[target])], dst_ref=two_v.at[place, part(way), :],
            send_sem=r_send.at[way, place], recv_sem=r_recv.at[way, place],
            device_id=(a, (xb, yb)[target if place else way]), device_id_type=MESH,
        )

    own_copies = [
        pltpu.make_async_copy(amp, a_v.at[pl.ds(pl.multiple_of(a * p, p), p), :], local_sem.at[0]),
        pltpu.make_async_copy(metric, m_v.at[:, wide(b)], local_sem.at[1]),
    ]

    gather_open(0)

    @pl.when(end)
    def _():
        lend().start()
        own(0, *range(2 * count))

    @pl.when(middle)
    def _():
        own(1, 2 * ha, 2 * ha + 1, 2 * ha + 2, 2 * ha + 3, 0, 1)
        own(0, *range(2 * ha, 2 * count))

    for copy in own_copies:
        copy.start()

    @pl.when(end)
    def _():
        gather_turn(0)
        gather_close(0)

    @pl.when(middle)
    def _():
        lend().wait_recv()
        gather_open(1)
        for k in range(2 * ha, 2 * ha + 4):
            relay(across, k, 0)
        relay(mate, 0, 1)
        relay(mate, 1, 1)
        own(1, 2, 3)
        gather_turn(1)
        relay(mate, 2, 1)
        relay(mate, 3, 1)
        own(1, 4, 5)
        gather_turn(0)
        relay(mate, 4, 1)
        relay(mate, 5, 1)
        own(1, 6)
        gather_close(1)

    for copy in own_copies:
        copy.wait()

    def first_share(low, high):
        @pl.loop(low, high)
        def _(h):
            j = 2 * h + 1 - parity

            @pl.loop(0, tiles)
            def _(r):
                o_m[row(r), wide(j)] = product(e_v, j, r, early).astype(o_m.dtype)

            first(0, j).start()

    def first_total(j, r):
        return product(e_v, j, r, early) + one_v[0, j // 2, row(r), :].astype(jnp.float32)

    def second_share(target):
        j = (xb, yb, fb)[target]
        first(0, j).wait_recv()

        @pl.loop(0, tiles)
        def _(r):
            o_m[row(r), wide(j)] = first_total(j, r).astype(o_m.dtype)

        if target == 2:
            early_piece(2, 0, 0).start()
            early_piece(2, 1, 0).start()
        else:
            early_piece(target, target, 1).start()

    def third_share():
        for way in range(2):
            other = 1 - way
            early_piece(2, way, 0).wait_recv()

            @pl.loop(way * tiles // 2, (way + 1) * tiles // 2)
            def _(r, j=(xb, yb)[other]):
                total = first_total(j, r) + two_v[0, row(r), :].astype(jnp.float32)
                o_m[row(r), wide(j)] = total.astype(o_m.dtype)

            early_piece(other, way, 2).start()

    def fourth_share():
        first(0, b).wait_recv()
        for way in range(2):
            early_piece(way, way, 1).wait_recv()
            early_piece(1 - way, way, 2).wait_recv()

        @pl.loop(0, tiles)
        def _(r):
            total = first_total(b, r)
            for place in (1, 2):
                total += two_v[place, row(r), :].astype(jnp.float32)
            o_m[row(r), wide(b)] = total.astype(o_m.dtype)

        for way in range(2):
            early_piece(2, way, 0).wait_send()
            early_piece(way, way, 1).wait_send()
            early_piece(1 - way, way, 2).wait_send()

    @pl.loop(0, ha - 1)
    def _(c):
        @pl.when(middle)
        def _():
            for k in (2 * c, 2 * c + 1):
                z(across, k, 0).wait_recv()
                z(beyond, k, 0).wait_recv()
            fit(o_m, e_v, cols(c))
            give(2 * c).start()
            give(2 * c + 1).start()
            relay(mate, 2 * c + 6, 1)

            @pl.when(c == 0)
            def _():
                own(1, 7)

            relay(mate, 2 * c + 7, 1)

            @pl.when(c == 2)
            def _():
                own(1, 12, 13)

            @pl.when(c == 0)
            def _():
                gather_close(0)

            fit(m_v, f_v, cols(c))

        @pl.when(end)
        def _():
            give(2 * c).wait_recv()
            give(2 * c + 1).wait_recv()

        regroup_all(c, functools.partial(cols, c))

    @pl.when(middle)
    def _():
        for k in (6, 7):
            z(across, k, 0).wait_recv()
            z(beyond, k, 0).wait_recv()
            fit(o_m, e_v, half(k))
            give(k).start()
            if k == 6:
                relay(mate, 12, 1)
                relay(mate, 13, 1)
                own(1, 14)
        relay(mate, 14, 1)
        own(1, 15)
        relay(mate, 15, 1)
        fit(m_v, f_v, cols(ha - 1))

    @pl.when(end)
    def _():
        give(6).wait_recv()
        give(7).wait_recv()

    regroup_all(ha - 1, functools.partial(cols, ha - 1))

    def all_in(k):
        for source in (mate, across, beyond):
            z(source, k, 0).wait_recv()

    @pl.loop(ha, last)
    def _(c):
        @pl.when(middle)
        def _():
            @pl.when(c == last - 1)
            def _():
                relay(across, 2 * c, 0)
                relay(across, 2 * c + 1, 0)

            relay(beyond, 2 * c, 0)

            @pl.when(c == ha)
            def _():
                first_share(0, 2)

            @pl.when(c == ha + 1)
            def _():
                second_share(2)

            relay(beyond, 2 * c + 1, 0)

            @pl.when(c == ha)
            def _():
                first_share(2, n // 2)

            @pl.when(c == ha + 1)
            def _():
                second_share(0)
                second_share(1)

            @pl.when(c == last - 1)
            def _():
                third_share()

        @pl.when(end)
        def _():
            all_in(2 * c)
            all_in(2 * c + 1)

        fit(m_v, f_v, cols(c))
        regroup_all(c, functools.partial(cols, c))

    for k in (2 * last, 2 * last + 1):
        @pl.when(middle)
        def _():
            relay(across, k, 0)
            relay(beyond, k, 0)

        @pl.when(end)
        def _():
            all_in(k)

        if k == 2 * last:
            fit(m_v, f_v, half(k))
            regroup_all(k - last, functools.partial(half, k))

            @pl.when(end)
            def _():
                for at, j in enumerate((2 * far + 1 - parity, 2 * far + parity)):
                    @pl.loop(0, tiles)
                    def _(r, at=at, j=j):
                        t_v[at, row(r), :] = product(f_v, j, r, slice(ha * w, per - v))

    @pl.when(middle)
    def _():
        @pl.loop(0, n // 2)
        def _(h):
            first(0, 2 * h + 1 - parity).wait_send()

    def by_role(act, low=0, high=tiles):
        for role, span in ((middle, whole), (end, rest)):
            @pl.when(role)
            def _():
                @pl.loop(low, high)
                def _(r):
                    act(r, span)

    def for_partner(slot):
        j = 2 * slot + 1 - parity

        def act(r, span):
            o_m[row(r), wide(j)] = product(f_v, j, r, span).astype(o_m.dtype)

        by_role(act)
        first(1, j).start()

    final = slice(per - v, per)

    def far_total(at, r, span):
        j = 2 * far + (parity if at else 1 - parity)
        if span is whole:
            return product(f_v, j, r, whole)
        return t_v[at, row(r), :] + product(f_v, j, r, final)

    def far_first(way):
        return pltpu.make_async_remote_copy(
            src_ref=o_m.at[part(way), wide(2 * far + 1 - parity)], dst_ref=one_v.at[1, far, part(way), :],
            send_sem=far_sem.at[0, way], recv_sem=far_sem.at[1, way],
            device_id=(a, partner), device_id_type=MESH,
        )

    for way in range(2):
        low, high = way * tiles // 2, (way + 1) * tiles // 2

        @pl.loop(low, high)
        def _(r):
            f_v[row(r), final] = jnp.dot(
                m_v[row(r), :], a_v[:, final], preferred_element_type=jnp.float32
            ).astype(f_v.dtype)

        def act(r, span):
            o_m[row(r), wide(2 * far + 1 - parity)] = far_total(0, r, span).astype(o_m.dtype)

        by_role(act, low, high)
        far_first(way).start()

    regroup_all(last + 1, functools.partial(half, 2 * last + 1))

    def piece(place_of, way, place, target):
        return pltpu.make_async_remote_copy(
            src_ref=s_v.at[place_of, part(way), :],
            dst_ref=two_v.at[3, part(way), :] if place == 0 else late_hbm.at[place - 1, part(way), :],
            send_sem=two_send.at[way, place], recv_sem=two_recv.at[way, place],
            device_id=(a, 2 * target + parity), device_id_type=MESH,
        )

    def turn(h):
        return jnp.where(h == 0, far, jnp.where(h == 1, near[0], jnp.where(h == 2, near[1], chip)))

    for way in range(2):
        far_first(way).wait_recv()

        def act(r, span):
            total = far_total(1, r, span) + one_v[1, far, row(r), :].astype(jnp.float32)
            s_v[0, row(r), :] = total.astype(s_v.dtype)

        by_role(act, way * tiles // 2, (way + 1) * tiles // 2)
        piece(0, way, 0, near[way]).start()

    @pl.loop(1, n // 2)
    def _(h):
        for_partner(turn(h))

    @pl.loop(1, n // 2)
    def _(h):
        slot = turn(h)
        j = 2 * slot + parity
        first(1, j).wait_recv()

        def act(r, span):
            total = product(f_v, j, r, span) + one_v[1, slot, row(r), :].astype(jnp.float32)
            s_v[h, row(r), :] = total.astype(s_v.dtype)
            t_v[h, row(r), :] = total

        by_role(act)

        for way in range(2):
            @pl.when(h == 1 + way)
            def _():
                piece(1 + way, way, 1, near[way]).start()

    @pl.when(middle)
    def _():
        fourth_share()
        finish().start()

    for way in range(2):
        at = 1 - way
        piece(0, way, 0, near[way]).wait_recv()
        s_v[1 + at, part(way), :] = (t_v[1 + at, part(way), :] + two_v[3, part(way), :].astype(jnp.float32)).astype(s_v.dtype)
        piece(1 + at, way, 2, near[at]).start()

    result = pltpu.make_async_copy(t_v.at[3], part_hbm, local_sem.at[1])
    result.start()

    coef = m_v.at[pl.ds(0, virt), pl.ds(0, ao)]
    load_coef = pltpu.make_async_copy(virt_coef, coef, local_sem.at[0])
    load_coef.start()

    def regrouped(slot, where):
        keep(slot, where).wait()

        @pl.loop(1, n)
        def _(d):
            regroup(lax.rem(b + n - d, n), b, slot, where).wait_recv()

    each_piece(regrouped)

    occ = n * per // virt

    def slot_rows(slot):
        return pl.ds(pl.multiple_of(slot * rows, rows), rows)

    def block_copy(i, slot):
        return pltpu.make_async_copy(
            g_hbm.at[:, pl.ds(pl.multiple_of(i * virt, virt), virt)],
            m_v.at[slot_rows(slot), pl.ds(ao, virt)], g_sem.at[slot],
        )

    def out_copy(i, slot):
        return pltpu.make_async_copy(
            m_v.at[slot_rows(slot), pl.ds(ao + virt, ao)],
            fitted_ao.at[:, pl.ds(pl.multiple_of(i * ao, ao), ao)], o_sem.at[slot],
        )

    block_copy(0, 0).start()
    load_coef.wait()

    @pl.loop(0, occ)
    def _(i):
        slot = lax.rem(i, 2)

        @pl.when(i + 1 < occ)
        def _():
            block_copy(i + 1, 1 - slot).start()

        @pl.when(i >= 2)
        def _():
            out_copy(i - 2, slot).wait()

        block_copy(i, slot).wait()
        m_v[slot_rows(slot), pl.ds(ao + virt, ao)] = jnp.dot(
            m_v[slot_rows(slot), pl.ds(ao, virt)], m_v[pl.ds(0, virt), pl.ds(0, ao)],
            preferred_element_type=jnp.float32,
        ).astype(m_v.dtype)
        out_copy(i, slot).start()

    for i in range(max(occ - 2, 0), occ):
        out_copy(i, i % 2).wait()

    for way in range(2):
        piece(1, way, 1, near[way]).wait_recv()
        piece(1, way, 2, near[1 - way]).wait_recv()

    @pl.when(end)
    def _():
        finish().wait_recv()

    @pl.loop(1, n // 2)
    def _(h):
        first(1, 2 * turn(h) + 1 - parity).wait_send()

    for way in range(2):
        far_first(way).wait_send()

    for way in range(2):
        piece(0, way, 0, near[way]).wait_send()
        piece(1, way, 1, near[way]).wait_send()
        piece(1, way, 2, near[1 - way]).wait_send()

    def regroup_sent(slot, where):
        @pl.loop(1, n)
        def _(d):
            regroup(b, lax.rem(b + d, n), slot, where).wait_send()

    each_piece(regroup_sent)

    @pl.when(end)
    def _():
        lend().wait_send()

        @pl.loop(0, 2 * count)
        def _(k):
            z(a, k, 0).wait_send()

    @pl.when(middle)
    def _():
        finish().wait_send()

        @pl.loop(0, 2 * ha)
        def _(k):
            give(k).wait_send()

        @pl.loop(0, 2 * count)
        def _(k):
            z(a, k, 1).wait_send()
            z(mate, k, 1).wait_send()

        @pl.loop(2 * ha, 2 * count)
        def _(k):
            z(a, k, 0).wait_send()
            z(across, k, 0).wait_send()
            z(beyond, k, 0).wait_send()

    result.wait()


def close_kernel(na, part, late, ao_in, density, ao_out, p_v, l_v, w_v, copy_sem, in_sem, out_sem):
    a = lax.axis_index("aux")
    cuts = copy_sem.shape[1]
    span = ao_in.shape[1] // cuts
    steps = out_sem.shape[0]
    size = part.shape[0] // steps
    held = [slice(k * span, (k + 1) * span) for k in range(cuts)]
    fetches = [pltpu.make_async_copy(ao_in.at[:, held[k]], w_v.at[:, held[k]], copy_sem.at[0, k]) for k in range(cuts)]
    writes = [pltpu.make_async_copy(w_v.at[:, held[k]], ao_out.at[:, held[k]], copy_sem.at[1, k]) for k in range(cuts)]
    where = [pl.ds(k * size, size) for k in range(steps)]
    loads = [
        (
            pltpu.make_async_copy(part.at[where[k], :], p_v.at[where[k], :], in_sem.at[0, k]),
            pltpu.make_async_copy(late.at[:, where[k], :], l_v.at[:, where[k], :], in_sem.at[1, k]),
        )
        for k in range(steps)
    ]
    stores = [pltpu.make_async_copy(p_v.at[where[k], :], density.at[where[k], :], out_sem.at[k]) for k in range(steps)]
    at_end = jnp.logical_or(a == 0, a == na - 1)
    for copy in fetches:
        copy.start()
    for pair in loads:
        for copy in pair:
            copy.start()
    for k in range(cuts):
        fetches[k].wait()
        writes[k].start()
    for k in range(steps):
        for copy in loads[k]:
            copy.wait()
        total = p_v[where[k], :] + l_v[0, where[k], :].astype(jnp.float32) + l_v[1, where[k], :].astype(jnp.float32)
        third = jnp.where(at_end, l_v[2, where[k], :].astype(jnp.float32), 0.0)
        p_v[where[k], :] = total + third
        stores[k].start()
    for copy in stores + writes:
        copy.wait()


def cube_shards(na, n, count, metric, amplitudes, virt_coef):
    p, q = metric.shape
    per = amplitudes.shape[1]
    virt, ao = virt_coef.shape
    ha = count // 2
    rows = p // n
    bf16 = jnp.bfloat16
    dma = pltpu.SemaphoreType.DMA
    part, late, blocks, _ = pl.pallas_call(
        functools.partial(cube_kernel, na, n, count, ha),
        out_shape=(
            jax.ShapeDtypeStruct((p, q), jnp.float32),
            jax.ShapeDtypeStruct((3, p, q), bf16),
            jax.ShapeDtypeStruct((rows, n * per // virt * ao), bf16),
            jax.ShapeDtypeStruct((rows, n * per), bf16),
        ),
        in_specs=[pl.BlockSpec(memory_space=pl.ANY)] * 3,
        out_specs=(pl.BlockSpec(memory_space=pl.ANY),) * 4,
        scratch_shapes=[
            pltpu.VMEM((p, n * q), bf16),
            pltpu.VMEM((p, n * q), bf16),
            pltpu.VMEM((na * p, per), bf16),
            pltpu.VMEM((4, p, q), jnp.float32),
            pltpu.VMEM((4, p, q), bf16),
            pltpu.VMEM((p, per), bf16),
            pltpu.VMEM((p, per * ha // count), bf16),
            pltpu.VMEM((2, n // 2, p, q), bf16),
            pltpu.VMEM((4, p, q), bf16),
            dma((2, 9)), dma((2, 9)),
            dma((2, na, 2 * count)), dma((na, 2 * count)),
            dma((2 * ha,)), dma((2 * ha,)),
            dma((n, count + 1)), dma((n, count + 1)),
            dma((2, n // 2)), dma((2, n // 2)),
            dma((2, 3)), dma((2, 3)),
            dma((2, 3)), dma((2, 3)),
            dma((2,)), dma((2,)), dma((2, 2)), dma((2,)), dma((2,)), dma((2,)),
        ],
        compiler_params=pltpu.CompilerParams(
            collective_id=0, has_side_effects=True, vmem_limit_bytes=67043328
        ),
    )(metric, amplitudes, virt_coef)
    return pl.pallas_call(
        functools.partial(close_kernel, na),
        out_shape=(jax.ShapeDtypeStruct(part.shape, part.dtype), jax.ShapeDtypeStruct(blocks.shape, blocks.dtype)),
        in_specs=[pl.BlockSpec(memory_space=pl.ANY)] * 3,
        out_specs=(pl.BlockSpec(memory_space=pl.ANY),) * 2,
        scratch_shapes=[
            pltpu.VMEM((p, q), jnp.float32), pltpu.VMEM((3, p, q), bf16), pltpu.VMEM(blocks.shape, bf16),
            dma((2, 8)), dma((2, 4)), dma((4,)),
        ],
        compiler_params=pltpu.CompilerParams(vmem_limit_bytes=67043328),
    )(part, late, blocks)


def fits_cube(na, n, metric, amplitudes, virt_coef):
    p, per, (virt, ao) = metric.shape[0], amplitudes.shape[1], virt_coef.shape
    return (
        na == 4 and n == 8 and per % 2048 == 0 and p % 256 == 0
        and metric.shape[1] * n == na * p and virt <= p and virt + 2 * ao <= na * p
        and virt % 128 == 0 and ao % 128 == 0 and n * per % virt == 0
    )


def any_shards(na, n, metric, amplitudes, virt_coef):
    if fits_cube(na, n, metric, amplitudes, virt_coef):
        return cube_shards(na, n, 8, metric, amplitudes, virt_coef)
    return shards(na, n, metric, amplitudes, virt_coef)


def solution(mesh):
    in_specs = (P("aux", "pair"), P("aux", "pair"), P())
    out_specs = (P("aux", "pair"), P(("aux", "pair"), None))
    body = functools.partial(any_shards, mesh.shape["aux"], mesh.shape["pair"])
    return jax.shard_map(body, mesh=mesh, in_specs=in_specs, out_specs=out_specs, check_vma=False)
```

```python
import functools

import jax
import jax.numpy as jnp
from jax import lax
from jax.experimental import pallas as pl
from jax.experimental.pallas import tpu as pltpu
from jax.sharding import PartitionSpec as P

MESH = pl.DeviceIdType.MESH


def kernel(
    na, n, count, metric, amp, virt_coef, density, fitted_ao,
    m_v, a_v, d_v, f_v, g_v, c_v, one_v, two_v, o_v,
    m_send, m_recv, z_send, z_recv, x_send, x_recv, one_send, one_recv, two_send, two_recv, o_sem, local_sem,
):
    a, b = lax.axis_index("aux"), lax.axis_index("pair")
    p, q = metric.shape
    per = amp.shape[1]
    w = per // count
    rows = p // n
    virt, ao = virt_coef.shape
    half = n // 2
    parity, chip = lax.rem(b, 2), b // 2
    partner = b + 1 - 2 * parity
    tile = min(256, p)
    tiles = p // tile

    barrier = pltpu.get_barrier_semaphore()
    for d in range(1, n):
        pl.semaphore_signal(barrier, inc=1, device_id=(a, lax.rem(b + d, n)), device_id_type=MESH)

    @pl.when(a > 0)
    def _():
        pl.semaphore_signal(barrier, inc=1, device_id=(a - 1, b), device_id_type=MESH)

    @pl.when(a < na - 1)
    def _():
        pl.semaphore_signal(barrier, inc=1, device_id=(a + 1, b), device_id_type=MESH)

    pl.semaphore_wait(barrier, n - 1 + jnp.where(a > 0, 1, 0) + jnp.where(a < na - 1, 1, 0))

    def block_of(s, c):
        return a_v.at[c, pl.ds(pl.multiple_of(s * p, p), p), :]

    def hop(src, s, c, way, target):
        return pltpu.make_async_remote_copy(
            src_ref=src, dst_ref=block_of(s, c), send_sem=z_send.at[way, s, c],
            recv_sem=z_recv.at[s, c], device_id=(target, b), device_id_type=MESH,
        )

    def metric_copy(owner, target):
        return pltpu.make_async_remote_copy(
            src_ref=metric, dst_ref=m_v.at[:, pl.ds(pl.multiple_of(owner * q, q), q)],
            send_sem=m_send.at[target], recv_sem=m_recv.at[owner],
            device_id=(a, target), device_id_type=MESH,
        )

    def regroup(owner, target, c):
        return pltpu.make_async_remote_copy(
            src_ref=f_v.at[c, pl.ds(pl.multiple_of(target * rows, rows), rows), :],
            dst_ref=g_v.at[:, pl.ds(pl.multiple_of(owner * per + c * w, w), w)],
            send_sem=x_send.at[target, c], recv_sem=x_recv.at[owner, c],
            device_id=(a, target), device_id_type=MESH,
        )

    def staged(j):
        return m_v.at[:, pl.ds(pl.multiple_of(j * q, q), q)]

    def first(j):
        return pltpu.make_async_remote_copy(
            src_ref=staged(j), dst_ref=one_v.at[j // 2], send_sem=one_send.at[j // 2],
            recv_sem=one_recv.at[j // 2], device_id=(a, partner), device_id_type=MESH,
        )

    def second(source, j):
        return pltpu.make_async_remote_copy(
            src_ref=staged(j), dst_ref=two_v.at[source], send_sem=two_send.at[0, j // 2],
            recv_sem=two_recv.at[0, source], device_id=(a, j), device_id_type=MESH,
        )

    def mine(c):
        return amp.at[:, c * w : (c + 1) * w]

    for c in range(count):
        @pl.when(a > 0)
        def _():
            hop(mine(c), a, c, 0, jnp.maximum(a - 1, 0)).start()

        @pl.when(a < na - 1)
        def _():
            hop(mine(c), a, c, 1, jnp.minimum(a + 1, na - 1)).start()

    @pl.loop(1, n)
    def _(d):
        metric_copy(b, lax.rem(b + d, n)).start()

    own_copies = [pltpu.make_async_copy(mine(c), block_of(a, c), local_sem.at[c]) for c in range(count)]
    own_copies.append(pltpu.make_async_copy(metric, staged(b), local_sem.at[count]))
    own_copies.append(pltpu.make_async_copy(virt_coef, c_v, local_sem.at[count + 1]))
    for copy in own_copies:
        copy.start()

    def arrive(t, c):
        @pl.when(a - t >= 0)
        def _():
            s = jnp.maximum(a - t, 0)
            hop(block_of(s, c), s, c, 1, a).wait_recv()

            @pl.when(a < na - 1)
            def _():
                hop(block_of(s, c), s, c, 1, jnp.minimum(a + 1, na - 1)).start()

        @pl.when(a + t < na)
        def _():
            s = jnp.minimum(a + t, na - 1)
            hop(block_of(s, c), s, c, 0, a).wait_recv()

            @pl.when(a > 0)
            def _():
                hop(block_of(s, c), s, c, 0, jnp.maximum(a - 1, 0)).start()

    @pl.loop(1, na - 1)
    def _(t):
        @pl.loop(0, count)
        def _(c):
            arrive(t, c)

    for copy in own_copies:
        copy.wait()

    @pl.loop(1, n)
    def _(d):
        metric_copy(lax.rem(b + n - d, n), b).wait_recv()

    @pl.loop(1, n)
    def _(d):
        metric_copy(b, lax.rem(b + d, n)).wait_send()

    def row(r):
        return pl.ds(pl.multiple_of(r * tile, tile), tile)

    def product(j, r, c):
        right = a_v[c, pl.ds(pl.multiple_of(j * q, q), q), :]
        return lax.dot_general(
            f_v[c, row(r), :], right, (((1,), (1,)), ((), ())), preferred_element_type=jnp.float32
        )

    def fit(c):
        @pl.loop(0, tiles)
        def _(r):
            f_v[c, row(r), :] = jnp.dot(
                m_v[row(r), :], a_v[c], preferred_element_type=jnp.float32
            ).astype(f_v.dtype)

        @pl.loop(1, n)
        def _(d):
            regroup(b, lax.rem(b + d, n), c).start()

        pltpu.make_async_copy(
            f_v.at[c, pl.ds(pl.multiple_of(b * rows, rows), rows), :],
            g_v.at[:, pl.ds(pl.multiple_of(b * per + c * w, w), w)], x_send.at[b, c],
        ).start()

    @pl.loop(0, n * tiles)
    def _(i):
        d_v[i // tiles, row(lax.rem(i, tiles)), :] = jnp.zeros((tile, q), jnp.float32)

    @pl.loop(0, count - 1)
    def _(c):
        arrive(na - 1, c)
        fit(c)

        @pl.loop(0, n * tiles)
        def _(i):
            j, r = i // tiles, lax.rem(i, tiles)
            d_v[j, row(r), :] += product(j, r, c)

    last = count - 1
    arrive(na - 1, last)
    fit(last)

    quad = half == 4
    mid = p // 2
    near = (chip + 1 - 2 * lax.rem(chip, 2), lax.rem(chip + 2, 4))
    far = 3 - chip

    def turn(h):
        if not quad:
            return lax.rem(chip + h, half)
        return jnp.where(h == 0, far, jnp.where(h == 1, near[0], jnp.where(h == 2, near[1], chip)))

    @pl.loop(0, half)
    def _(h):
        j = 2 * turn(h) + 1 - parity

        @pl.loop(0, tiles)
        def _(r):
            m_v[row(r), pl.ds(pl.multiple_of(j * q, q), q)] = (
                d_v[j, row(r), :] + product(j, r, last)
            ).astype(m_v.dtype)

        first(j).start()

    @pl.loop(0, 0 if quad else half)
    def _(h):
        j = 2 * lax.rem(chip + h, half) + parity

        @pl.loop(0, tiles)
        def _(r):
            d_v[j, row(r), :] += product(j, r, last)

    def part(way):
        return pl.ds(way * mid, mid)

    def cast(slot, way):
        j = 2 * slot + parity
        m_v[part(way), pl.ds(pl.multiple_of(j * q, q), q)] = d_v[j, part(way), :].astype(m_v.dtype)

    def piece(slot, way, place, target):
        j = 2 * slot + parity
        return pltpu.make_async_remote_copy(
            src_ref=m_v.at[part(way), pl.ds(pl.multiple_of(j * q, q), q)],
            dst_ref=two_v.at[place, part(way), :], send_sem=two_send.at[way, place],
            recv_sem=two_recv.at[way, place], device_id=(a, 2 * target + parity), device_id_type=MESH,
        )

    def add_in(slot, place, way):
        j = 2 * slot + parity
        d_v[j, part(way), :] += two_v[place, part(way), :].astype(jnp.float32)

    if quad:
        for h in range(4):
            slot = (far, near[0], near[1], chip)[h]

            @pl.loop(0, tiles)
            def _(r, slot=slot):
                d_v[2 * slot + parity, row(r), :] += product(2 * slot + parity, r, last)

            first(2 * slot + parity).wait_recv()

            @pl.loop(0, tiles)
            def _(r, slot=slot):
                j = 2 * slot + parity
                d_v[j, row(r), :] += one_v[slot, row(r), :].astype(jnp.float32)

            if h == 0:
                for way in range(2):
                    cast(far, way)
                    piece(far, way, 0, near[way]).start()
            elif h < 3:
                cast(near[h - 1], h - 1)
                piece(near[h - 1], h - 1, 1, near[h - 1]).start()
    else:
        @pl.loop(1, half)
        def _(h):
            slot = lax.rem(chip + h, half)
            j = 2 * slot + parity
            first(j).wait_recv()

            @pl.loop(0, tiles)
            def _(r):
                m_v[row(r), pl.ds(pl.multiple_of(j * q, q), q)] = (
                    d_v[j, row(r), :] + one_v[slot, row(r), :].astype(jnp.float32)
                ).astype(m_v.dtype)

            second(chip, j).start()

        first(b).wait_recv()

        @pl.loop(0, tiles)
        def _(r):
            d_v[b, row(r), :] += one_v[chip, row(r), :].astype(jnp.float32)

    if quad:
        for way in range(2):
            other = near[1 - way]
            piece(other, way, 0, near[way]).wait_recv()
            add_in(other, 0, way)
            cast(other, way)
            piece(other, way, 2, other).start()

    @pl.loop(0, count)
    def _(c):
        pltpu.make_async_copy(
            f_v.at[c, pl.ds(pl.multiple_of(b * rows, rows), rows), :],
            g_v.at[:, pl.ds(pl.multiple_of(b * per + c * w, w), w)], x_send.at[b, c],
        ).wait()

        @pl.loop(1, n)
        def _(d):
            regroup(lax.rem(b + n - d, n), b, c).wait_recv()

    occ = n * per // virt

    def out_copy(i, slot):
        return pltpu.make_async_copy(
            o_v.at[slot], fitted_ao.at[:, pl.ds(pl.multiple_of(i * ao, ao), ao)], o_sem.at[slot]
        )

    @pl.loop(0, occ)
    def _(i):
        slot = lax.rem(i, 2)

        @pl.when(i >= 2)
        def _():
            out_copy(i - 2, slot).wait()

        o_v[slot] = jnp.dot(
            g_v[:, pl.ds(pl.multiple_of(i * virt, virt), virt)], c_v[...], preferred_element_type=jnp.float32
        ).astype(o_v.dtype)
        out_copy(i, slot).start()

    for i in range(max(occ - 2, 0), occ):
        out_copy(i, i % 2).wait()

    if quad:
        for way in range(2):
            piece(chip, way, 1, near[way]).wait_recv()
            add_in(chip, 1, way)
        for way in range(2):
            piece(chip, way, 2, near[1 - way]).wait_recv()
            add_in(chip, 2, way)
    else:
        @pl.loop(1, half)
        def _(h):
            source = lax.rem(chip + half - h, half)
            second(source, b).wait_recv()

            @pl.loop(0, tiles)
            def _(r):
                d_v[b, row(r), :] += two_v[source, row(r), :].astype(jnp.float32)

    result = pltpu.make_async_copy(d_v.at[b], density, local_sem.at[0])
    result.start()

    @pl.loop(0, half)
    def _(h):
        first(2 * h + 1 - parity).wait_send()

    if quad:
        for way in range(2):
            piece(far, way, 0, near[way]).wait_send()
            piece(near[way], way, 1, near[way]).wait_send()
            piece(near[1 - way], way, 2, near[1 - way]).wait_send()
    else:
        @pl.loop(1, half)
        def _(h):
            second(chip, 2 * lax.rem(chip + h, half) + parity).wait_send()

    @pl.loop(0, count)
    def _(c):
        @pl.loop(1, n)
        def _(d):
            regroup(b, lax.rem(b + d, n), c).wait_send()

        @pl.loop(0, na)
        def _(s):
            @pl.when(jnp.logical_and(s >= a, a > 0))
            def _():
                hop(block_of(s, c), s, c, 0, jnp.maximum(a - 1, 0)).wait_send()

            @pl.when(jnp.logical_and(s <= a, a < na - 1))
            def _():
                hop(block_of(s, c), s, c, 1, jnp.minimum(a + 1, na - 1)).wait_send()

    result.wait()


def shards(na, n, metric, amplitudes, virt_coef):
    p, q = metric.shape
    per = amplitudes.shape[1]
    virt, ao = virt_coef.shape
    count = next(c for c in (8, 4, 2, 1) if per % (128 * c) == 0)
    w = per // count
    rows = p // n
    bf16 = jnp.bfloat16
    dma = pltpu.SemaphoreType.DMA
    return pl.pallas_call(
        functools.partial(kernel, na, n, count),
        out_shape=(
            jax.ShapeDtypeStruct((p, q), jnp.float32),
            jax.ShapeDtypeStruct((rows, n * per // virt * ao), bf16),
        ),
        in_specs=[pl.BlockSpec(memory_space=pl.ANY)] * 3,
        out_specs=(pl.BlockSpec(memory_space=pl.ANY), pl.BlockSpec(memory_space=pl.ANY)),
        scratch_shapes=[
            pltpu.VMEM((p, n * q), bf16),
            pltpu.VMEM((count, na * p, w), bf16),
            pltpu.VMEM((n, p, q), jnp.float32),
            pltpu.VMEM((count, p, w), bf16),
            pltpu.VMEM((rows, n * per), bf16),
            pltpu.VMEM((virt, ao), bf16),
            pltpu.VMEM((n // 2, p, q), bf16),
            pltpu.VMEM((n // 2, p, q), bf16),
            pltpu.VMEM((2, rows, ao), bf16),
            dma((n,)), dma((n,)),
            dma((2, na, count)), dma((na, count)),
            dma((n, count)), dma((n, count)),
            dma((n // 2,)), dma((n // 2,)),
            dma((2, n // 2)), dma((2, n // 2)),
            dma((2,)), dma((count + 2,)),
        ],
        compiler_params=pltpu.CompilerParams(
            collective_id=0, has_side_effects=True, vmem_limit_bytes=67043328
        ),
    )(metric, amplitudes, virt_coef)

def cube_kernel(
    na, n, count, ha, metric, amp, virt_coef, part_out, late_out, blocks_out, g_hbm,
    m_v, o_m, a_v, t_v, f_v, e_v, one_v, two_v,
    m_send, m_recv, z_send, z_recv, e_send, e_recv, x_send, x_recv,
    one_send, one_recv, two_send, two_recv, r_send, r_recv,
    mm_sem, fin_sem, far_sem, g_sem, local_sem,
):
    a, b = lax.axis_index("aux"), lax.axis_index("pair")
    p, q = metric.shape
    per = amp.shape[1]
    w = per // count
    rows = p // n
    virt, ao = virt_coef.shape
    parity, chip = lax.rem(b, 2), b // 2
    flip = 1 - 2 * parity
    partner = b + flip
    near = (chip + 1 - 2 * lax.rem(chip, 2), lax.rem(chip + 2, 4))
    far = 3 - chip
    xb, yb, fb = 2 * near[0] + parity, 2 * near[1] + parity, 2 * far + parity
    tile = 256 if p % 512 == 0 else 128
    tiles = p // tile
    mid = p // 2
    last = count - 1

    middle = jnp.logical_and(a > 0, a < na - 1)
    end = jnp.logical_not(middle)
    mate = a + 1 - 2 * lax.rem(a, 2)
    across = na - 1 - a
    beyond = na - 1 - mate

    barrier = pltpu.get_barrier_semaphore()
    for d in range(1, n):
        pl.semaphore_signal(barrier, inc=1, device_id=(a, lax.rem(b + d, n)), device_id_type=MESH)
    pl.semaphore_signal(barrier, inc=1, device_id=(mate, b), device_id_type=MESH)

    @pl.when(middle)
    def _():
        pl.semaphore_signal(barrier, inc=1, device_id=(across, b), device_id_type=MESH)

    pl.semaphore_wait(barrier, n + jnp.where(middle, 1, 0))

    v = w // 2

    def cols(c, base=0):
        return pl.ds(pl.multiple_of(base + c * w, w), w)

    def half(k, base=0):
        return pl.ds(pl.multiple_of(base + k * v, v), v)

    def row(r):
        return pl.ds(pl.multiple_of(r * tile, tile), tile)

    def part(way):
        return pl.ds(way * mid, mid)

    def wide(j):
        return pl.ds(pl.multiple_of(j * q, q), q)

    def block_of(s, k):
        return a_v.at[pl.ds(pl.multiple_of(s * p, p), p), half(k)]

    def z(s, k, way, own=False):
        return pltpu.make_async_remote_copy(
            src_ref=amp.at[:, half(k)] if own else block_of(s, k), dst_ref=block_of(s, k),
            send_sem=z_send.at[way, s, k], recv_sem=z_recv.at[s, k],
            device_id=(mate if way == 0 else across, b), device_id_type=MESH,
        )

    def own(way, *halves):
        for k in halves:
            z(a, k, way, True).start()

    def relay(s, k, way):
        z(s, k, way).wait_recv()
        z(s, k, way).start()

    def lend():
        return pltpu.make_async_remote_copy(
            src_ref=metric, dst_ref=o_m.at[:, wide(b)], send_sem=mm_sem.at[0], recv_sem=mm_sem.at[1],
            device_id=(mate, b), device_id_type=MESH,
        )

    def give(k):
        return pltpu.make_async_remote_copy(
            src_ref=e_v.at[:, half(k)], dst_ref=f_v.at[:, half(k)], send_sem=e_send.at[k], recv_sem=e_recv.at[k],
            device_id=(mate, b), device_id_type=MESH,
        )

    def staged(j):
        return o_m.at[:, wide(j)]

    def finish():
        return pltpu.make_async_remote_copy(
            src_ref=staged(b), dst_ref=two_v.at[0], send_sem=fin_sem.at[0], recv_sem=fin_sem.at[1],
            device_id=(mate, b), device_id_type=MESH,
        )

    def region(kind, mirror):
        mine = (b, b, b, xb, yb, xb, yb, fb, fb)
        theirs = (xb, yb, partner, fb, fb, xb + flip, yb + flip, fb + flip, fb + flip)
        side = (None, None, None, 0, 1, None, None, 0, 1)[kind]
        j = (theirs if mirror else mine)[kind]
        return (slice(None) if side is None else part(side), wide(j))

    def gather(g, kind, mirror=False):
        buf = (m_v, o_m)[g]
        where = region(kind, mirror)
        target = (xb, yb, partner, yb, xb, partner, partner, partner, partner)[kind]
        return pltpu.make_async_remote_copy(
            src_ref=metric if g == 0 and kind < 3 and not mirror else buf.at[where], dst_ref=buf.at[where],
            send_sem=m_send.at[g, kind], recv_sem=m_recv.at[g, kind],
            device_id=(a, target), device_id_type=MESH,
        )

    def got(g, kind):
        gather(g, kind, True).wait_recv()

    def gather_open(g):
        for kind in range(3):
            gather(g, kind).start()

    def gather_turn(g):
        got(g, 0)
        gather(g, 3).start()
        gather(g, 5).start()
        got(g, 1)
        gather(g, 4).start()
        gather(g, 6).start()

    def gather_close(g):
        got(g, 3)
        gather(g, 7).start()
        got(g, 4)
        gather(g, 8).start()
        for kind in (2, 5, 6, 7, 8):
            got(g, kind)
        for kind in range(9):
            gather(g, kind).wait_send()

    def regroup(owner, target, slot, where):
        return pltpu.make_async_remote_copy(
            src_ref=f_v.at[pl.ds(pl.multiple_of(target * rows, rows), rows), where()],
            dst_ref=g_hbm.at[:, where(owner * per)],
            send_sem=x_send.at[target, slot], recv_sem=x_recv.at[owner, slot],
            device_id=(a, target), device_id_type=MESH,
        )

    def keep(slot, where):
        return pltpu.make_async_copy(
            f_v.at[pl.ds(pl.multiple_of(b * rows, rows), rows), where()],
            g_hbm.at[:, where(b * per)], x_send.at[b, slot],
        )

    def regroup_all(slot, where):
        @pl.loop(1, n)
        def _(d):
            regroup(b, lax.rem(b + d, n), slot, where).start()

        keep(slot, where).start()

    def each_piece(act):
        @pl.loop(0, last)
        def _(c):
            act(c, functools.partial(cols, c))

        for k in (2 * last, 2 * last + 1):
            act(k - last, functools.partial(half, k))

    def fit(mat, dst, where):
        @pl.loop(0, tiles)
        def _(r):
            dst[row(r), where] = jnp.dot(
                mat[row(r), :], a_v[:, where], preferred_element_type=jnp.float32
            ).astype(dst.dtype)

    def product(left, j, r, span):
        return lax.dot_general(
            left[row(r), span], a_v[wide(j), span], (((1,), (1,)), ((), ())), preferred_element_type=jnp.float32
        )

    early, rest, whole = slice(0, ha * w), slice(ha * w, per), slice(0, per)

    def first(turn, j):
        return pltpu.make_async_remote_copy(
            src_ref=staged(j), dst_ref=one_v.at[turn, j // 2], send_sem=one_send.at[turn, j // 2],
            recv_sem=one_recv.at[turn, j // 2], device_id=(a, partner), device_id_type=MESH,
        )

    def early_piece(target, way, place):
        return pltpu.make_async_remote_copy(
            src_ref=o_m.at[part(way), wide((xb, yb, fb)[target])], dst_ref=two_v.at[place, part(way), :],
            send_sem=r_send.at[way, place], recv_sem=r_recv.at[way, place],
            device_id=(a, (xb, yb)[target if place else way]), device_id_type=MESH,
        )

    own_copies = [
        pltpu.make_async_copy(amp, a_v.at[pl.ds(pl.multiple_of(a * p, p), p), :], local_sem.at[0]),
        pltpu.make_async_copy(metric, m_v.at[:, wide(b)], local_sem.at[1]),
    ]

    gather_open(0)

    @pl.when(end)
    def _():
        lend().start()
        own(0, *range(2 * count))

    @pl.when(middle)
    def _():
        own(1, 2 * ha, 2 * ha + 1, 2 * ha + 2, 2 * ha + 3, 0, 1)
        own(0, *range(2 * ha, 2 * count))

    for copy in own_copies:
        copy.start()

    @pl.when(end)
    def _():
        gather_turn(0)
        gather_close(0)

    @pl.when(middle)
    def _():
        lend().wait_recv()
        gather_open(1)
        for k in range(2 * ha, 2 * ha + 4):
            relay(across, k, 0)
        relay(mate, 0, 1)
        relay(mate, 1, 1)
        own(1, 2, 3)
        gather_turn(1)
        relay(mate, 2, 1)
        relay(mate, 3, 1)
        own(1, 4, 5)
        gather_turn(0)
        relay(mate, 4, 1)
        relay(mate, 5, 1)
        own(1, 6)
        gather_close(1)

    for copy in own_copies:
        copy.wait()

    def first_share(low, high):
        @pl.loop(low, high)
        def _(h):
            j = 2 * h + 1 - parity

            @pl.loop(0, tiles)
            def _(r):
                o_m[row(r), wide(j)] = product(e_v, j, r, early).astype(o_m.dtype)

            first(0, j).start()

    def first_total(j, r):
        return product(e_v, j, r, early) + one_v[0, j // 2, row(r), :].astype(jnp.float32)

    def second_share(target):
        j = (xb, yb, fb)[target]
        first(0, j).wait_recv()

        @pl.loop(0, tiles)
        def _(r):
            o_m[row(r), wide(j)] = first_total(j, r).astype(o_m.dtype)

        if target == 2:
            early_piece(2, 0, 0).start()
            early_piece(2, 1, 0).start()
        else:
            early_piece(target, target, 1).start()

    def third_share():
        for way in range(2):
            other = 1 - way
            early_piece(2, way, 0).wait_recv()

            @pl.loop(way * tiles // 2, (way + 1) * tiles // 2)
            def _(r, j=(xb, yb)[other]):
                total = first_total(j, r) + two_v[0, row(r), :].astype(jnp.float32)
                o_m[row(r), wide(j)] = total.astype(o_m.dtype)

            early_piece(other, way, 2).start()

    def fourth_share():
        first(0, b).wait_recv()
        for way in range(2):
            early_piece(way, way, 1).wait_recv()
            early_piece(1 - way, way, 2).wait_recv()

        @pl.loop(0, tiles)
        def _(r):
            total = first_total(b, r)
            for place in (1, 2):
                total += two_v[place, row(r), :].astype(jnp.float32)
            o_m[row(r), wide(b)] = total.astype(o_m.dtype)

        for way in range(2):
            early_piece(2, way, 0).wait_send()
            early_piece(way, way, 1).wait_send()
            early_piece(1 - way, way, 2).wait_send()

    @pl.loop(0, ha - 1)
    def _(c):
        @pl.when(middle)
        def _():
            for k in (2 * c, 2 * c + 1):
                z(across, k, 0).wait_recv()
                z(beyond, k, 0).wait_recv()
            fit(o_m, e_v, cols(c))
            give(2 * c).start()
            give(2 * c + 1).start()
            relay(mate, 2 * c + 6, 1)

            @pl.when(c == 0)
            def _():
                own(1, 7)

            relay(mate, 2 * c + 7, 1)

            @pl.when(c == 2)
            def _():
                own(1, 12, 13)

            @pl.when(c == 0)
            def _():
                gather_close(0)

            fit(m_v, f_v, cols(c))

        @pl.when(end)
        def _():
            give(2 * c).wait_recv()
            give(2 * c + 1).wait_recv()

        regroup_all(c, functools.partial(cols, c))

    @pl.when(middle)
    def _():
        for k in (6, 7):
            z(across, k, 0).wait_recv()
            z(beyond, k, 0).wait_recv()
            fit(o_m, e_v, half(k))
            give(k).start()
            if k == 6:
                relay(mate, 12, 1)
                relay(mate, 13, 1)
                own(1, 14)
        relay(mate, 14, 1)
        own(1, 15)
        relay(mate, 15, 1)
        fit(m_v, f_v, cols(ha - 1))

    @pl.when(end)
    def _():
        give(6).wait_recv()
        give(7).wait_recv()

    regroup_all(ha - 1, functools.partial(cols, ha - 1))

    def all_in(k):
        for source in (mate, across, beyond):
            z(source, k, 0).wait_recv()

    @pl.loop(ha, last)
    def _(c):
        @pl.when(middle)
        def _():
            @pl.when(c == last - 1)
            def _():
                relay(across, 2 * c, 0)
                relay(across, 2 * c + 1, 0)

            relay(beyond, 2 * c, 0)

            @pl.when(c == ha)
            def _():
                first_share(0, 2)

            @pl.when(c == ha + 1)
            def _():
                second_share(2)

            relay(beyond, 2 * c + 1, 0)

            @pl.when(c == ha)
            def _():
                first_share(2, n // 2)

            @pl.when(c == ha + 1)
            def _():
                second_share(0)
                second_share(1)

            @pl.when(c == last - 1)
            def _():
                third_share()

        @pl.when(end)
        def _():
            all_in(2 * c)
            all_in(2 * c + 1)

        fit(m_v, f_v, cols(c))
        regroup_all(c, functools.partial(cols, c))

    for k in (2 * last, 2 * last + 1):
        @pl.when(middle)
        def _():
            relay(across, k, 0)
            relay(beyond, k, 0)

        @pl.when(end)
        def _():
            all_in(k)

        if k == 2 * last:
            fit(m_v, f_v, half(k))
            regroup_all(k - last, functools.partial(half, k))

            @pl.when(end)
            def _():
                for at, j in enumerate((2 * far + 1 - parity, 2 * far + parity)):
                    @pl.loop(0, tiles)
                    def _(r, at=at, j=j):
                        (part_out, t_v)[at][row(r), :] = product(f_v, j, r, slice(ha * w, per - v))

    @pl.when(middle)
    def _():
        @pl.loop(0, n // 2)
        def _(h):
            first(0, 2 * h + 1 - parity).wait_send()

    def by_role(act, low=0, high=tiles):
        for role, span in ((middle, whole), (end, rest)):
            @pl.when(role)
            def _():
                @pl.loop(low, high)
                def _(r):
                    act(r, span)

    def for_partner(slot):
        j = 2 * slot + 1 - parity

        def act(r, span):
            o_m[row(r), wide(j)] = product(f_v, j, r, span).astype(o_m.dtype)

        by_role(act)
        first(1, j).start()

    final = slice(per - v, per)

    def far_total(at, r, span):
        j = 2 * far + (parity if at else 1 - parity)
        if span is whole:
            return product(f_v, j, r, whole)
        return (part_out, t_v)[at][row(r), :] + product(f_v, j, r, final)

    def far_first(way):
        return pltpu.make_async_remote_copy(
            src_ref=o_m.at[part(way), wide(2 * far + 1 - parity)], dst_ref=one_v.at[1, far, part(way), :],
            send_sem=far_sem.at[0, way], recv_sem=far_sem.at[1, way],
            device_id=(a, partner), device_id_type=MESH,
        )

    for way in range(2):
        low, high = way * tiles // 2, (way + 1) * tiles // 2

        @pl.loop(low, high)
        def _(r):
            f_v[row(r), final] = jnp.dot(
                m_v[row(r), :], a_v[:, final], preferred_element_type=jnp.float32
            ).astype(f_v.dtype)

        def act(r, span):
            o_m[row(r), wide(2 * far + 1 - parity)] = far_total(0, r, span).astype(o_m.dtype)

        by_role(act, low, high)
        far_first(way).start()

    regroup_all(last + 1, functools.partial(half, 2 * last + 1))

    spare = n * q - 3 * q

    def sent(at):
        return pl.ds(spare + at * q, q)

    def piece(place_of, way, place, target):
        return pltpu.make_async_remote_copy(
            src_ref=m_v.at[part(way), sent(place_of)],
            dst_ref=two_v.at[3, part(way), :] if place == 0 else late_out.at[place - 1, part(way), :],
            send_sem=two_send.at[way, place], recv_sem=two_recv.at[way, place],
            device_id=(a, 2 * target + parity), device_id_type=MESH,
        )

    def turn(h):
        return jnp.where(h == 0, far, jnp.where(h == 1, near[0], jnp.where(h == 2, near[1], chip)))

    for way in range(2):
        far_first(way).wait_recv()

        def act(r, span):
            total = far_total(1, r, span) + one_v[1, far, row(r), :].astype(jnp.float32)
            m_v[row(r), sent(0)] = total.astype(m_v.dtype)

        by_role(act, way * tiles // 2, (way + 1) * tiles // 2)
        piece(0, way, 0, near[way]).start()

    @pl.loop(1, n // 2)
    def _(h):
        for_partner(turn(h))

    @pl.loop(1, n // 2)
    def _(h):
        slot = turn(h)
        j = 2 * slot + parity
        first(1, j).wait_recv()

        def act(r, span):
            total = product(f_v, j, r, span) + one_v[1, slot, row(r), :].astype(jnp.float32)
            for at in (1, 2):
                @pl.when(h == at)
                def _():
                    m_v[row(r), sent(at)] = total.astype(m_v.dtype)

                @pl.when(jnp.logical_and(h == at, r >= tiles // 2 if at == 1 else r < tiles // 2))
                def _():
                    t_v[row(r), :] = total

            @pl.when(h == 3)
            def _():
                part_out[row(r), :] = total

        by_role(act)

        for way in range(2):
            @pl.when(h == 1 + way)
            def _():
                piece(1 + way, way, 1, near[way]).start()

    @pl.when(middle)
    def _():
        fourth_share()
        finish().start()

    for way in range(2):
        at = 1 - way
        piece(0, way, 0, near[way]).wait_recv()
        m_v[part(way), sent(1 + at)] = (t_v[part(way), :] + two_v[3, part(way), :].astype(jnp.float32)).astype(m_v.dtype)
        piece(1 + at, way, 2, near[at]).start()

    coef = m_v.at[pl.ds(0, virt), pl.ds(0, ao)]
    load_coef = pltpu.make_async_copy(virt_coef, coef, local_sem.at[0])
    load_coef.start()

    def regrouped(slot, where):
        keep(slot, where).wait()

        @pl.loop(1, n)
        def _(d):
            regroup(lax.rem(b + n - d, n), b, slot, where).wait_recv()

    each_piece(regrouped)

    occ = n * per // virt

    def slot_rows(slot):
        return pl.ds(pl.multiple_of(slot * rows, rows), rows)

    def block_copy(i, slot):
        return pltpu.make_async_copy(
            g_hbm.at[:, pl.ds(pl.multiple_of(i * virt, virt), virt)],
            e_v.at[slot_rows(slot), pl.ds(0, virt)], g_sem.at[slot],
        )

    @pl.when(middle)
    def _():
        @pl.loop(0, 2 * ha)
        def _(k):
            give(k).wait_send()

    block_copy(0, 0).start()
    load_coef.wait()

    @pl.loop(0, occ)
    def _(i):
        slot = lax.rem(i, 2)

        @pl.when(i + 1 < occ)
        def _():
            block_copy(i + 1, 1 - slot).start()

        block_copy(i, slot).wait()
        blocks_out[:, pl.ds(pl.multiple_of(i * ao, ao), ao)] = jnp.dot(
            e_v[slot_rows(slot), pl.ds(0, virt)], m_v[pl.ds(0, virt), pl.ds(0, ao)],
            preferred_element_type=jnp.float32,
        ).astype(blocks_out.dtype)

    for way in range(2):
        piece(1, way, 1, near[way]).wait_recv()
        piece(1, way, 2, near[1 - way]).wait_recv()

    @pl.when(end)
    def _():
        finish().wait_recv()

        @pl.loop(0, tiles)
        def _(r):
            part_out[row(r), :] += two_v[0, row(r), :].astype(jnp.float32)

    @pl.loop(1, n // 2)
    def _(h):
        first(1, 2 * turn(h) + 1 - parity).wait_send()

    for way in range(2):
        far_first(way).wait_send()

    for way in range(2):
        piece(0, way, 0, near[way]).wait_send()
        piece(1, way, 1, near[way]).wait_send()
        piece(1, way, 2, near[1 - way]).wait_send()

    def regroup_sent(slot, where):
        @pl.loop(1, n)
        def _(d):
            regroup(b, lax.rem(b + d, n), slot, where).wait_send()

    each_piece(regroup_sent)

    @pl.when(end)
    def _():
        lend().wait_send()

        @pl.loop(0, 2 * count)
        def _(k):
            z(a, k, 0).wait_send()

    @pl.when(middle)
    def _():
        finish().wait_send()

        @pl.loop(0, 2 * count)
        def _(k):
            z(a, k, 1).wait_send()
            z(mate, k, 1).wait_send()

        @pl.loop(2 * ha, 2 * count)
        def _(k):
            z(a, k, 0).wait_send()
            z(across, k, 0).wait_send()
            z(beyond, k, 0).wait_send()


def close_kernel(part, late, ao_in, density, ao_out, sum_v, copy_sem, out_sem):
    cuts, steps = copy_sem.shape[0], out_sem.shape[0]
    span, size = ao_in.shape[1] // cuts, part.shape[0] // steps
    writes = []
    for k in range(cuts):
        held = slice(k * span, (k + 1) * span)
        writes.append(pltpu.make_async_copy(ao_in.at[:, held], ao_out.at[:, held], copy_sem.at[k]))
    for copy in writes[: cuts // 2]:
        copy.start()
    for k in range(steps):
        where = pl.ds(k * size, size)
        sum_v[where, :] = (
            part[where, :] + late[0, where, :].astype(jnp.float32) + late[1, where, :].astype(jnp.float32)
        )
        store = pltpu.make_async_copy(sum_v.at[where, :], density.at[where, :], out_sem.at[k])
        store.start()
        writes.append(store)
    for copy in writes[cuts // 2 : cuts]:
        copy.start()
    for copy in writes:
        copy.wait()


def cube_shards(na, n, count, metric, amplitudes, virt_coef):
    p, q = metric.shape
    per = amplitudes.shape[1]
    virt, ao = virt_coef.shape
    ha = count // 2
    rows = p // n
    bf16 = jnp.bfloat16
    dma = pltpu.SemaphoreType.DMA
    part, late, blocks, _ = pl.pallas_call(
        functools.partial(cube_kernel, na, n, count, ha),
        out_shape=(
            pltpu.VMEM((p, q), jnp.float32),
            pltpu.VMEM((2, p, q), bf16),
            pltpu.VMEM((rows, n * per // virt * ao), bf16),
            jax.ShapeDtypeStruct((rows, n * per), bf16),
        ),
        in_specs=[pl.BlockSpec(memory_space=pl.ANY)] * 3,
        out_specs=(pl.BlockSpec(memory_space=pltpu.VMEM),) * 3 + (pl.BlockSpec(memory_space=pl.ANY),),
        scratch_shapes=[
            pltpu.VMEM((p, n * q), bf16),
            pltpu.VMEM((p, n * q), bf16),
            pltpu.VMEM((na * p, per), bf16),
            pltpu.VMEM((p, q), jnp.float32),
            pltpu.VMEM((p, per), bf16),
            pltpu.VMEM((p, per * ha // count), bf16),
            pltpu.VMEM((2, n // 2, p, q), bf16),
            pltpu.VMEM((4, p, q), bf16),
            dma((2, 9)), dma((2, 9)),
            dma((2, na, 2 * count)), dma((na, 2 * count)),
            dma((2 * ha,)), dma((2 * ha,)),
            dma((n, count + 1)), dma((n, count + 1)),
            dma((2, n // 2)), dma((2, n // 2)),
            dma((2, 3)), dma((2, 3)),
            dma((2, 3)), dma((2, 3)),
            dma((2,)), dma((2,)), dma((2, 2)), dma((2,)), dma((2,)),
        ],
        compiler_params=pltpu.CompilerParams(
            collective_id=0, has_side_effects=True, vmem_limit_bytes=54 * 2**20
        ),
    )(metric, amplitudes, virt_coef)
    return pl.pallas_call(
        close_kernel,
        out_shape=(jax.ShapeDtypeStruct(part.shape, part.dtype), jax.ShapeDtypeStruct(blocks.shape, bf16)),
        in_specs=[pl.BlockSpec(memory_space=pltpu.VMEM)] * 3,
        out_specs=(pl.BlockSpec(memory_space=pl.ANY),) * 2,
        scratch_shapes=[
            pltpu.VMEM((p, q), jnp.float32), dma((4,)), dma((4,)),
        ],
        compiler_params=pltpu.CompilerParams(vmem_limit_bytes=8 * 2**20),
    )(part, late, blocks)


def fits_cube(na, n, metric, amplitudes, virt_coef):
    p, per, (virt, ao) = metric.shape[0], amplitudes.shape[1], virt_coef.shape
    return (
        na == 4 and n == 8 and per % 2048 == 0 and p % 256 == 0
        and metric.shape[1] * n == na * p and virt <= min(p, per // 2) and ao <= (n - 3) * metric.shape[1]
        and virt % 128 == 0 and ao % 128 == 0 and n * per % virt == 0
    )


def any_shards(na, n, metric, amplitudes, virt_coef):
    if fits_cube(na, n, metric, amplitudes, virt_coef):
        return cube_shards(na, n, 8, metric, amplitudes, virt_coef)
    return shards(na, n, metric, amplitudes, virt_coef)


def solution(mesh):
    in_specs = (P("aux", "pair"), P("aux", "pair"), P())
    out_specs = (P("aux", "pair"), P(("aux", "pair"), None))
    body = functools.partial(any_shards, mesh.shape["aux"], mesh.shape["pair"])
    return jax.shard_map(body, mesh=mesh, in_specs=in_specs, out_specs=out_specs, check_vma=False)
```

```python
import functools

import jax
import jax.numpy as jnp
from jax import lax
from jax.experimental import pallas as pl
from jax.experimental.pallas import tpu as pltpu
from jax.sharding import PartitionSpec as P

MESH = pl.DeviceIdType.MESH


def kernel(
    na, n, count, metric, amp, virt_coef, density, fitted_ao,
    m_v, a_v, d_v, f_v, g_v, c_v, one_v, two_v, o_v,
    m_send, m_recv, z_send, z_recv, x_send, x_recv, one_send, one_recv, two_send, two_recv, o_sem, local_sem,
):
    a, b = lax.axis_index("aux"), lax.axis_index("pair")
    p, q = metric.shape
    per = amp.shape[1]
    w = per // count
    rows = p // n
    virt, ao = virt_coef.shape
    half = n // 2
    parity, chip = lax.rem(b, 2), b // 2
    partner = b + 1 - 2 * parity
    tile = min(256, p)
    tiles = p // tile

    barrier = pltpu.get_barrier_semaphore()
    for d in range(1, n):
        pl.semaphore_signal(barrier, inc=1, device_id=(a, lax.rem(b + d, n)), device_id_type=MESH)

    @pl.when(a > 0)
    def _():
        pl.semaphore_signal(barrier, inc=1, device_id=(a - 1, b), device_id_type=MESH)

    @pl.when(a < na - 1)
    def _():
        pl.semaphore_signal(barrier, inc=1, device_id=(a + 1, b), device_id_type=MESH)

    pl.semaphore_wait(barrier, n - 1 + jnp.where(a > 0, 1, 0) + jnp.where(a < na - 1, 1, 0))

    def block_of(s, c):
        return a_v.at[c, pl.ds(pl.multiple_of(s * p, p), p), :]

    def hop(src, s, c, way, target):
        return pltpu.make_async_remote_copy(
            src_ref=src, dst_ref=block_of(s, c), send_sem=z_send.at[way, s, c],
            recv_sem=z_recv.at[s, c], device_id=(target, b), device_id_type=MESH,
        )

    def metric_copy(owner, target):
        return pltpu.make_async_remote_copy(
            src_ref=metric, dst_ref=m_v.at[:, pl.ds(pl.multiple_of(owner * q, q), q)],
            send_sem=m_send.at[target], recv_sem=m_recv.at[owner],
            device_id=(a, target), device_id_type=MESH,
        )

    def regroup(owner, target, c):
        return pltpu.make_async_remote_copy(
            src_ref=f_v.at[c, pl.ds(pl.multiple_of(target * rows, rows), rows), :],
            dst_ref=g_v.at[:, pl.ds(pl.multiple_of(owner * per + c * w, w), w)],
            send_sem=x_send.at[target, c], recv_sem=x_recv.at[owner, c],
            device_id=(a, target), device_id_type=MESH,
        )

    def staged(j):
        return m_v.at[:, pl.ds(pl.multiple_of(j * q, q), q)]

    def first(j):
        return pltpu.make_async_remote_copy(
            src_ref=staged(j), dst_ref=one_v.at[j // 2], send_sem=one_send.at[j // 2],
            recv_sem=one_recv.at[j // 2], device_id=(a, partner), device_id_type=MESH,
        )

    def second(source, j):
        return pltpu.make_async_remote_copy(
            src_ref=staged(j), dst_ref=two_v.at[source], send_sem=two_send.at[0, j // 2],
            recv_sem=two_recv.at[0, source], device_id=(a, j), device_id_type=MESH,
        )

    def mine(c):
        return amp.at[:, c * w : (c + 1) * w]

    for c in range(count):
        @pl.when(a > 0)
        def _():
            hop(mine(c), a, c, 0, jnp.maximum(a - 1, 0)).start()

        @pl.when(a < na - 1)
        def _():
            hop(mine(c), a, c, 1, jnp.minimum(a + 1, na - 1)).start()

    @pl.loop(1, n)
    def _(d):
        metric_copy(b, lax.rem(b + d, n)).start()

    own_copies = [pltpu.make_async_copy(mine(c), block_of(a, c), local_sem.at[c]) for c in range(count)]
    own_copies.append(pltpu.make_async_copy(metric, staged(b), local_sem.at[count]))
    own_copies.append(pltpu.make_async_copy(virt_coef, c_v, local_sem.at[count + 1]))
    for copy in own_copies:
        copy.start()

    def arrive(t, c):
        @pl.when(a - t >= 0)
        def _():
            s = jnp.maximum(a - t, 0)
            hop(block_of(s, c), s, c, 1, a).wait_recv()

            @pl.when(a < na - 1)
            def _():
                hop(block_of(s, c), s, c, 1, jnp.minimum(a + 1, na - 1)).start()

        @pl.when(a + t < na)
        def _():
            s = jnp.minimum(a + t, na - 1)
            hop(block_of(s, c), s, c, 0, a).wait_recv()

            @pl.when(a > 0)
            def _():
                hop(block_of(s, c), s, c, 0, jnp.maximum(a - 1, 0)).start()

    @pl.loop(1, na - 1)
    def _(t):
        @pl.loop(0, count)
        def _(c):
            arrive(t, c)

    for copy in own_copies:
        copy.wait()

    @pl.loop(1, n)
    def _(d):
        metric_copy(lax.rem(b + n - d, n), b).wait_recv()

    @pl.loop(1, n)
    def _(d):
        metric_copy(b, lax.rem(b + d, n)).wait_send()

    def row(r):
        return pl.ds(pl.multiple_of(r * tile, tile), tile)

    def product(j, r, c):
        right = a_v[c, pl.ds(pl.multiple_of(j * q, q), q), :]
        return lax.dot_general(
            f_v[c, row(r), :], right, (((1,), (1,)), ((), ())), preferred_element_type=jnp.float32
        )

    def fit(c):
        @pl.loop(0, tiles)
        def _(r):
            f_v[c, row(r), :] = jnp.dot(
                m_v[row(r), :], a_v[c], preferred_element_type=jnp.float32
            ).astype(f_v.dtype)

        @pl.loop(1, n)
        def _(d):
            regroup(b, lax.rem(b + d, n), c).start()

        pltpu.make_async_copy(
            f_v.at[c, pl.ds(pl.multiple_of(b * rows, rows), rows), :],
            g_v.at[:, pl.ds(pl.multiple_of(b * per + c * w, w), w)], x_send.at[b, c],
        ).start()

    @pl.loop(0, n * tiles)
    def _(i):
        d_v[i // tiles, row(lax.rem(i, tiles)), :] = jnp.zeros((tile, q), jnp.float32)

    @pl.loop(0, count - 1)
    def _(c):
        arrive(na - 1, c)
        fit(c)

        @pl.loop(0, n * tiles)
        def _(i):
            j, r = i // tiles, lax.rem(i, tiles)
            d_v[j, row(r), :] += product(j, r, c)

    last = count - 1
    arrive(na - 1, last)
    fit(last)

    quad = half == 4
    mid = p // 2
    near = (chip + 1 - 2 * lax.rem(chip, 2), lax.rem(chip + 2, 4))
    far = 3 - chip

    def turn(h):
        if not quad:
            return lax.rem(chip + h, half)
        return jnp.where(h == 0, far, jnp.where(h == 1, near[0], jnp.where(h == 2, near[1], chip)))

    @pl.loop(0, half)
    def _(h):
        j = 2 * turn(h) + 1 - parity

        @pl.loop(0, tiles)
        def _(r):
            m_v[row(r), pl.ds(pl.multiple_of(j * q, q), q)] = (
                d_v[j, row(r), :] + product(j, r, last)
            ).astype(m_v.dtype)

        first(j).start()

    @pl.loop(0, 0 if quad else half)
    def _(h):
        j = 2 * lax.rem(chip + h, half) + parity

        @pl.loop(0, tiles)
        def _(r):
            d_v[j, row(r), :] += product(j, r, last)

    def part(way):
        return pl.ds(way * mid, mid)

    def cast(slot, way):
        j = 2 * slot + parity
        m_v[part(way), pl.ds(pl.multiple_of(j * q, q), q)] = d_v[j, part(way), :].astype(m_v.dtype)

    def piece(slot, way, place, target):
        j = 2 * slot + parity
        return pltpu.make_async_remote_copy(
            src_ref=m_v.at[part(way), pl.ds(pl.multiple_of(j * q, q), q)],
            dst_ref=two_v.at[place, part(way), :], send_sem=two_send.at[way, place],
            recv_sem=two_recv.at[way, place], device_id=(a, 2 * target + parity), device_id_type=MESH,
        )

    def add_in(slot, place, way):
        j = 2 * slot + parity
        d_v[j, part(way), :] += two_v[place, part(way), :].astype(jnp.float32)

    if quad:
        for h in range(4):
            slot = (far, near[0], near[1], chip)[h]

            @pl.loop(0, tiles)
            def _(r, slot=slot):
                d_v[2 * slot + parity, row(r), :] += product(2 * slot + parity, r, last)

            first(2 * slot + parity).wait_recv()

            @pl.loop(0, tiles)
            def _(r, slot=slot):
                j = 2 * slot + parity
                d_v[j, row(r), :] += one_v[slot, row(r), :].astype(jnp.float32)

            if h == 0:
                for way in range(2):
                    cast(far, way)
                    piece(far, way, 0, near[way]).start()
            elif h < 3:
                cast(near[h - 1], h - 1)
                piece(near[h - 1], h - 1, 1, near[h - 1]).start()
    else:
        @pl.loop(1, half)
        def _(h):
            slot = lax.rem(chip + h, half)
            j = 2 * slot + parity
            first(j).wait_recv()

            @pl.loop(0, tiles)
            def _(r):
                m_v[row(r), pl.ds(pl.multiple_of(j * q, q), q)] = (
                    d_v[j, row(r), :] + one_v[slot, row(r), :].astype(jnp.float32)
                ).astype(m_v.dtype)

            second(chip, j).start()

        first(b).wait_recv()

        @pl.loop(0, tiles)
        def _(r):
            d_v[b, row(r), :] += one_v[chip, row(r), :].astype(jnp.float32)

    if quad:
        for way in range(2):
            other = near[1 - way]
            piece(other, way, 0, near[way]).wait_recv()
            add_in(other, 0, way)
            cast(other, way)
            piece(other, way, 2, other).start()

    @pl.loop(0, count)
    def _(c):
        pltpu.make_async_copy(
            f_v.at[c, pl.ds(pl.multiple_of(b * rows, rows), rows), :],
            g_v.at[:, pl.ds(pl.multiple_of(b * per + c * w, w), w)], x_send.at[b, c],
        ).wait()

        @pl.loop(1, n)
        def _(d):
            regroup(lax.rem(b + n - d, n), b, c).wait_recv()

    occ = n * per // virt

    def out_copy(i, slot):
        return pltpu.make_async_copy(
            o_v.at[slot], fitted_ao.at[:, pl.ds(pl.multiple_of(i * ao, ao), ao)], o_sem.at[slot]
        )

    @pl.loop(0, occ)
    def _(i):
        slot = lax.rem(i, 2)

        @pl.when(i >= 2)
        def _():
            out_copy(i - 2, slot).wait()

        o_v[slot] = jnp.dot(
            g_v[:, pl.ds(pl.multiple_of(i * virt, virt), virt)], c_v[...], preferred_element_type=jnp.float32
        ).astype(o_v.dtype)
        out_copy(i, slot).start()

    for i in range(max(occ - 2, 0), occ):
        out_copy(i, i % 2).wait()

    if quad:
        for way in range(2):
            piece(chip, way, 1, near[way]).wait_recv()
            add_in(chip, 1, way)
        for way in range(2):
            piece(chip, way, 2, near[1 - way]).wait_recv()
            add_in(chip, 2, way)
    else:
        @pl.loop(1, half)
        def _(h):
            source = lax.rem(chip + half - h, half)
            second(source, b).wait_recv()

            @pl.loop(0, tiles)
            def _(r):
                d_v[b, row(r), :] += two_v[source, row(r), :].astype(jnp.float32)

    result = pltpu.make_async_copy(d_v.at[b], density, local_sem.at[0])
    result.start()

    @pl.loop(0, half)
    def _(h):
        first(2 * h + 1 - parity).wait_send()

    if quad:
        for way in range(2):
            piece(far, way, 0, near[way]).wait_send()
            piece(near[way], way, 1, near[way]).wait_send()
            piece(near[1 - way], way, 2, near[1 - way]).wait_send()
    else:
        @pl.loop(1, half)
        def _(h):
            second(chip, 2 * lax.rem(chip + h, half) + parity).wait_send()

    @pl.loop(0, count)
    def _(c):
        @pl.loop(1, n)
        def _(d):
            regroup(b, lax.rem(b + d, n), c).wait_send()

        @pl.loop(0, na)
        def _(s):
            @pl.when(jnp.logical_and(s >= a, a > 0))
            def _():
                hop(block_of(s, c), s, c, 0, jnp.maximum(a - 1, 0)).wait_send()

            @pl.when(jnp.logical_and(s <= a, a < na - 1))
            def _():
                hop(block_of(s, c), s, c, 1, jnp.minimum(a + 1, na - 1)).wait_send()

    result.wait()


def shards(na, n, metric, amplitudes, virt_coef):
    p, q = metric.shape
    per = amplitudes.shape[1]
    virt, ao = virt_coef.shape
    count = next(c for c in (8, 4, 2, 1) if per % (128 * c) == 0)
    w = per // count
    rows = p // n
    bf16 = jnp.bfloat16
    dma = pltpu.SemaphoreType.DMA
    return pl.pallas_call(
        functools.partial(kernel, na, n, count),
        out_shape=(
            jax.ShapeDtypeStruct((p, q), jnp.float32),
            jax.ShapeDtypeStruct((rows, n * per // virt * ao), bf16),
        ),
        in_specs=[pl.BlockSpec(memory_space=pl.ANY)] * 3,
        out_specs=(pl.BlockSpec(memory_space=pl.ANY), pl.BlockSpec(memory_space=pl.ANY)),
        scratch_shapes=[
            pltpu.VMEM((p, n * q), bf16),
            pltpu.VMEM((count, na * p, w), bf16),
            pltpu.VMEM((n, p, q), jnp.float32),
            pltpu.VMEM((count, p, w), bf16),
            pltpu.VMEM((rows, n * per), bf16),
            pltpu.VMEM((virt, ao), bf16),
            pltpu.VMEM((n // 2, p, q), bf16),
            pltpu.VMEM((n // 2, p, q), bf16),
            pltpu.VMEM((2, rows, ao), bf16),
            dma((n,)), dma((n,)),
            dma((2, na, count)), dma((na, count)),
            dma((n, count)), dma((n, count)),
            dma((n // 2,)), dma((n // 2,)),
            dma((2, n // 2)), dma((2, n // 2)),
            dma((2,)), dma((count + 2,)),
        ],
        compiler_params=pltpu.CompilerParams(
            collective_id=0, has_side_effects=True, vmem_limit_bytes=67043328
        ),
    )(metric, amplitudes, virt_coef)

def cube_kernel(
    na, n, count, ha, metric, amp, virt_coef, part_out, late_out, blocks_out, g_hbm,
    m_v, o_m, a_v, t_v, f_v, e_v, one_v, two_v,
    m_send, m_recv, z_send, z_recv, e_send, e_recv, x_send, x_recv,
    one_send, one_recv, two_send, two_recv, r_send, r_recv,
    mm_sem, fin_sem, far_sem, g_sem, local_sem,
):
    a, b = lax.axis_index("aux"), lax.axis_index("pair")
    p, q = metric.shape
    per = amp.shape[1]
    w = per // count
    rows = p // n
    virt, ao = virt_coef.shape
    parity, chip = lax.rem(b, 2), b // 2
    flip = 1 - 2 * parity
    partner = b + flip
    near = (chip + 1 - 2 * lax.rem(chip, 2), lax.rem(chip + 2, 4))
    far = 3 - chip
    xb, yb, fb = 2 * near[0] + parity, 2 * near[1] + parity, 2 * far + parity
    tile = 256 if p % 512 == 0 else 128
    tiles = p // tile
    mid = p // 2
    last = count - 1

    middle = jnp.logical_and(a > 0, a < na - 1)
    end = jnp.logical_not(middle)
    mate = a + 1 - 2 * lax.rem(a, 2)
    across = na - 1 - a
    beyond = na - 1 - mate

    barrier = pltpu.get_barrier_semaphore()
    for d in range(1, n):
        pl.semaphore_signal(barrier, inc=1, device_id=(a, lax.rem(b + d, n)), device_id_type=MESH)
    pl.semaphore_signal(barrier, inc=1, device_id=(mate, b), device_id_type=MESH)

    @pl.when(middle)
    def _():
        pl.semaphore_signal(barrier, inc=1, device_id=(across, b), device_id_type=MESH)

    pl.semaphore_wait(barrier, n + jnp.where(middle, 1, 0))

    v = w // 2

    def cols(c, base=0):
        return pl.ds(pl.multiple_of(base + c * w, w), w)

    def half(k, base=0):
        return pl.ds(pl.multiple_of(base + k * v, v), v)

    def row(r):
        return pl.ds(pl.multiple_of(r * tile, tile), tile)

    def part(way):
        return pl.ds(pl.multiple_of(way * mid, mid), mid)

    def wide(j):
        return pl.ds(pl.multiple_of(j * q, q), q)

    def block_of(s, k):
        return a_v.at[pl.ds(pl.multiple_of(s * p, p), p), half(k)]

    def z(s, k, way, own=False):
        return pltpu.make_async_remote_copy(
            src_ref=amp.at[:, half(k)] if own else block_of(s, k), dst_ref=block_of(s, k),
            send_sem=z_send.at[way, s, k], recv_sem=z_recv.at[s, k],
            device_id=(mate if way == 0 else across, b), device_id_type=MESH,
        )

    def own(way, *halves):
        for k in halves:
            z(a, k, way, True).start()

    def relay(s, k, way):
        z(s, k, way).wait_recv()
        z(s, k, way).start()

    def lend():
        return pltpu.make_async_remote_copy(
            src_ref=metric, dst_ref=o_m.at[:, wide(b)], send_sem=mm_sem.at[0], recv_sem=mm_sem.at[1],
            device_id=(mate, b), device_id_type=MESH,
        )

    def give(k):
        return pltpu.make_async_remote_copy(
            src_ref=e_v.at[:, half(k)], dst_ref=f_v.at[:, half(k)], send_sem=e_send.at[k], recv_sem=e_recv.at[k],
            device_id=(mate, b), device_id_type=MESH,
        )

    def staged(j):
        return o_m.at[:, wide(j)]

    def finish():
        return pltpu.make_async_remote_copy(
            src_ref=staged(b), dst_ref=two_v.at[0], send_sem=fin_sem.at[0], recv_sem=fin_sem.at[1],
            device_id=(mate, b), device_id_type=MESH,
        )

    def region(kind, mirror):
        mine = (b, b, b, xb, yb, xb, yb, fb, fb)
        theirs = (xb, yb, partner, fb, fb, xb + flip, yb + flip, fb + flip, fb + flip)
        side = (None, None, None, 0, 1, None, None, 0, 1)[kind]
        j = (theirs if mirror else mine)[kind]
        return (slice(None) if side is None else part(side), wide(j))

    def gather(g, kind, mirror=False):
        buf = (m_v, o_m)[g]
        where = region(kind, mirror)
        target = (xb, yb, partner, yb, xb, partner, partner, partner, partner)[kind]
        return pltpu.make_async_remote_copy(
            src_ref=metric if g == 0 and kind < 3 and not mirror else buf.at[where], dst_ref=buf.at[where],
            send_sem=m_send.at[g, kind], recv_sem=m_recv.at[g, kind],
            device_id=(a, target), device_id_type=MESH,
        )

    def got(g, kind):
        gather(g, kind, True).wait_recv()

    def gather_open(g):
        for kind in range(3):
            gather(g, kind).start()

    def gather_turn(g):
        got(g, 0)
        gather(g, 3).start()
        gather(g, 5).start()
        got(g, 1)
        gather(g, 4).start()
        gather(g, 6).start()

    def gather_close(g):
        got(g, 3)
        gather(g, 7).start()
        got(g, 4)
        gather(g, 8).start()
        for kind in (2, 5, 6, 7, 8):
            got(g, kind)
        for kind in range(9):
            gather(g, kind).wait_send()

    def regroup(owner, target, slot, where):
        return pltpu.make_async_remote_copy(
            src_ref=f_v.at[pl.ds(pl.multiple_of(target * rows, rows), rows), where()],
            dst_ref=g_hbm.at[:, where(owner * per)],
            send_sem=x_send.at[target, slot], recv_sem=x_recv.at[owner, slot],
            device_id=(a, target), device_id_type=MESH,
        )

    def keep(slot, where):
        return pltpu.make_async_copy(
            f_v.at[pl.ds(pl.multiple_of(b * rows, rows), rows), where()],
            g_hbm.at[:, where(b * per)], x_send.at[b, slot],
        )

    def regroup_all(slot, where):
        @pl.loop(1, n)
        def _(d):
            regroup(b, lax.rem(b + d, n), slot, where).start()

        keep(slot, where).start()

    def each_piece(act):
        @pl.loop(0, last)
        def _(c):
            act(c, functools.partial(cols, c))

        for k in (2 * last, 2 * last + 1):
            act(k - last, functools.partial(half, k))

    def fit(mat, dst, where):
        @pl.loop(0, tiles)
        def _(r):
            dst[row(r), where] = jnp.dot(
                mat[row(r), :], a_v[:, where], preferred_element_type=jnp.float32
            ).astype(dst.dtype)

    def product(left, j, r, span):
        return lax.dot_general(
            left[row(r), span], a_v[wide(j), span], (((1,), (1,)), ((), ())), preferred_element_type=jnp.float32
        )

    early, rest, whole = slice(0, ha * w), slice(ha * w, per), slice(0, per)
    most = slice(ha * w, per - v)

    def first(turn, j):
        return pltpu.make_async_remote_copy(
            src_ref=staged(j), dst_ref=one_v.at[turn, j // 2], send_sem=one_send.at[turn, j // 2],
            recv_sem=one_recv.at[turn, j // 2], device_id=(a, partner), device_id_type=MESH,
        )

    def early_piece(target, way, place):
        return pltpu.make_async_remote_copy(
            src_ref=o_m.at[part(way), wide((xb, yb, fb)[target])], dst_ref=two_v.at[place, part(way), :],
            send_sem=r_send.at[way, place], recv_sem=r_recv.at[way, place],
            device_id=(a, (xb, yb)[target if place else way]), device_id_type=MESH,
        )

    own_copies = [
        pltpu.make_async_copy(amp, a_v.at[pl.ds(pl.multiple_of(a * p, p), p), :], local_sem.at[0]),
        pltpu.make_async_copy(metric, m_v.at[:, wide(b)], local_sem.at[1]),
    ]

    @pl.when(end)
    def _():
        lend().start()
        gather_open(0)
        own(0, *range(2 * count))

    @pl.when(middle)
    def _():
        own(1, 2 * ha, 2 * ha + 1)
        own(0, 2 * ha, 2 * ha + 1)
        gather_open(0)
        own(1, 2 * ha + 2, 2 * ha + 3, 0, 1)
        own(0, *range(2 * ha + 2, 2 * count))

    for copy in own_copies:
        copy.start()

    @pl.when(end)
    def _():
        gather_turn(0)
        gather_close(0)

    @pl.when(middle)
    def _():
        lend().wait_recv()
        gather_open(1)
        for k in range(2 * ha, 2 * ha + 4):
            relay(across, k, 0)
        relay(mate, 0, 1)
        relay(mate, 1, 1)
        own(1, 2, 3)
        gather_turn(1)
        relay(mate, 2, 1)
        relay(mate, 3, 1)
        own(1, 4, 5)
        gather_turn(0)
        relay(mate, 4, 1)
        relay(mate, 5, 1)
        own(1, 6)
        gather_close(1)

    for copy in own_copies:
        copy.wait()

    def first_share(low, high):
        @pl.loop(low, high)
        def _(h):
            j = 2 * h + 1 - parity

            @pl.loop(0, tiles)
            def _(r):
                o_m[row(r), wide(j)] = product(e_v, j, r, early).astype(o_m.dtype)

            first(0, j).start()

    def first_total(j, r):
        return product(e_v, j, r, early) + one_v[0, j // 2, row(r), :].astype(jnp.float32)

    def second_share(target):
        j = (xb, yb, fb)[target]
        first(0, j).wait_recv()

        @pl.loop(0, tiles)
        def _(r):
            o_m[row(r), wide(j)] = first_total(j, r).astype(o_m.dtype)

        if target == 2:
            early_piece(2, 0, 0).start()
            early_piece(2, 1, 0).start()
        else:
            early_piece(target, target, 1).start()

    def third_share():
        for way in range(2):
            other = 1 - way
            early_piece(2, way, 0).wait_recv()

            @pl.loop(way * tiles // 2, (way + 1) * tiles // 2)
            def _(r, j=(xb, yb)[other]):
                total = first_total(j, r) + two_v[0, row(r), :].astype(jnp.float32)
                o_m[row(r), wide(j)] = total.astype(o_m.dtype)

            early_piece(other, way, 2).start()

    def fourth_share():
        first(0, b).wait_recv()
        for way in range(2):
            early_piece(way, way, 1).wait_recv()
            early_piece(1 - way, way, 2).wait_recv()

        @pl.loop(0, tiles)
        def _(r):
            total = first_total(b, r)
            for place in (1, 2):
                total += two_v[place, row(r), :].astype(jnp.float32)
            o_m[row(r), wide(b)] = total.astype(o_m.dtype)

        for way in range(2):
            early_piece(2, way, 0).wait_send()
            early_piece(way, way, 1).wait_send()
            early_piece(1 - way, way, 2).wait_send()

    @pl.loop(0, ha - 1)
    def _(c):
        @pl.when(middle)
        def _():
            for k in (2 * c, 2 * c + 1):
                z(across, k, 0).wait_recv()
                z(beyond, k, 0).wait_recv()
            fit(o_m, e_v, cols(c))
            give(2 * c).start()
            give(2 * c + 1).start()
            relay(mate, 2 * c + 6, 1)

            @pl.when(c == 0)
            def _():
                own(1, 7)

            relay(mate, 2 * c + 7, 1)

            @pl.when(c == 2)
            def _():
                own(1, 12, 13)

            @pl.when(c == 0)
            def _():
                gather_close(0)

            fit(m_v, f_v, cols(c))

        @pl.when(end)
        def _():
            give(2 * c).wait_recv()
            give(2 * c + 1).wait_recv()

        regroup_all(c, functools.partial(cols, c))

    @pl.when(middle)
    def _():
        @pl.loop(6, 8)
        def _(k):
            z(across, k, 0).wait_recv()
            z(beyond, k, 0).wait_recv()
            fit(o_m, e_v, half(k))
            give(k).start()

            @pl.when(k == 6)
            def _():
                relay(mate, 12, 1)
                relay(mate, 13, 1)
                own(1, 14)

        relay(mate, 14, 1)
        own(1, 15)
        relay(mate, 15, 1)
        fit(m_v, f_v, cols(ha - 1))

    @pl.when(end)
    def _():
        give(6).wait_recv()
        give(7).wait_recv()

    regroup_all(ha - 1, functools.partial(cols, ha - 1))

    def all_in(k):
        for source in (mate, across, beyond):
            z(source, k, 0).wait_recv()

    @pl.loop(ha, last)
    def _(c):
        @pl.when(jnp.logical_and(middle, c == ha))
        def _():
            relay(beyond, 2 * ha, 0)
            first_share(0, 2)
            relay(beyond, 2 * ha + 1, 0)
            first_share(2, n // 2)
            relay(beyond, 2 * ha + 2, 0)

        @pl.when(jnp.logical_and(middle, c == ha + 1))
        def _():
            relay(beyond, 2 * ha + 3, 0)
            second_share(2)

        @pl.when(jnp.logical_and(middle, c == last - 1))
        def _():
            relay(across, 2 * last - 2, 0)
            second_share(0)
            relay(across, 2 * last - 1, 0)
            second_share(1)
            relay(beyond, 2 * last - 2, 0)
            relay(beyond, 2 * last - 1, 0)
            third_share()

        @pl.when(end)
        def _():
            all_in(2 * c)
            all_in(2 * c + 1)

        fit(m_v, f_v, cols(c))
        regroup_all(c, functools.partial(cols, c))

    for k in (2 * last, 2 * last + 1):
        @pl.when(middle)
        def _():
            relay(across, k, 0)
            relay(beyond, k, 0)

        @pl.when(end)
        def _():
            all_in(k)

        if k == 2 * last:
            fit(m_v, f_v, half(k))
            regroup_all(k - last, functools.partial(half, k))

            @pl.when(end)
            def _():
                for at, j in enumerate((2 * far + 1 - parity, 2 * far + parity)):
                    @pl.loop(0, tiles)
                    def _(r, at=at, j=j):
                        (part_out, t_v)[at][row(r), :] = product(f_v, j, r, most)

    @pl.when(middle)
    def _():
        @pl.loop(0, n // 2)
        def _(h):
            first(0, 2 * h + 1 - parity).wait_send()

    def by_role(act, low=0, high=tiles):
        for role, span in ((middle, whole), (end, rest)):
            @pl.when(role)
            def _():
                @pl.loop(low, high)
                def _(r):
                    act(r, span)

    def for_partner(slot):
        j = 2 * slot + 1 - parity

        def act(r, span):
            o_m[row(r), wide(j)] = product(f_v, j, r, span).astype(o_m.dtype)

        by_role(act)
        first(1, j).start()

    final = slice(per - v, per)

    def far_total(at, r, span):
        j = 2 * far + (parity if at else 1 - parity)
        if span is whole:
            return product(f_v, j, r, whole)
        return (part_out, t_v)[at][row(r), :] + product(f_v, j, r, final)

    def far_first(way):
        return pltpu.make_async_remote_copy(
            src_ref=o_m.at[part(way), wide(2 * far + 1 - parity)], dst_ref=one_v.at[1, far, part(way), :],
            send_sem=far_sem.at[0, way], recv_sem=far_sem.at[1, way],
            device_id=(a, partner), device_id_type=MESH,
        )

    @pl.loop(0, 2)
    def _(way):
        low, high = way * (tiles // 2), (way + 1) * (tiles // 2)

        @pl.loop(low, high)
        def _(r):
            f_v[row(r), final] = jnp.dot(
                m_v[row(r), :], a_v[:, final], preferred_element_type=jnp.float32
            ).astype(f_v.dtype)

        def act(r, span):
            o_m[row(r), wide(2 * far + 1 - parity)] = far_total(0, r, span).astype(o_m.dtype)

        by_role(act, low, high)
        far_first(way).start()

    regroup_all(last + 1, functools.partial(half, 2 * last + 1))

    spare = n * q - 3 * q

    def sent(at):
        return pl.ds(spare + at * q, q)

    def piece(place_of, way, place, target):
        return pltpu.make_async_remote_copy(
            src_ref=m_v.at[part(way), sent(place_of)],
            dst_ref=two_v.at[3, part(way), :] if place == 0 else late_out.at[place - 1, part(way), :],
            send_sem=two_send.at[way, place], recv_sem=two_recv.at[way, place],
            device_id=(a, 2 * target + parity), device_id_type=MESH,
        )

    def turn(h):
        return jnp.where(h == 0, far, jnp.where(h == 1, near[0], jnp.where(h == 2, near[1], chip)))

    @pl.loop(0, 2)
    def _(way):
        far_first(way).wait_recv()

        def act(r, span):
            total = far_total(1, r, span) + one_v[1, far, row(r), :].astype(jnp.float32)
            m_v[row(r), sent(0)] = total.astype(m_v.dtype)

        by_role(act, way * (tiles // 2), (way + 1) * (tiles // 2))
        piece(0, way, 0, jnp.where(way == 0, near[0], near[1])).start()

    @pl.when(middle)
    def _():
        fourth_share()
        finish().start()

    @pl.loop(1, n // 2)
    def _(h):
        for_partner(turn(h))

    @pl.loop(1, n // 2)
    def _(h):
        slot = turn(h)
        j = 2 * slot + parity
        first(1, j).wait_recv()

        def act(r, span):
            total = product(f_v, j, r, span) + one_v[1, slot, row(r), :].astype(jnp.float32)
            for at in (1, 2):
                @pl.when(h == at)
                def _():
                    m_v[row(r), sent(at)] = total.astype(m_v.dtype)

                @pl.when(jnp.logical_and(h == at, r >= tiles // 2 if at == 1 else r < tiles // 2))
                def _():
                    t_v[row(r), :] = total

            @pl.when(h == 3)
            def _():
                part_out[row(r), :] = total

        by_role(act)

        for way in range(2):
            @pl.when(h == 1 + way)
            def _():
                piece(1 + way, way, 1, near[way]).start()

    for way in range(2):
        at = 1 - way
        piece(0, way, 0, near[way]).wait_recv()
        m_v[part(way), sent(1 + at)] = (t_v[part(way), :] + two_v[3, part(way), :].astype(jnp.float32)).astype(m_v.dtype)
        piece(1 + at, way, 2, near[at]).start()

    coef = m_v.at[pl.ds(0, virt), pl.ds(0, ao)]
    load_coef = pltpu.make_async_copy(virt_coef, coef, local_sem.at[0])
    load_coef.start()

    def regrouped(slot, where):
        keep(slot, where).wait()

        @pl.loop(1, n)
        def _(d):
            regroup(lax.rem(b + n - d, n), b, slot, where).wait_recv()

    each_piece(regrouped)

    occ = n * per // virt

    def slot_rows(slot):
        return pl.ds(pl.multiple_of(slot * rows, rows), rows)

    def block_copy(i, slot):
        return pltpu.make_async_copy(
            g_hbm.at[:, pl.ds(pl.multiple_of(i * virt, virt), virt)],
            e_v.at[slot_rows(slot), pl.ds(0, virt)], g_sem.at[slot],
        )

    @pl.when(middle)
    def _():
        @pl.loop(0, 2 * ha)
        def _(k):
            give(k).wait_send()

    block_copy(0, 0).start()
    load_coef.wait()

    @pl.loop(0, occ)
    def _(i):
        slot = lax.rem(i, 2)

        @pl.when(i + 1 < occ)
        def _():
            block_copy(i + 1, 1 - slot).start()

        block_copy(i, slot).wait()
        blocks_out[:, pl.ds(pl.multiple_of(i * ao, ao), ao)] = jnp.dot(
            e_v[slot_rows(slot), pl.ds(0, virt)], m_v[pl.ds(0, virt), pl.ds(0, ao)],
            preferred_element_type=jnp.float32,
        ).astype(blocks_out.dtype)

    @pl.when(end)
    def _():
        finish().wait_recv()

        @pl.loop(0, tiles)
        def _(r):
            part_out[row(r), :] += two_v[0, row(r), :].astype(jnp.float32)

    @pl.loop(1, n // 2)
    def _(h):
        first(1, 2 * turn(h) + 1 - parity).wait_send()

    for way in range(2):
        far_first(way).wait_send()

    for way in range(2):
        piece(0, way, 0, near[way]).wait_send()
        piece(1, way, 1, near[way]).wait_send()

    def regroup_sent(slot, where):
        @pl.loop(1, n)
        def _(d):
            regroup(b, lax.rem(b + d, n), slot, where).wait_send()

    each_piece(regroup_sent)

    @pl.when(end)
    def _():
        lend().wait_send()

        @pl.loop(0, 2 * count)
        def _(k):
            z(a, k, 0).wait_send()

    @pl.when(middle)
    def _():
        finish().wait_send()

        @pl.loop(0, 2 * count)
        def _(k):
            z(a, k, 1).wait_send()
            z(mate, k, 1).wait_send()

        @pl.loop(2 * ha, 2 * count)
        def _(k):
            z(a, k, 0).wait_send()
            z(across, k, 0).wait_send()
            z(beyond, k, 0).wait_send()

    for way in range(2):
        piece(1, way, 1, near[way]).wait_recv()
        piece(1, way, 2, near[1 - way]).wait_recv()
        piece(1, way, 2, near[1 - way]).wait_send()


def close_kernel(part, late, ao_in, density, ao_out, sum_v, copy_sem, out_sem):
    cuts, steps = copy_sem.shape[0], out_sem.shape[0]
    span, size = ao_in.shape[1] // cuts, part.shape[0] // steps
    writes = []
    for k in range(cuts):
        held = slice(k * span, (k + 1) * span)
        writes.append(pltpu.make_async_copy(ao_in.at[:, held], ao_out.at[:, held], copy_sem.at[k]))
    for copy in writes[: cuts // 2]:
        copy.start()
    for k in range(steps):
        where = pl.ds(k * size, size)
        sum_v[where, :] = (
            part[where, :] + late[0, where, :].astype(jnp.float32) + late[1, where, :].astype(jnp.float32)
        )
        store = pltpu.make_async_copy(sum_v.at[where, :], density.at[where, :], out_sem.at[k])
        store.start()
        writes.append(store)
    for copy in writes[cuts // 2 : cuts]:
        copy.start()
    for copy in writes:
        copy.wait()


def cube_shards(na, n, count, metric, amplitudes, virt_coef):
    p, q = metric.shape
    per = amplitudes.shape[1]
    virt, ao = virt_coef.shape
    ha = count // 2
    rows = p // n
    bf16 = jnp.bfloat16
    dma = pltpu.SemaphoreType.DMA
    part, late, blocks, _ = pl.pallas_call(
        functools.partial(cube_kernel, na, n, count, ha),
        out_shape=(
            pltpu.VMEM((p, q), jnp.float32),
            pltpu.VMEM((2, p, q), bf16),
            pltpu.VMEM((rows, n * per // virt * ao), bf16),
            jax.ShapeDtypeStruct((rows, n * per), bf16),
        ),
        in_specs=[pl.BlockSpec(memory_space=pl.ANY)] * 3,
        out_specs=(pl.BlockSpec(memory_space=pltpu.VMEM),) * 3 + (pl.BlockSpec(memory_space=pl.ANY),),
        scratch_shapes=[
            pltpu.VMEM((p, n * q), bf16),
            pltpu.VMEM((p, n * q), bf16),
            pltpu.VMEM((na * p, per), bf16),
            pltpu.VMEM((p, q), jnp.float32),
            pltpu.VMEM((p, per), bf16),
            pltpu.VMEM((p, per * ha // count), bf16),
            pltpu.VMEM((2, n // 2, p, q), bf16),
            pltpu.VMEM((4, p, q), bf16),
            dma((2, 9)), dma((2, 9)),
            dma((2, na, 2 * count)), dma((na, 2 * count)),
            dma((2 * ha,)), dma((2 * ha,)),
            dma((n, count + 1)), dma((n, count + 1)),
            dma((2, n // 2)), dma((2, n // 2)),
            dma((2, 3)), dma((2, 3)),
            dma((2, 3)), dma((2, 3)),
            dma((2,)), dma((2,)), dma((2, 2)), dma((2,)), dma((2,)),
        ],
        compiler_params=pltpu.CompilerParams(
            collective_id=0, has_side_effects=True, vmem_limit_bytes=54 * 2**20
        ),
    )(metric, amplitudes, virt_coef)
    return pl.pallas_call(
        close_kernel,
        out_shape=(jax.ShapeDtypeStruct(part.shape, part.dtype), jax.ShapeDtypeStruct(blocks.shape, bf16)),
        in_specs=[pl.BlockSpec(memory_space=pltpu.VMEM)] * 3,
        out_specs=(pl.BlockSpec(memory_space=pl.ANY),) * 2,
        scratch_shapes=[
            pltpu.VMEM((p, q), jnp.float32), dma((4,)), dma((4,)),
        ],
        compiler_params=pltpu.CompilerParams(vmem_limit_bytes=8 * 2**20),
    )(part, late, blocks)


def fits_cube(na, n, metric, amplitudes, virt_coef):
    p, per, (virt, ao) = metric.shape[0], amplitudes.shape[1], virt_coef.shape
    return (
        na == 4 and n == 8 and per % 2048 == 0 and p % 256 == 0
        and metric.shape[1] * n == na * p and virt <= min(p, per // 2) and ao <= (n - 3) * metric.shape[1]
        and virt % 128 == 0 and ao % 128 == 0 and n * per % virt == 0
    )


def any_shards(na, n, metric, amplitudes, virt_coef):
    if fits_cube(na, n, metric, amplitudes, virt_coef):
        return cube_shards(na, n, 8, metric, amplitudes, virt_coef)
    return shards(na, n, metric, amplitudes, virt_coef)


def solution(mesh):
    in_specs = (P("aux", "pair"), P("aux", "pair"), P())
    out_specs = (P("aux", "pair"), P(("aux", "pair"), None))
    body = functools.partial(any_shards, mesh.shape["aux"], mesh.shape["pair"])
    return jax.shard_map(body, mesh=mesh, in_specs=in_specs, out_specs=out_specs, check_vma=False)
```

```python
import functools

import jax
import jax.numpy as jnp
from jax import lax
from jax.experimental import pallas as pl
from jax.experimental.pallas import tpu as pltpu
from jax.sharding import PartitionSpec as P

MESH = pl.DeviceIdType.MESH


def kernel(
    na, n, count, metric, amp, virt_coef, density, fitted_ao,
    m_v, a_v, d_v, f_v, g_v, c_v, one_v, two_v, o_v,
    m_send, m_recv, z_send, z_recv, x_send, x_recv, one_send, one_recv, two_send, two_recv, o_sem, local_sem,
):
    a, b = lax.axis_index("aux"), lax.axis_index("pair")
    p, q = metric.shape
    per = amp.shape[1]
    w = per // count
    rows = p // n
    virt, ao = virt_coef.shape
    half = n // 2
    parity, chip = lax.rem(b, 2), b // 2
    partner = b + 1 - 2 * parity
    tile = min(256, p)
    tiles = p // tile

    barrier = pltpu.get_barrier_semaphore()
    for d in range(1, n):
        pl.semaphore_signal(barrier, inc=1, device_id=(a, lax.rem(b + d, n)), device_id_type=MESH)

    @pl.when(a > 0)
    def _():
        pl.semaphore_signal(barrier, inc=1, device_id=(a - 1, b), device_id_type=MESH)

    @pl.when(a < na - 1)
    def _():
        pl.semaphore_signal(barrier, inc=1, device_id=(a + 1, b), device_id_type=MESH)

    pl.semaphore_wait(barrier, n - 1 + jnp.where(a > 0, 1, 0) + jnp.where(a < na - 1, 1, 0))

    def block_of(s, c):
        return a_v.at[c, pl.ds(pl.multiple_of(s * p, p), p), :]

    def hop(src, s, c, way, target):
        return pltpu.make_async_remote_copy(
            src_ref=src, dst_ref=block_of(s, c), send_sem=z_send.at[way, s, c],
            recv_sem=z_recv.at[s, c], device_id=(target, b), device_id_type=MESH,
        )

    def metric_copy(owner, target):
        return pltpu.make_async_remote_copy(
            src_ref=metric, dst_ref=m_v.at[:, pl.ds(pl.multiple_of(owner * q, q), q)],
            send_sem=m_send.at[target], recv_sem=m_recv.at[owner],
            device_id=(a, target), device_id_type=MESH,
        )

    def regroup(owner, target, c):
        return pltpu.make_async_remote_copy(
            src_ref=f_v.at[c, pl.ds(pl.multiple_of(target * rows, rows), rows), :],
            dst_ref=g_v.at[:, pl.ds(pl.multiple_of(owner * per + c * w, w), w)],
            send_sem=x_send.at[target, c], recv_sem=x_recv.at[owner, c],
            device_id=(a, target), device_id_type=MESH,
        )

    def staged(j):
        return m_v.at[:, pl.ds(pl.multiple_of(j * q, q), q)]

    def first(j):
        return pltpu.make_async_remote_copy(
            src_ref=staged(j), dst_ref=one_v.at[j // 2], send_sem=one_send.at[j // 2],
            recv_sem=one_recv.at[j // 2], device_id=(a, partner), device_id_type=MESH,
        )

    def second(source, j):
        return pltpu.make_async_remote_copy(
            src_ref=staged(j), dst_ref=two_v.at[source], send_sem=two_send.at[0, j // 2],
            recv_sem=two_recv.at[0, source], device_id=(a, j), device_id_type=MESH,
        )

    def mine(c):
        return amp.at[:, c * w : (c + 1) * w]

    for c in range(count):
        @pl.when(a > 0)
        def _():
            hop(mine(c), a, c, 0, jnp.maximum(a - 1, 0)).start()

        @pl.when(a < na - 1)
        def _():
            hop(mine(c), a, c, 1, jnp.minimum(a + 1, na - 1)).start()

    @pl.loop(1, n)
    def _(d):
        metric_copy(b, lax.rem(b + d, n)).start()

    own_copies = [pltpu.make_async_copy(mine(c), block_of(a, c), local_sem.at[c]) for c in range(count)]
    own_copies.append(pltpu.make_async_copy(metric, staged(b), local_sem.at[count]))
    own_copies.append(pltpu.make_async_copy(virt_coef, c_v, local_sem.at[count + 1]))
    for copy in own_copies:
        copy.start()

    def arrive(t, c):
        @pl.when(a - t >= 0)
        def _():
            s = jnp.maximum(a - t, 0)
            hop(block_of(s, c), s, c, 1, a).wait_recv()

            @pl.when(a < na - 1)
            def _():
                hop(block_of(s, c), s, c, 1, jnp.minimum(a + 1, na - 1)).start()

        @pl.when(a + t < na)
        def _():
            s = jnp.minimum(a + t, na - 1)
            hop(block_of(s, c), s, c, 0, a).wait_recv()

            @pl.when(a > 0)
            def _():
                hop(block_of(s, c), s, c, 0, jnp.maximum(a - 1, 0)).start()

    @pl.loop(1, na - 1)
    def _(t):
        @pl.loop(0, count)
        def _(c):
            arrive(t, c)

    for copy in own_copies:
        copy.wait()

    @pl.loop(1, n)
    def _(d):
        metric_copy(lax.rem(b + n - d, n), b).wait_recv()

    @pl.loop(1, n)
    def _(d):
        metric_copy(b, lax.rem(b + d, n)).wait_send()

    def row(r):
        return pl.ds(pl.multiple_of(r * tile, tile), tile)

    def product(j, r, c):
        right = a_v[c, pl.ds(pl.multiple_of(j * q, q), q), :]
        return lax.dot_general(
            f_v[c, row(r), :], right, (((1,), (1,)), ((), ())), preferred_element_type=jnp.float32
        )

    def fit(c):
        @pl.loop(0, tiles)
        def _(r):
            f_v[c, row(r), :] = jnp.dot(
                m_v[row(r), :], a_v[c], preferred_element_type=jnp.float32
            ).astype(f_v.dtype)

        @pl.loop(1, n)
        def _(d):
            regroup(b, lax.rem(b + d, n), c).start()

        pltpu.make_async_copy(
            f_v.at[c, pl.ds(pl.multiple_of(b * rows, rows), rows), :],
            g_v.at[:, pl.ds(pl.multiple_of(b * per + c * w, w), w)], x_send.at[b, c],
        ).start()

    @pl.loop(0, n * tiles)
    def _(i):
        d_v[i // tiles, row(lax.rem(i, tiles)), :] = jnp.zeros((tile, q), jnp.float32)

    @pl.loop(0, count - 1)
    def _(c):
        arrive(na - 1, c)
        fit(c)

        @pl.loop(0, n * tiles)
        def _(i):
            j, r = i // tiles, lax.rem(i, tiles)
            d_v[j, row(r), :] += product(j, r, c)

    last = count - 1
    arrive(na - 1, last)
    fit(last)

    quad = half == 4
    mid = p // 2
    near = (chip + 1 - 2 * lax.rem(chip, 2), lax.rem(chip + 2, 4))
    far = 3 - chip

    def turn(h):
        if not quad:
            return lax.rem(chip + h, half)
        return jnp.where(h == 0, far, jnp.where(h == 1, near[0], jnp.where(h == 2, near[1], chip)))

    @pl.loop(0, half)
    def _(h):
        j = 2 * turn(h) + 1 - parity

        @pl.loop(0, tiles)
        def _(r):
            m_v[row(r), pl.ds(pl.multiple_of(j * q, q), q)] = (
                d_v[j, row(r), :] + product(j, r, last)
            ).astype(m_v.dtype)

        first(j).start()

    @pl.loop(0, 0 if quad else half)
    def _(h):
        j = 2 * lax.rem(chip + h, half) + parity

        @pl.loop(0, tiles)
        def _(r):
            d_v[j, row(r), :] += product(j, r, last)

    def part(way):
        return pl.ds(way * mid, mid)

    def cast(slot, way):
        j = 2 * slot + parity
        m_v[part(way), pl.ds(pl.multiple_of(j * q, q), q)] = d_v[j, part(way), :].astype(m_v.dtype)

    def piece(slot, way, place, target):
        j = 2 * slot + parity
        return pltpu.make_async_remote_copy(
            src_ref=m_v.at[part(way), pl.ds(pl.multiple_of(j * q, q), q)],
            dst_ref=two_v.at[place, part(way), :], send_sem=two_send.at[way, place],
            recv_sem=two_recv.at[way, place], device_id=(a, 2 * target + parity), device_id_type=MESH,
        )

    def add_in(slot, place, way):
        j = 2 * slot + parity
        d_v[j, part(way), :] += two_v[place, part(way), :].astype(jnp.float32)

    if quad:
        for h in range(4):
            slot = (far, near[0], near[1], chip)[h]

            @pl.loop(0, tiles)
            def _(r, slot=slot):
                d_v[2 * slot + parity, row(r), :] += product(2 * slot + parity, r, last)

            first(2 * slot + parity).wait_recv()

            @pl.loop(0, tiles)
            def _(r, slot=slot):
                j = 2 * slot + parity
                d_v[j, row(r), :] += one_v[slot, row(r), :].astype(jnp.float32)

            if h == 0:
                for way in range(2):
                    cast(far, way)
                    piece(far, way, 0, near[way]).start()
            elif h < 3:
                cast(near[h - 1], h - 1)
                piece(near[h - 1], h - 1, 1, near[h - 1]).start()
    else:
        @pl.loop(1, half)
        def _(h):
            slot = lax.rem(chip + h, half)
            j = 2 * slot + parity
            first(j).wait_recv()

            @pl.loop(0, tiles)
            def _(r):
                m_v[row(r), pl.ds(pl.multiple_of(j * q, q), q)] = (
                    d_v[j, row(r), :] + one_v[slot, row(r), :].astype(jnp.float32)
                ).astype(m_v.dtype)

            second(chip, j).start()

        first(b).wait_recv()

        @pl.loop(0, tiles)
        def _(r):
            d_v[b, row(r), :] += one_v[chip, row(r), :].astype(jnp.float32)

    if quad:
        for way in range(2):
            other = near[1 - way]
            piece(other, way, 0, near[way]).wait_recv()
            add_in(other, 0, way)
            cast(other, way)
            piece(other, way, 2, other).start()

    @pl.loop(0, count)
    def _(c):
        pltpu.make_async_copy(
            f_v.at[c, pl.ds(pl.multiple_of(b * rows, rows), rows), :],
            g_v.at[:, pl.ds(pl.multiple_of(b * per + c * w, w), w)], x_send.at[b, c],
        ).wait()

        @pl.loop(1, n)
        def _(d):
            regroup(lax.rem(b + n - d, n), b, c).wait_recv()

    occ = n * per // virt

    def out_copy(i, slot):
        return pltpu.make_async_copy(
            o_v.at[slot], fitted_ao.at[:, pl.ds(pl.multiple_of(i * ao, ao), ao)], o_sem.at[slot]
        )

    @pl.loop(0, occ)
    def _(i):
        slot = lax.rem(i, 2)

        @pl.when(i >= 2)
        def _():
            out_copy(i - 2, slot).wait()

        o_v[slot] = jnp.dot(
            g_v[:, pl.ds(pl.multiple_of(i * virt, virt), virt)], c_v[...], preferred_element_type=jnp.float32
        ).astype(o_v.dtype)
        out_copy(i, slot).start()

    for i in range(max(occ - 2, 0), occ):
        out_copy(i, i % 2).wait()

    if quad:
        for way in range(2):
            piece(chip, way, 1, near[way]).wait_recv()
            add_in(chip, 1, way)
        for way in range(2):
            piece(chip, way, 2, near[1 - way]).wait_recv()
            add_in(chip, 2, way)
    else:
        @pl.loop(1, half)
        def _(h):
            source = lax.rem(chip + half - h, half)
            second(source, b).wait_recv()

            @pl.loop(0, tiles)
            def _(r):
                d_v[b, row(r), :] += two_v[source, row(r), :].astype(jnp.float32)

    result = pltpu.make_async_copy(d_v.at[b], density, local_sem.at[0])
    result.start()

    @pl.loop(0, half)
    def _(h):
        first(2 * h + 1 - parity).wait_send()

    if quad:
        for way in range(2):
            piece(far, way, 0, near[way]).wait_send()
            piece(near[way], way, 1, near[way]).wait_send()
            piece(near[1 - way], way, 2, near[1 - way]).wait_send()
    else:
        @pl.loop(1, half)
        def _(h):
            second(chip, 2 * lax.rem(chip + h, half) + parity).wait_send()

    @pl.loop(0, count)
    def _(c):
        @pl.loop(1, n)
        def _(d):
            regroup(b, lax.rem(b + d, n), c).wait_send()

        @pl.loop(0, na)
        def _(s):
            @pl.when(jnp.logical_and(s >= a, a > 0))
            def _():
                hop(block_of(s, c), s, c, 0, jnp.maximum(a - 1, 0)).wait_send()

            @pl.when(jnp.logical_and(s <= a, a < na - 1))
            def _():
                hop(block_of(s, c), s, c, 1, jnp.minimum(a + 1, na - 1)).wait_send()

    result.wait()


def shards(na, n, metric, amplitudes, virt_coef):
    p, q = metric.shape
    per = amplitudes.shape[1]
    virt, ao = virt_coef.shape
    count = next(c for c in (8, 4, 2, 1) if per % (128 * c) == 0)
    w = per // count
    rows = p // n
    bf16 = jnp.bfloat16
    dma = pltpu.SemaphoreType.DMA
    return pl.pallas_call(
        functools.partial(kernel, na, n, count),
        out_shape=(
            jax.ShapeDtypeStruct((p, q), jnp.float32),
            jax.ShapeDtypeStruct((rows, n * per // virt * ao), bf16),
        ),
        in_specs=[pl.BlockSpec(memory_space=pl.ANY)] * 3,
        out_specs=(pl.BlockSpec(memory_space=pl.ANY), pl.BlockSpec(memory_space=pl.ANY)),
        scratch_shapes=[
            pltpu.VMEM((p, n * q), bf16),
            pltpu.VMEM((count, na * p, w), bf16),
            pltpu.VMEM((n, p, q), jnp.float32),
            pltpu.VMEM((count, p, w), bf16),
            pltpu.VMEM((rows, n * per), bf16),
            pltpu.VMEM((virt, ao), bf16),
            pltpu.VMEM((n // 2, p, q), bf16),
            pltpu.VMEM((n // 2, p, q), bf16),
            pltpu.VMEM((2, rows, ao), bf16),
            dma((n,)), dma((n,)),
            dma((2, na, count)), dma((na, count)),
            dma((n, count)), dma((n, count)),
            dma((n // 2,)), dma((n // 2,)),
            dma((2, n // 2)), dma((2, n // 2)),
            dma((2,)), dma((count + 2,)),
        ],
        compiler_params=pltpu.CompilerParams(
            collective_id=0, has_side_effects=True, vmem_limit_bytes=67043328
        ),
    )(metric, amplitudes, virt_coef)

def cube_kernel(
    na, n, count, ha, metric, amp, virt_coef, part_out, late_out, blocks_out, g_hbm,
    m_v, o_m, a_v, t_v, f_v, e_v, one_v, two_v,
    m_send, m_recv, z_send, z_recv, e_send, e_recv, x_send, x_recv,
    one_send, one_recv, two_send, two_recv, r_send, r_recv,
    mm_sem, fin_sem, far_sem, g_sem, local_sem,
):
    a, b = lax.axis_index("aux"), lax.axis_index("pair")
    p, q = metric.shape
    per = amp.shape[1]
    w = per // count
    rows = p // n
    virt, ao = virt_coef.shape
    parity, chip = lax.rem(b, 2), b // 2
    flip = 1 - 2 * parity
    partner = b + flip
    near = (chip + 1 - 2 * lax.rem(chip, 2), lax.rem(chip + 2, 4))
    far = 3 - chip
    xb, yb, fb = 2 * near[0] + parity, 2 * near[1] + parity, 2 * far + parity
    tile = 256 if p % 512 == 0 else 128
    tiles = p // tile
    mid = p // 2
    last = count - 1

    middle = jnp.logical_and(a > 0, a < na - 1)
    end = jnp.logical_not(middle)
    mate = a + 1 - 2 * lax.rem(a, 2)
    across = na - 1 - a
    beyond = na - 1 - mate

    barrier = pltpu.get_barrier_semaphore()
    for d in range(1, n):
        pl.semaphore_signal(barrier, inc=1, device_id=(a, lax.rem(b + d, n)), device_id_type=MESH)
    pl.semaphore_signal(barrier, inc=1, device_id=(mate, b), device_id_type=MESH)

    @pl.when(middle)
    def _():
        pl.semaphore_signal(barrier, inc=1, device_id=(across, b), device_id_type=MESH)

    pl.semaphore_wait(barrier, n + jnp.where(middle, 1, 0))

    v = w // 2

    def cols(c, base=0):
        return pl.ds(pl.multiple_of(base + c * w, w), w)

    def half(k, base=0):
        return pl.ds(pl.multiple_of(base + k * v, v), v)

    def row(r):
        return pl.ds(pl.multiple_of(r * tile, tile), tile)

    def part(way):
        return pl.ds(pl.multiple_of(way * mid, mid), mid)

    def wide(j):
        return pl.ds(pl.multiple_of(j * q, q), q)

    def block_of(s, k):
        return a_v.at[pl.ds(pl.multiple_of(s * p, p), p), half(k)]

    def z(s, k, way, own=False):
        return pltpu.make_async_remote_copy(
            src_ref=amp.at[:, half(k)] if own else block_of(s, k), dst_ref=block_of(s, k),
            send_sem=z_send.at[way, s, k], recv_sem=z_recv.at[s, k],
            device_id=(mate if way == 0 else across, b), device_id_type=MESH,
        )

    def own(way, *halves):
        for k in halves:
            z(a, k, way, True).start()

    def relay(s, k, way):
        z(s, k, way).wait_recv()
        z(s, k, way).start()

    def lend():
        return pltpu.make_async_remote_copy(
            src_ref=metric, dst_ref=o_m.at[:, wide(b)], send_sem=mm_sem.at[0], recv_sem=mm_sem.at[1],
            device_id=(mate, b), device_id_type=MESH,
        )

    def give(k):
        return pltpu.make_async_remote_copy(
            src_ref=e_v.at[:, half(k)], dst_ref=f_v.at[:, half(k)], send_sem=e_send.at[k], recv_sem=e_recv.at[k],
            device_id=(mate, b), device_id_type=MESH,
        )

    def staged(j):
        return o_m.at[:, wide(j)]

    def finish():
        return pltpu.make_async_remote_copy(
            src_ref=staged(b), dst_ref=two_v.at[0], send_sem=fin_sem.at[0], recv_sem=fin_sem.at[1],
            device_id=(mate, b), device_id_type=MESH,
        )

    def region(kind, mirror):
        mine = (b, b, b, xb, yb, xb, yb, fb, fb)
        theirs = (xb, yb, partner, fb, fb, xb + flip, yb + flip, fb + flip, fb + flip)
        side = (None, None, None, 0, 1, None, None, 0, 1)[kind]
        j = (theirs if mirror else mine)[kind]
        return (slice(None) if side is None else part(side), wide(j))

    def gather(g, kind, mirror=False):
        buf = (m_v, o_m)[g]
        where = region(kind, mirror)
        target = (xb, yb, partner, yb, xb, partner, partner, partner, partner)[kind]
        return pltpu.make_async_remote_copy(
            src_ref=metric if g == 0 and kind < 3 and not mirror else buf.at[where], dst_ref=buf.at[where],
            send_sem=m_send.at[g, kind], recv_sem=m_recv.at[g, kind],
            device_id=(a, target), device_id_type=MESH,
        )

    def got(g, kind):
        gather(g, kind, True).wait_recv()

    def gather_open(g):
        for kind in range(3):
            gather(g, kind).start()

    def gather_turn(g):
        got(g, 0)
        gather(g, 3).start()
        gather(g, 5).start()
        got(g, 1)
        gather(g, 4).start()
        gather(g, 6).start()

    def gather_close(g):
        got(g, 3)
        gather(g, 7).start()
        got(g, 4)
        gather(g, 8).start()
        for kind in (2, 5, 6, 7, 8):
            got(g, kind)
        for kind in range(9):
            gather(g, kind).wait_send()

    def regroup(owner, target, slot, where):
        return pltpu.make_async_remote_copy(
            src_ref=f_v.at[pl.ds(pl.multiple_of(target * rows, rows), rows), where()],
            dst_ref=g_hbm.at[:, where(owner * per)],
            send_sem=x_send.at[target, slot], recv_sem=x_recv.at[owner, slot],
            device_id=(a, target), device_id_type=MESH,
        )

    def keep(slot, where):
        return pltpu.make_async_copy(
            f_v.at[pl.ds(pl.multiple_of(b * rows, rows), rows), where()],
            g_hbm.at[:, where(b * per)], x_send.at[b, slot],
        )

    def regroup_all(slot, where):
        @pl.loop(1, n)
        def _(d):
            regroup(b, lax.rem(b + d, n), slot, where).start()

        keep(slot, where).start()

    def each_piece(act):
        @pl.loop(0, last)
        def _(c):
            act(c, functools.partial(cols, c))

        for k in (2 * last, 2 * last + 1):
            act(k - last, functools.partial(half, k))

    def fit(mat, dst, where):
        @pl.loop(0, tiles)
        def _(r):
            dst[row(r), where] = jnp.dot(
                mat[row(r), :], a_v[:, where], preferred_element_type=jnp.float32
            ).astype(dst.dtype)

    def product(left, j, r, span):
        return lax.dot_general(
            left[row(r), span], a_v[wide(j), span], (((1,), (1,)), ((), ())), preferred_element_type=jnp.float32
        )

    early, rest, whole = slice(0, ha * w), slice(ha * w, per), slice(0, per)
    most = slice(ha * w, per - v)

    def first(turn, j):
        return pltpu.make_async_remote_copy(
            src_ref=staged(j), dst_ref=one_v.at[turn, j // 2], send_sem=one_send.at[turn, j // 2],
            recv_sem=one_recv.at[turn, j // 2], device_id=(a, partner), device_id_type=MESH,
        )

    def early_piece(target, way, place):
        return pltpu.make_async_remote_copy(
            src_ref=o_m.at[part(way), wide((xb, yb, fb)[target])], dst_ref=two_v.at[place, part(way), :],
            send_sem=r_send.at[way, place], recv_sem=r_recv.at[way, place],
            device_id=(a, (xb, yb)[target if place else way]), device_id_type=MESH,
        )

    own_copies = [
        pltpu.make_async_copy(amp, a_v.at[pl.ds(pl.multiple_of(a * p, p), p), :], local_sem.at[0]),
        pltpu.make_async_copy(metric, m_v.at[:, wide(b)], local_sem.at[1]),
    ]

    @pl.when(end)
    def _():
        lend().start()
        gather_open(0)
        own(0, *range(2 * count))

    @pl.when(middle)
    def _():
        own(1, 2 * ha, 2 * ha + 1)
        own(0, 2 * ha, 2 * ha + 1)
        gather_open(0)
        own(1, 2 * ha + 2, 2 * ha + 3, 0, 1)
        own(0, *range(2 * ha + 2, 2 * count))

    for copy in own_copies:
        copy.start()

    @pl.when(end)
    def _():
        gather_turn(0)
        gather_close(0)

    @pl.when(middle)
    def _():
        lend().wait_recv()
        gather_open(1)
        for k in range(2 * ha, 2 * ha + 4):
            relay(across, k, 0)
        relay(mate, 0, 1)
        relay(mate, 1, 1)
        own(1, 2, 3)
        gather_turn(1)
        relay(mate, 2, 1)
        relay(mate, 3, 1)
        own(1, 4, 5)
        gather_turn(0)
        relay(mate, 4, 1)
        relay(mate, 5, 1)
        own(1, 6)
        gather_close(1)

    for copy in own_copies:
        copy.wait()

    def first_share(low, high):
        @pl.loop(low, high)
        def _(h):
            j = 2 * h + 1 - parity

            @pl.loop(0, tiles)
            def _(r):
                o_m[row(r), wide(j)] = product(e_v, j, r, early).astype(o_m.dtype)

            first(0, j).start()

    def first_total(j, r):
        return product(e_v, j, r, early) + one_v[0, j // 2, row(r), :].astype(jnp.float32)

    def second_share(target):
        j = (xb, yb, fb)[target]
        first(0, j).wait_recv()

        @pl.loop(0, tiles)
        def _(r):
            o_m[row(r), wide(j)] = first_total(j, r).astype(o_m.dtype)

        if target == 2:
            early_piece(2, 0, 0).start()
            early_piece(2, 1, 0).start()
        else:
            early_piece(target, target, 1).start()

    def third_share():
        for way in range(2):
            other = 1 - way
            early_piece(2, way, 0).wait_recv()

            @pl.loop(way * tiles // 2, (way + 1) * tiles // 2)
            def _(r, j=(xb, yb)[other]):
                total = first_total(j, r) + two_v[0, row(r), :].astype(jnp.float32)
                o_m[row(r), wide(j)] = total.astype(o_m.dtype)

            early_piece(other, way, 2).start()

    def fourth_share():
        first(0, b).wait_recv()
        for way in range(2):
            early_piece(way, way, 1).wait_recv()
            early_piece(1 - way, way, 2).wait_recv()

        @pl.loop(0, tiles)
        def _(r):
            total = first_total(b, r)
            for place in (1, 2):
                total += two_v[place, row(r), :].astype(jnp.float32)
            o_m[row(r), wide(b)] = total.astype(o_m.dtype)

        for way in range(2):
            early_piece(2, way, 0).wait_send()
            early_piece(way, way, 1).wait_send()
            early_piece(1 - way, way, 2).wait_send()

    @pl.loop(0, ha - 1)
    def _(c):
        @pl.when(middle)
        def _():
            for k in (2 * c, 2 * c + 1):
                z(across, k, 0).wait_recv()
                z(beyond, k, 0).wait_recv()
            fit(o_m, e_v, cols(c))
            give(2 * c).start()
            give(2 * c + 1).start()
            relay(mate, 2 * c + 6, 1)

            @pl.when(c == 0)
            def _():
                own(1, 7)

            relay(mate, 2 * c + 7, 1)

            @pl.when(c == 2)
            def _():
                own(1, 12, 13)

            @pl.when(c == 0)
            def _():
                gather_close(0)

            fit(m_v, f_v, cols(c))

        @pl.when(end)
        def _():
            give(2 * c).wait_recv()
            give(2 * c + 1).wait_recv()

        regroup_all(c, functools.partial(cols, c))

    @pl.when(middle)
    def _():
        @pl.loop(6, 8)
        def _(k):
            z(across, k, 0).wait_recv()
            z(beyond, k, 0).wait_recv()
            fit(o_m, e_v, half(k))
            give(k).start()

            @pl.when(k == 6)
            def _():
                relay(mate, 12, 1)
                relay(mate, 13, 1)
                own(1, 14)

        relay(mate, 14, 1)
        own(1, 15)
        relay(mate, 15, 1)
        fit(m_v, f_v, cols(ha - 1))

    @pl.when(end)
    def _():
        give(6).wait_recv()
        give(7).wait_recv()

    regroup_all(ha - 1, functools.partial(cols, ha - 1))

    def all_in(k):
        for source in (mate, across, beyond):
            z(source, k, 0).wait_recv()

    @pl.loop(ha, last)
    def _(c):
        @pl.when(jnp.logical_and(middle, c == ha))
        def _():
            relay(beyond, 2 * ha, 0)
            first_share(0, 2)
            relay(beyond, 2 * ha + 1, 0)
            first_share(2, n // 2)
            relay(beyond, 2 * ha + 2, 0)

        @pl.when(jnp.logical_and(middle, c == ha + 1))
        def _():
            relay(beyond, 2 * ha + 3, 0)
            second_share(2)

        @pl.when(jnp.logical_and(middle, c == last - 1))
        def _():
            relay(across, 2 * last - 2, 0)
            second_share(0)
            relay(across, 2 * last - 1, 0)
            second_share(1)
            relay(beyond, 2 * last - 2, 0)
            relay(beyond, 2 * last - 1, 0)
            third_share()

        @pl.when(end)
        def _():
            all_in(2 * c)
            all_in(2 * c + 1)

        fit(m_v, f_v, cols(c))
        regroup_all(c, functools.partial(cols, c))

    for k in (2 * last, 2 * last + 1):
        @pl.when(middle)
        def _():
            relay(across, k, 0)
            relay(beyond, k, 0)

        @pl.when(end)
        def _():
            all_in(k)

        if k == 2 * last:
            fit(m_v, f_v, half(k))
            regroup_all(k - last, functools.partial(half, k))

            @pl.when(end)
            def _():
                for at, j in enumerate((2 * far + 1 - parity, 2 * far + parity)):
                    @pl.loop(0, tiles)
                    def _(r, at=at, j=j):
                        (part_out, t_v)[at][row(r), :] = product(f_v, j, r, most)

    @pl.when(middle)
    def _():
        @pl.loop(0, n // 2)
        def _(h):
            first(0, 2 * h + 1 - parity).wait_send()

    def by_role(act, low=0, high=tiles):
        for role, span in ((middle, whole), (end, rest)):
            @pl.when(role)
            def _():
                @pl.loop(low, high)
                def _(r):
                    act(r, span)

    def for_partner(slot):
        j = 2 * slot + 1 - parity

        def act(r, span):
            o_m[row(r), wide(j)] = product(f_v, j, r, span).astype(o_m.dtype)

        by_role(act)
        first(1, j).start()

    final = slice(per - v, per)

    def far_total(at, r, span):
        j = 2 * far + (parity if at else 1 - parity)
        if span is whole:
            return product(f_v, j, r, whole)
        return (part_out, t_v)[at][row(r), :] + product(f_v, j, r, final)

    def far_first(way):
        return pltpu.make_async_remote_copy(
            src_ref=o_m.at[part(way), wide(2 * far + 1 - parity)], dst_ref=one_v.at[1, far, part(way), :],
            send_sem=far_sem.at[0, way], recv_sem=far_sem.at[1, way],
            device_id=(a, partner), device_id_type=MESH,
        )

    @pl.loop(0, 2)
    def _(way):
        low, high = way * (tiles // 2), (way + 1) * (tiles // 2)

        @pl.loop(low, high)
        def _(r):
            f_v[row(r), final] = jnp.dot(
                m_v[row(r), :], a_v[:, final], preferred_element_type=jnp.float32
            ).astype(f_v.dtype)

        def act(r, span):
            o_m[row(r), wide(2 * far + 1 - parity)] = far_total(0, r, span).astype(o_m.dtype)

        by_role(act, low, high)
        far_first(way).start()

    regroup_all(last + 1, functools.partial(half, 2 * last + 1))

    spare = n * q - 3 * q

    def sent(at):
        return pl.ds(spare + at * q, q)

    def piece(place_of, way, place, target):
        return pltpu.make_async_remote_copy(
            src_ref=m_v.at[part(way), sent(place_of)],
            dst_ref=two_v.at[3, part(way), :] if place == 0 else late_out.at[place - 1, part(way), :],
            send_sem=two_send.at[way, place], recv_sem=two_recv.at[way, place],
            device_id=(a, 2 * target + parity), device_id_type=MESH,
        )

    def turn(h):
        return jnp.where(h == 0, far, jnp.where(h == 1, near[0], jnp.where(h == 2, near[1], chip)))

    @pl.loop(0, 2)
    def _(way):
        far_first(way).wait_recv()

        def act(r, span):
            total = far_total(1, r, span) + one_v[1, far, row(r), :].astype(jnp.float32)
            m_v[row(r), sent(0)] = total.astype(m_v.dtype)

        by_role(act, way * (tiles // 2), (way + 1) * (tiles // 2))
        piece(0, way, 0, jnp.where(way == 0, near[0], near[1])).start()

    @pl.when(middle)
    def _():
        fourth_share()
        finish().start()

    @pl.loop(1, n // 2 - 1)
    def _(h):
        for_partner(turn(h))

    @pl.loop(1, n // 2)
    def _(h):
        slot = turn(h)
        j = 2 * slot + parity
        first(1, j).wait_recv()

        def act(r, span):
            total = product(f_v, j, r, span) + one_v[1, slot, row(r), :].astype(jnp.float32)
            for at in (1, 2):
                @pl.when(h == at)
                def _():
                    m_v[row(r), sent(at)] = total.astype(m_v.dtype)

                @pl.when(jnp.logical_and(h == at, r >= tiles // 2 if at == 1 else r < tiles // 2))
                def _():
                    t_v[row(r), :] = total

            @pl.when(h == 3)
            def _():
                part_out[row(r), :] = total

        by_role(act)

        for way in range(2):
            @pl.when(h == 1 + way)
            def _():
                piece(1 + way, way, 1, near[way]).start()

        @pl.when(h == n // 2 - 2)
        def _():
            for_partner(chip)

    for way in range(2):
        at = 1 - way
        piece(0, way, 0, near[way]).wait_recv()
        m_v[part(way), sent(1 + at)] = (t_v[part(way), :] + two_v[3, part(way), :].astype(jnp.float32)).astype(m_v.dtype)
        piece(1 + at, way, 2, near[at]).start()

    coef = m_v.at[pl.ds(0, virt), pl.ds(0, ao)]
    load_coef = pltpu.make_async_copy(virt_coef, coef, local_sem.at[0])
    load_coef.start()

    def regrouped(slot, where):
        keep(slot, where).wait()

        @pl.loop(1, n)
        def _(d):
            regroup(lax.rem(b + n - d, n), b, slot, where).wait_recv()

    each_piece(regrouped)

    occ = n * per // virt

    def slot_rows(slot):
        return pl.ds(pl.multiple_of(slot * rows, rows), rows)

    def block_copy(i, slot):
        return pltpu.make_async_copy(
            g_hbm.at[:, pl.ds(pl.multiple_of(i * virt, virt), virt)],
            e_v.at[slot_rows(slot), pl.ds(0, virt)], g_sem.at[slot],
        )

    @pl.when(middle)
    def _():
        @pl.loop(0, 2 * ha)
        def _(k):
            give(k).wait_send()

    block_copy(0, 0).start()
    load_coef.wait()

    @pl.loop(0, occ)
    def _(i):
        slot = lax.rem(i, 2)

        @pl.when(i + 1 < occ)
        def _():
            block_copy(i + 1, 1 - slot).start()

        block_copy(i, slot).wait()
        blocks_out[:, pl.ds(pl.multiple_of(i * ao, ao), ao)] = jnp.dot(
            e_v[slot_rows(slot), pl.ds(0, virt)], m_v[pl.ds(0, virt), pl.ds(0, ao)],
            preferred_element_type=jnp.float32,
        ).astype(blocks_out.dtype)

    @pl.when(end)
    def _():
        finish().wait_recv()

        @pl.loop(0, tiles)
        def _(r):
            part_out[row(r), :] += two_v[0, row(r), :].astype(jnp.float32)

    @pl.loop(1, n // 2)
    def _(h):
        first(1, 2 * turn(h) + 1 - parity).wait_send()

    for way in range(2):
        far_first(way).wait_send()

    for way in range(2):
        piece(0, way, 0, near[way]).wait_send()
        piece(1, way, 1, near[way]).wait_send()

    def regroup_sent(slot, where):
        @pl.loop(1, n)
        def _(d):
            regroup(b, lax.rem(b + d, n), slot, where).wait_send()

    each_piece(regroup_sent)

    @pl.when(end)
    def _():
        lend().wait_send()

        @pl.loop(0, 2 * count)
        def _(k):
            z(a, k, 0).wait_send()

    @pl.when(middle)
    def _():
        finish().wait_send()

        @pl.loop(0, 2 * count)
        def _(k):
            z(a, k, 1).wait_send()
            z(mate, k, 1).wait_send()

        @pl.loop(2 * ha, 2 * count)
        def _(k):
            z(a, k, 0).wait_send()
            z(across, k, 0).wait_send()
            z(beyond, k, 0).wait_send()

    for way in range(2):
        piece(1, way, 1, near[way]).wait_recv()
        piece(1, way, 2, near[1 - way]).wait_recv()
        piece(1, way, 2, near[1 - way]).wait_send()


def close_kernel(part, late, ao_in, density, ao_out, sum_v, copy_sem, out_sem):
    cuts, steps = copy_sem.shape[0], out_sem.shape[0]
    span, size = ao_in.shape[1] // cuts, part.shape[0] // steps
    writes = []
    for k in range(cuts):
        held = slice(k * span, (k + 1) * span)
        writes.append(pltpu.make_async_copy(ao_in.at[:, held], ao_out.at[:, held], copy_sem.at[k]))
    for copy in writes[: cuts // 2]:
        copy.start()
    for k in range(steps):
        where = pl.ds(k * size, size)
        sum_v[where, :] = (
            part[where, :] + late[0, where, :].astype(jnp.float32) + late[1, where, :].astype(jnp.float32)
        )
        store = pltpu.make_async_copy(sum_v.at[where, :], density.at[where, :], out_sem.at[k])
        store.start()
        writes.append(store)
    for copy in writes[cuts // 2 : cuts]:
        copy.start()
    for copy in writes:
        copy.wait()


def cube_shards(na, n, count, metric, amplitudes, virt_coef):
    p, q = metric.shape
    per = amplitudes.shape[1]
    virt, ao = virt_coef.shape
    ha = count // 2
    rows = p // n
    bf16 = jnp.bfloat16
    dma = pltpu.SemaphoreType.DMA
    part, late, blocks, _ = pl.pallas_call(
        functools.partial(cube_kernel, na, n, count, ha),
        out_shape=(
            pltpu.VMEM((p, q), jnp.float32),
            pltpu.VMEM((2, p, q), bf16),
            pltpu.VMEM((rows, n * per // virt * ao), bf16),
            jax.ShapeDtypeStruct((rows, n * per), bf16),
        ),
        in_specs=[pl.BlockSpec(memory_space=pl.ANY)] * 3,
        out_specs=(pl.BlockSpec(memory_space=pltpu.VMEM),) * 3 + (pl.BlockSpec(memory_space=pl.ANY),),
        scratch_shapes=[
            pltpu.VMEM((p, n * q), bf16),
            pltpu.VMEM((p, n * q), bf16),
            pltpu.VMEM((na * p, per), bf16),
            pltpu.VMEM((p, q), jnp.float32),
            pltpu.VMEM((p, per), bf16),
            pltpu.VMEM((p, per * ha // count), bf16),
            pltpu.VMEM((2, n // 2, p, q), bf16),
            pltpu.VMEM((4, p, q), bf16),
            dma((2, 9)), dma((2, 9)),
            dma((2, na, 2 * count)), dma((na, 2 * count)),
            dma((2 * ha,)), dma((2 * ha,)),
            dma((n, count + 1)), dma((n, count + 1)),
            dma((2, n // 2)), dma((2, n // 2)),
            dma((2, 3)), dma((2, 3)),
            dma((2, 3)), dma((2, 3)),
            dma((2,)), dma((2,)), dma((2, 2)), dma((2,)), dma((2,)),
        ],
        compiler_params=pltpu.CompilerParams(
            collective_id=0, has_side_effects=True, vmem_limit_bytes=54 * 2**20
        ),
    )(metric, amplitudes, virt_coef)
    return pl.pallas_call(
        close_kernel,
        out_shape=(jax.ShapeDtypeStruct(part.shape, part.dtype), jax.ShapeDtypeStruct(blocks.shape, bf16)),
        in_specs=[pl.BlockSpec(memory_space=pltpu.VMEM)] * 3,
        out_specs=(pl.BlockSpec(memory_space=pl.ANY),) * 2,
        scratch_shapes=[
            pltpu.VMEM((p, q), jnp.float32), dma((4,)), dma((4,)),
        ],
        compiler_params=pltpu.CompilerParams(vmem_limit_bytes=8 * 2**20),
    )(part, late, blocks)


def fits_cube(na, n, metric, amplitudes, virt_coef):
    p, per, (virt, ao) = metric.shape[0], amplitudes.shape[1], virt_coef.shape
    return (
        na == 4 and n == 8 and per % 2048 == 0 and p % 256 == 0
        and metric.shape[1] * n == na * p and virt <= min(p, per // 2) and ao <= (n - 3) * metric.shape[1]
        and virt % 128 == 0 and ao % 128 == 0 and n * per % virt == 0
    )


def any_shards(na, n, metric, amplitudes, virt_coef):
    if fits_cube(na, n, metric, amplitudes, virt_coef):
        return cube_shards(na, n, 8, metric, amplitudes, virt_coef)
    return shards(na, n, metric, amplitudes, virt_coef)


def solution(mesh):
    in_specs = (P("aux", "pair"), P("aux", "pair"), P())
    out_specs = (P("aux", "pair"), P(("aux", "pair"), None))
    body = functools.partial(any_shards, mesh.shape["aux"], mesh.shape["pair"])
    return jax.shard_map(body, mesh=mesh, in_specs=in_specs, out_specs=out_specs, check_vma=False)
```
